32 devices in a mesh: comp: 4 (over z), lon: 8 (over y, x, core).
Axes of the slice: x: 2, y: 2, z: 4, core: 2. Of those that a mesh axis runs over, the one named last changes fastest.
Arguments:
- atm_state: float32 [4, 4, 1024, 1024], P(None, None, 'comp', 'lon'), may hold values from -6 to 6
- ocean_state: float32 [4, 4, 1024, 1024], P(None, None, 'comp', 'lon'), may hold values from -6 to 6
- surface_state: float32 [3, 1024, 1024], P(None, 'comp', 'lon'), may hold values from -6 to 6
- atm_diffusion: float32 [1024, 1024], P('comp', 'lon'), may hold values from 0.02 to 0.2
- land_sea: int32 [1024, 1024], P('comp', 'lon'), may hold values 0 or 1
- flux_dest: int32 [8192, 1], P(('comp', 'lon')), may hold values from 0 to 31; in each aligned block of 256 rows (0 to 255, 256 to 511, ...) at most 16 rows name the same one
- flux_row: int32 [8192], P(('comp', 'lon')), may hold values from 0 to 255
- flux_weight: bfloat16 [8192, 128, 128], P(('comp', 'lon')), may hold values from -0.5 to 0.5
- surface_dest: int32 [8192, 1], P(('comp', 'lon')), may hold values from 0 to 31; in each aligned block of 256 rows (0 to 255, 256 to 511, ...) at most 16 rows name the same one
- surface_row: int32 [8192], P(('comp', 'lon')), may hold values from 0 to 255
- surface_weight: bfloat16 [8192, 128, 128], P(('comp', 'lon')), may hold values from -0.5 to 0.5
Outputs:
- atm_next: float32 [4, 4, 1024, 1024], P(None, None, 'comp', 'lon')
- ocean_next: float32 [4, 4, 1024, 1024], P(None, None, 'comp', 'lon')
- surface_next: float32 [3, 1024, 1024], P(None, 'comp', 'lon')
The draws below stay inside these ranges and needn't reach their ends.
Inputs may be any that keep to these rules, and one draw needn't show every extreme that they name: `flux_dest`: in the rows of one device, no device is named more than 16 times, and some device is named exactly 16 times. `surface_dest`: in the rows of one device, no device is named more than 16 times, and some device is named exactly 16 times.
All inputs are finite; a program needn't handle non-finite values. No bound on the sum of `land_sea` on one device may be relied on, other than what follows from the above.
Results may differ from the reference program's by a relative error of at most 0.0003.
Values sent between devices are 32-bit elements; how exact they have to be, the bound alone decides.
No kernel may reach another device: no remote copies, remote signals or barrier semaphores. Data moves between devices by JAX's collectives and lax.ppermute only.
A program may use at most 128 MiB of HBM per device.

```python
import math
import jax
import jax.numpy as jnp
import numpy as np
from jax import lax

LEVELS = 4
ROWS = 256
COLS = 128
VARIABLES = 4
SURFACE = 3
NDEV = 32
CAP = 16
GRID_ROWS = 1024
GRID_COLS = 1024
BLOCKS = 8192
N_COMP = 4
N_LON = 8


def plant(entries, rng, least, high):
    place = [jax.random.randint(jax.random.fold_in(rng, axis), (), 0, length) for axis, length in enumerate(entries.shape)]
    widest = entries.shape.index(max(entries.shape))
    beside = place[:widest] + [(place[widest] + 1) % entries.shape[widest]] + place[widest + 1:]
    return entries.at[tuple(place)].set(least).at[tuple(beside)].set(high)


def shard_levels(key, shape, split, low, largest):
    def one(axis_at, shards_of):
        draws = jax.random.uniform(jax.random.fold_in(jax.random.fold_in(key, 6), axis_at), (shards_of,), jnp.float32, low / len(split), largest / len(split))
        return jnp.repeat(jnp.exp(draws), shape[axis_at] // shards_of).reshape((-1,) + (1,) * (len(shape) - axis_at - 1))

    factor_of = one(*split[0])
    for cut in split[1:]:
        factor_of = factor_of * one(*cut)
    return factor_of


def shared_out(key, own, number, rows, amount, top, reach, skew):
    ranking = jax.random.permutation(key, amount)
    crowded, ordinary = load_shares(amount, rows * top, reach, skew, True), load_shares(amount, rows * top, reach, skew, False)
    places = jnp.arange(amount)

    def named(tallies, turn):
        used = int((tallies > 0).sum())
        fixed = max(1, used // 4)
        moved = fixed + (places - fixed + turn * (used - fixed)) % max(1, amount - fixed)
        return jnp.zeros((amount,), jnp.int32).at[ranking[jnp.where(places < fixed, places, moved)]].set(jnp.asarray(tallies, jnp.int32))

    tallies = jnp.where(number % 4 == 0, named(crowded, number // 4), named(ordinary, number - number // 4 - 1))
    mixed = jax.random.permutation(jax.random.fold_in(own, 3), amount)
    source_of, sink = mixed[0:amount // 2 * 2:2], mixed[1:amount // 2 * 2:2]
    margin = jnp.minimum(tallies[source_of] - 1, reach - tallies[sink]) // 2
    margin = jnp.where((source_of == ranking[0]) | (sink == ranking[0]) | (tallies[sink] == 0), 0, jnp.maximum(margin, 0))
    moved = jax.random.randint(jax.random.fold_in(own, 4), (amount // 2,), 0, 1 << 20) % (margin + 1)
    tallies = tallies.at[source_of].add(-moved).at[sink].add(moved)
    labels = jnp.searchsorted(jnp.cumsum(tallies), jnp.arange(rows * top), side="right").astype(jnp.int32)
    table = labels.reshape(top, rows).T
    table = table[jax.random.permutation(jax.random.fold_in(own, 1), rows)]
    turn = jax.random.randint(jax.random.fold_in(own, 2), (rows, 1), 0, top)
    return jnp.take_along_axis(table, (jnp.arange(top)[None, :] + turn) % top, axis=1)


def load_shares(number_of, total, bound, skew, full):
    weights = [(1 << 20) // math.isqrt(standing ** skew) + 1 for standing in range(1, number_of + 1)]
    largest = bound if full else min(bound, max(-(-total // number_of), total * weights[0] // sum(weights)))
    least = 1 if total - largest >= number_of - 1 else 0
    counts, spare = [largest] + [least] * (number_of - 1), total - largest - least * (number_of - 1)
    while spare > 0:
        free = [i for i in range(1, number_of) if counts[i] < largest] or [i for i in range(1, number_of) if counts[i] < bound]
        mass, remaining = sum([weights[i] for i in free]), spare
        for i in free:
            extra = min(bound - counts[i], max(1, remaining * weights[i] // mass), spare)
            counts[i] = counts[i] + extra
            spare = spare - extra
    return np.array(counts)


def gaussian(stream_key, extent, deviation, limit, cuts=(), held_as=jnp.bfloat16):
    level = shard_levels(stream_key, extent, cuts, -0.22, 0.18) if cuts else 1.0
    drawn = jax.random.normal(stream_key, extent, jnp.float32) * deviation * level
    return jnp.minimum(jnp.maximum(drawn, -limit), limit).astype(held_as)


def setup_inputs(seed: int = 0) -> dict:
    seeds = jax.random.split(jax.random.key(seed), 12)
    atm_state = gaussian(seeds[0], (VARIABLES, LEVELS, GRID_ROWS, GRID_COLS), 1.0, 6.0, ((2, 4), (3, 8)), jnp.float32)
    ocean_state = gaussian(seeds[1], (VARIABLES, LEVELS, GRID_ROWS, GRID_COLS), 1.0, 6.0, ((2, 4), (3, 8)), jnp.float32)
    surface_state = gaussian(seeds[2], (SURFACE, GRID_ROWS, GRID_COLS), 1.0, 6.0, ((1, 4), (2, 8)), jnp.float32)
    atm_diffusion = jnp.clip(jnp.exp(math.log(0.2) - 2.3025851 * jax.random.uniform(seeds[3], (GRID_ROWS, GRID_COLS), jnp.float32) ** shard_levels(seeds[3], (GRID_ROWS, GRID_COLS), ((0, 4), (1, 8)), -0.2, 0.2)), 0.02, 0.2)
    land_sea = plant((jax.random.randint(seeds[4], (GRID_ROWS, GRID_COLS), 0, 10) < 7).astype(jnp.int32), jax.random.fold_in(seeds[4], 1), 0, 1)
    flux_dest_keys = jax.random.split(jax.random.fold_in(seeds[5], 1), BLOCKS // ROWS)
    flux_dest_turns = jax.random.permutation(jax.random.fold_in(seeds[5], 3), BLOCKS // ROWS)
    flux_dest = jax.vmap(lambda own, number: shared_out(jax.random.fold_in(seeds[5], 2), own, number, ROWS, NDEV, 1, CAP, 2))(flux_dest_keys, flux_dest_turns).reshape((BLOCKS, 1))
    flux_row = plant(jax.random.randint(seeds[6], (BLOCKS,), 0, ROWS), jax.random.fold_in(seeds[6], 1), 0, ROWS - 1).astype(jnp.int32)
    flux_weight = gaussian(seeds[7], (BLOCKS, COLS, COLS), COLS ** -0.5, 0.5, ((0, 32),))
    surface_dest_keys = jax.random.split(jax.random.fold_in(seeds[8], 1), BLOCKS // ROWS)
    surface_dest_turns = jax.random.permutation(jax.random.fold_in(seeds[8], 3), BLOCKS // ROWS)
    surface_dest = jax.vmap(lambda own, number: shared_out(jax.random.fold_in(seeds[8], 2), own, number, ROWS, NDEV, 1, CAP, 2))(surface_dest_keys, surface_dest_turns).reshape((BLOCKS, 1))
    surface_row = plant(jax.random.randint(seeds[9], (BLOCKS,), 0, ROWS), jax.random.fold_in(seeds[9], 1), 0, ROWS - 1).astype(jnp.int32)
    surface_weight = gaussian(seeds[10], (BLOCKS, COLS, COLS), COLS ** -0.5, 0.5, ((0, 32),))
    return dict(atm_state=atm_state, ocean_state=ocean_state, surface_state=surface_state, atm_diffusion=atm_diffusion, land_sea=land_sea, flux_dest=flux_dest, flux_row=flux_row, flux_weight=flux_weight, surface_dest=surface_dest, surface_row=surface_row, surface_weight=surface_weight)


time_step = 0.1
ocean_diffusion = 0.2
vertical_mixing = 0.2
drag_coef = 0.4
heat_coef = 0.5
moisture_coef = 0.3
rain_coef = 0.2
forcing_gain = 0.5

def lateral(source_field):
    padded = jnp.pad(source_field, [(0, 0)] * (source_field.ndim - 2) + [(1, 1), (0, 0)])
    return (padded[..., 2:, :], padded[..., :-2, :], jnp.roll(source_field, -1, axis=-1), jnp.roll(source_field, 1, axis=-1))

def atmosphere_step(atm_state, atm_diffusion):
    north_side, south_side, east_side, west_side = lateral(atm_state)
    laplace = north_side + south_side + east_side + west_side - 4.0 * atm_state
    advection = atm_state[0:1] * (east_side - west_side) + atm_state[1:2] * (north_side - south_side)
    return atm_state + atm_diffusion * laplace - 0.5 * time_step * advection

def surface_fluxes(atm_next, surface_state):
    wind_east = atm_next[0, 0] - surface_state[1]
    wind_north = atm_next[1, 0] - surface_state[2]
    wind_speed = jnp.sqrt(1.0 + wind_east * wind_east + wind_north * wind_north)
    humidity = atm_next[3, 0]
    return jnp.stack([drag_coef * wind_speed * wind_east, drag_coef * wind_speed * wind_north, heat_coef * wind_speed * (atm_next[2, 0] - surface_state[0]), moisture_coef * wind_speed * (surface_state[0] - humidity), rain_coef * humidity * humidity])

def ocean_step(ocean_state, land_sea, ocean_fluxes):
    mask_float = land_sea.astype(jnp.float32)
    north_side, south_side, east_side, west_side = lateral(ocean_state * mask_float)
    mask_north, mask_south, mask_east, mask_west = lateral(mask_float)
    mask_count = mask_north + mask_south + mask_east + mask_west
    laplace = north_side + south_side + east_side + west_side - mask_count * ocean_state
    upper_level = jnp.concatenate([ocean_state[:, :1], ocean_state[:, :-1]], axis=1)
    lower_level = jnp.concatenate([ocean_state[:, 1:], ocean_state[:, -1:]], axis=1)
    vertical = upper_level + lower_level - 2.0 * ocean_state
    forcing = forcing_gain * jnp.stack([ocean_fluxes[2], ocean_fluxes[3] - ocean_fluxes[4], ocean_fluxes[0], ocean_fluxes[1]])
    forcing_levels = jnp.concatenate([forcing[:, None], jnp.zeros_like(ocean_state[:, 1:])], axis=1)
    return mask_float * (ocean_state + ocean_diffusion * laplace + vertical_mixing * vertical + forcing_levels)

def to_blocks(grid_field):
    channels = grid_field.shape[0]
    reshaped = grid_field.reshape(channels, N_COMP, ROWS, N_LON, COLS)
    return reshaped.transpose(1, 3, 2, 0, 4).reshape(N_COMP * N_LON * ROWS, channels, COLS)

def from_blocks(block_field):
    channels = block_field.shape[1]
    reshaped = block_field.reshape(N_COMP, N_LON, ROWS, channels, COLS)
    return reshaped.transpose(3, 0, 2, 1, 4).reshape(channels, N_COMP * ROWS, N_LON * COLS)

def remap(grid_field, destination, target_row, weight):
    blocks = to_blocks(grid_field)
    channels = blocks.shape[1]
    device_blocks = blocks.reshape(N_COMP * N_LON, ROWS, channels, COLS)
    device_weight = weight.reshape(N_COMP * N_LON, ROWS, COLS, COLS)

    def one_device(operands):
        return jnp.einsum('rkc,rcd->rkd', operands[0], operands[1].astype(jnp.float32), precision=lax.Precision.HIGHEST)
    mapped = lax.map(one_device, (device_blocks, device_weight)).reshape(N_COMP * N_LON * ROWS, channels * COLS)
    target = (destination[:, 0] * ROWS + target_row).astype(jnp.int32)
    summed = jax.ops.segment_sum(mapped, target, num_segments=N_COMP * N_LON * ROWS)
    return from_blocks(summed.reshape(N_COMP * N_LON * ROWS, channels, COLS))

def reference(atm_state, ocean_state, surface_state, atm_diffusion, land_sea, flux_dest, flux_row, flux_weight, surface_dest, surface_row, surface_weight):
    atm_next = atmosphere_step(atm_state, atm_diffusion)
    fluxes = surface_fluxes(atm_next, surface_state)
    ocean_fluxes = remap(fluxes, flux_dest, flux_row, flux_weight)
    ocean_next = ocean_step(ocean_state, land_sea, ocean_fluxes)
    surface_out = jnp.stack([ocean_next[0, 0], ocean_next[2, 0], ocean_next[3, 0]])
    surface_next = remap(surface_out, surface_dest, surface_row, surface_weight)
    return (atm_next, ocean_next, surface_next)
```

```python
import functools

import jax
import jax.numpy as jnp
from jax import lax
from jax.experimental import pallas as pl
from jax.experimental.pallas import tpu as pltpu
from jax.sharding import PartitionSpec as P

time_step = 0.1
ocean_diffusion = 0.2
vertical_mixing = 0.2
drag_coef = 0.4
heat_coef = 0.5
moisture_coef = 0.3
rain_coef = 0.2
forcing_gain = 0.5

AXES = ("comp", "lon")
LANES = 128
CHUNKS = 8
F32 = jnp.float32
BF16 = jnp.bfloat16
VMEM_LIMIT = 48 << 20


def params(**kw):
    return pltpu.CompilerParams(vmem_limit_bytes=VMEM_LIMIT, **kw)


def shift(x, axis, up, wrap):
    devices = lax.axis_size(axis)
    pairs = [(i, (i + 1) % devices) for i in range(devices if wrap else devices - 1)]
    if not up:
        pairs = [(j, i) for i, j in pairs]
    return lax.ppermute(x, axis, pairs)


def exchange(first_rows, last_rows, first_cols, last_cols):
    north = shift(first_rows, "comp", False, False)
    south = shift(last_rows, "comp", True, False)
    east = shift(first_cols, "lon", False, True)
    west = shift(last_cols, "lon", True, True)
    return north, south, east, west


def put_edges(field, at, halves, refs):
    first_rows, last_rows, first_cols, last_cols = refs
    rows = field.shape[0]
    first_rows[at : at + 1, :] = field[0:1, :]
    last_rows[at : at + 1, :] = field[rows - 1 : rows, :]
    for h in range(halves):
        turned = jnp.transpose(field[h * LANES : (h + 1) * LANES, :])
        row = at * halves + h
        first_cols[row : row + 1, :] = turned[0:1, :]
        last_cols[row : row + 1, :] = turned[LANES - 1 : LANES, :]


def neighbours(x, north, south, east, west):
    rows, cols = x.shape
    row = lax.broadcasted_iota(jnp.int32, x.shape, 0)
    col = lax.broadcasted_iota(jnp.int32, x.shape, 1)
    n = jnp.where(row == rows - 1, north, pltpu.roll(x, rows - 1, 0))
    s = jnp.where(row == 0, south, pltpu.roll(x, 1, 0))
    e = jnp.where(col == cols - 1, east, pltpu.roll(x, cols - 1, 1))
    w = jnp.where(col == 0, west, pltpu.roll(x, 1, 1))
    return n, s, e, w


def column(turned, at, halves):
    parts = [turned[:, at * halves + h : at * halves + h + 1] for h in range(halves)]
    return jnp.concatenate(parts, axis=0)


def atm_edges_kernel(halves, count, atm, *outs):
    for at in range(count):
        put_edges(atm[at, 0], at, halves, outs)


def rest_edges_kernel(halves, variables, levels, atm, ocean, land, *outs):
    at = 0
    for v in range(variables):
        for level in range(1, levels):
            put_edges(atm[v, level], at, halves, outs)
            at += 1
    mask = land[...].astype(F32)
    for v in range(variables):
        for level in range(levels):
            put_edges(ocean[v, level] * mask, at, halves, outs)
            at += 1
    put_edges(mask, at, halves, outs)
    for ref in outs:
        used = (at + 1) * (ref.shape[0] // outs[0].shape[0])
        if used < ref.shape[0]:
            ref[used:, :] = jnp.zeros((ref.shape[0] - used, LANES), F32)


def atm_step(a, u, v, diffusion, sides):
    n, s, e, w = sides
    laplace = n + s + e + w - 4.0 * a
    advection = u * (e - w) + v * (n - s)
    return a + diffusion * laplace - 0.5 * time_step * advection


def start_weights(weight, held, sems):
    rows = held.shape[0] // CHUNKS
    for c in range(CHUNKS):
        part = pl.ds(c * rows, rows)
        pltpu.make_async_copy(weight.at[part], held.at[part], sems.at[c]).start()


def put_split(fields, split):
    rows = fields[0].shape[0]
    for i in range(4):
        if i < len(fields):
            high = fields[i].astype(BF16).astype(F32)
            low = fields[i] - high
        else:
            high = low = jnp.zeros((rows, LANES), F32)
        split[pl.ds(i, rows, stride=8), :] = high
        split[pl.ds(4 + i, rows, stride=8), :] = low


def product_rows(slots, weight, held, sems, split, placed, sent, channels):
    rows = held.shape[0] // CHUNKS

    def chunk(c, carry):
        part = pl.ds(c * rows, rows)
        pltpu.make_async_copy(weight.at[part], held.at[part], sems.at[c]).wait()
        for i in range(rows):
            r = c * rows + i
            left = split[pl.ds(pl.multiple_of(r * 8, 8), 8), :].astype(BF16)
            placed[slots[r]] = jnp.dot(left, held[r], preferred_element_type=F32)
        return carry

    lax.fori_loop(0, CHUNKS, chunk, 0)
    count = placed.shape[0]
    for i in range(channels):
        total = placed[:, i, :] + placed[:, 4 + i, :]
        sent[pl.ds(i, count, stride=channels), :] = total


def flux_kernel(halves, slots, atm, diffusion, surface, north, south, east, west, weight, next_ref, sent, held, split, placed, sems):
    start_weights(weight, held, sems)
    placed[...] = jnp.zeros(placed.shape, F32)
    east_turned, west_turned = jnp.transpose(east[...]), jnp.transpose(west[...])
    u, v, coef = atm[0, 0], atm[1, 0], diffusion[...]
    after = []
    for i in range(4):
        a = atm[i, 0]
        sides = neighbours(
            a, north[i : i + 1, :], south[i : i + 1, :], column(east_turned, i, halves), column(west_turned, i, halves)
        )
        after.append(atm_step(a, u, v, coef, sides))
        next_ref[i, 0] = after[i]
    du, dv = after[0] - surface[1], after[1] - surface[2]
    speed = jnp.sqrt(1.0 + du * du + dv * dv)
    sst, humidity = surface[0], after[3]
    moisture = moisture_coef * speed * (sst - humidity) - rain_coef * humidity * humidity
    put_split(
        [heat_coef * speed * (after[2] - sst), moisture, drag_coef * speed * du, drag_coef * speed * dv], split
    )
    product_rows(slots, weight, held, sems, split, placed, sent, 4)


def atm_rest_kernel(halves, atm, diffusion, north, south, east, west, started, out, turned_e, turned_w):
    level = pl.program_id(0)

    @pl.when(level == 0)
    def _():
        turned_e[...] = jnp.transpose(east[...])
        turned_w[...] = jnp.transpose(west[...])

    u, v, coef = atm[0, 0], atm[1, 0], diffusion[...]
    te, tw = turned_e[...], turned_w[...]
    per_variable = 3
    lane = lax.broadcasted_iota(jnp.int32, te.shape, 1)
    for i in range(4):
        at = i * per_variable + level
        a = atm[i, 0]

        def pick(t, at=at):
            parts = [
                jnp.sum(jnp.where(lane == at * halves + h, t, 0.0), axis=1, keepdims=True) for h in range(halves)
            ]
            return jnp.concatenate(parts, axis=0)

        sides = neighbours(a, north[pl.ds(at, 1), :], south[pl.ds(at, 1), :], pick(te), pick(tw))
        out[i, 0] = atm_step(a, u, v, coef, sides)


def ocean_kernel(halves, base, levels, ocean, land, north, south, east, west, out, count, turned_e, turned_w):
    var = pl.program_id(0)
    mask = land[...].astype(F32)

    @pl.when(var == 0)
    def _():
        turned_e[...] = jnp.transpose(east[...])
        turned_w[...] = jnp.transpose(west[...])
        at = base + 4 * levels
        n, s, e, w = neighbours(
            mask,
            north[at : at + 1, :],
            south[at : at + 1, :],
            column(turned_e[...], at, halves),
            column(turned_w[...], at, halves),
        )
        count[...] = n + s + e + w

    te, tw = turned_e[...], turned_w[...]
    lane = lax.broadcasted_iota(jnp.int32, te.shape, 1)
    for level in range(levels):
        at = base + var * levels + level
        o = ocean[0, level]

        def pick(t, at=at):
            parts = [
                jnp.sum(jnp.where(lane == at * halves + h, t, 0.0), axis=1, keepdims=True) for h in range(halves)
            ]
            return jnp.concatenate(parts, axis=0)

        n, s, e, w = neighbours(o * mask, north[pl.ds(at, 1), :], south[pl.ds(at, 1), :], pick(te), pick(tw))
        lateral = n + s + e + w - count[...] * o
        vertical = ocean[0, max(level - 1, 0)] + ocean[0, min(level + 1, levels - 1)] - 2.0 * o
        out[0, level] = mask * (o + ocean_diffusion * lateral + vertical_mixing * vertical)


def arrivals_kernel(devices, capacity, me, lists, first, second):
    rows = lists.shape[2]
    j = lax.broadcasted_iota(jnp.int32, (rows, rows), 0)
    i = lax.broadcasted_iota(jnp.int32, (rows, rows), 1)
    before = jnp.where(j < i, 1.0, 0.0).astype(BF16)
    for which, out in enumerate((first, second)):
        named = lists[2 * which] == me[0]
        rank = jnp.dot(
            jnp.where(named, 1.0, 0.0).astype(BF16), before, preferred_element_type=F32
        )
        row = jnp.where(named, (lists[2 * which + 1] + 1).astype(F32), 0.0)
        parts = [jnp.where(rank == float(k), row, 0.0) for k in range(capacity)]
        table = jnp.concatenate(parts, axis=0).astype(BF16)
        total = lax.dot_general(
            jnp.ones((8, rows), BF16), table, (((1,), (1,)), ((), ())), preferred_element_type=F32
        )
        out[...] = total.astype(jnp.int32) - 1


def summed_rows(devices, capacity, rows, arrived, target, channels):
    width = devices * capacity
    row = lax.broadcasted_iota(jnp.int32, (rows, width), 0)
    chosen = jnp.where(row == target[0:1, :], 1.0, 0.0).astype(BF16)
    columns = []
    for i in range(channels):
        parts = [
            arrived[pl.ds(k * channels + i, devices, stride=capacity * channels), :] for k in range(capacity)
        ]
        x = jnp.concatenate(parts, axis=0)
        high = x.astype(BF16)
        columns += [high, (x - high.astype(F32)).astype(BF16)]
    total = jnp.dot(chosen, jnp.concatenate(columns, axis=1), preferred_element_type=F32)
    return [
        total[:, 2 * i * LANES : (2 * i + 1) * LANES] + total[:, (2 * i + 1) * LANES : (2 * i + 2) * LANES]
        for i in range(channels)
    ]


def forced_kernel(devices, capacity, slots, arrived, target, land, base, weight, next_ref, sent, held, split, placed, sems):
    start_weights(weight, held, sems)
    placed[...] = jnp.zeros(placed.shape, F32)
    rows = held.shape[0]
    mask = land[...].astype(F32)
    forcing = summed_rows(devices, capacity, rows, arrived, target, 4)
    after = []
    for i in range(4):
        after.append(base[i, 0] + mask * (forcing_gain * forcing[i]))
        next_ref[i, 0] = after[i]
    put_split([after[0], after[2], after[3]], split)
    product_rows(slots, weight, held, sems, split, placed, sent, 3)


def surface_kernel(devices, capacity, arrived, target, out):
    for i, total in enumerate(summed_rows(devices, capacity, out.shape[1], arrived, target, 3)):
        out[i] = total


def slots_of(destination, capacity):
    owner = destination[:, 0]
    positions = jnp.arange(owner.shape[0], dtype=jnp.int32)
    earlier = (owner[:, None] == owner[None, :]) & (positions[None, :] < positions[:, None])
    return owner * capacity + jnp.sum(earlier.astype(jnp.int32), axis=1)


def whole(x):
    return pl.BlockSpec(x.shape, lambda *_: (0,) * len(x.shape))


def level_zero(x):
    return pl.BlockSpec((x.shape[0], 1) + x.shape[2:], lambda *_: (0, 0, 0, 0))


ANY = pl.BlockSpec(memory_space=pl.ANY)


def body(
    atm_state, ocean_state, surface_state, atm_diffusion, land_sea, flux_dest, flux_row, flux_weight, surface_dest,
    surface_row, surface_weight,
):
    variables, levels, rows, cols = atm_state.shape
    devices = lax.axis_size("comp") * lax.axis_size("lon")
    capacity = max(2, 2 * rows // devices)
    width = devices * capacity
    halves = rows // LANES
    f32 = functools.partial(jax.ShapeDtypeStruct, dtype=F32)

    lists = jnp.stack([flux_dest[:, 0], flux_row, surface_dest[:, 0], surface_row])
    gathered = jnp.transpose(lax.all_gather(lists, AXES), (1, 0, 2))
    me = (lax.axis_index("comp") * lax.axis_size("lon") + lax.axis_index("lon")).reshape(1)
    flux_slots, surface_slots = slots_of(flux_dest, capacity), slots_of(surface_dest, capacity)

    edge_rows, edge_cols = f32((8, cols)), f32((8 * halves, cols))
    edge_rows0, edge_cols0 = f32((variables, cols)), f32((variables * halves, cols))
    edges = pl.pallas_call(
        functools.partial(atm_edges_kernel, halves, variables),
        grid=(1,),
        in_specs=[level_zero(atm_state)],
        out_specs=[whole(e) for e in (edge_rows0, edge_rows0, edge_cols0, edge_cols0)],
        out_shape=[edge_rows0, edge_rows0, edge_cols0, edge_cols0],
        compiler_params=params(),
        name="atm_edges",
    )(atm_state)
    north, south, east, west = exchange(*edges)

    work = [
        pltpu.VMEM((rows, cols, cols), BF16),
        pltpu.VMEM((rows * 8, cols), F32),
        pltpu.VMEM((width, 8, cols), F32),
        pltpu.SemaphoreType.DMA((CHUNKS,)),
    ]
    sent_shape = f32((width * 4, cols))
    atm_started, sent = pl.pallas_call(
        functools.partial(flux_kernel, halves),
        grid_spec=pltpu.PrefetchScalarGridSpec(
            num_scalar_prefetch=1,
            grid=(1,),
            in_specs=[level_zero(atm_state), whole(atm_diffusion), whole(surface_state)]
            + [whole(e) for e in (north, south, east, west)]
            + [ANY],
            out_specs=[level_zero(atm_state), whole(sent_shape)],
            scratch_shapes=work,
        ),
        out_shape=[f32(atm_state.shape), sent_shape],
        compiler_params=params(),
        name="fluxes",
    )(flux_slots, atm_state, atm_diffusion, surface_state, north, south, east, west, flux_weight)
    arrived = lax.all_to_all(
        sent.reshape(devices, capacity * 4, cols), AXES, split_axis=0, concat_axis=0, tiled=True
    ).reshape(width * 4, cols)

    count = variables * (levels - 1) + variables * levels + 1
    padded = -(-count // 8) * 8
    rest_rows, rest_cols = f32((padded, cols)), f32((padded * halves, cols))
    rest = pl.pallas_call(
        functools.partial(rest_edges_kernel, halves, variables, levels),
        grid=(1,),
        in_specs=[whole(atm_state), whole(ocean_state), whole(land_sea)],
        out_specs=[whole(e) for e in (rest_rows, rest_rows, rest_cols, rest_cols)],
        out_shape=[rest_rows, rest_rows, rest_cols, rest_cols],
        compiler_params=params(),
        name="rest_edges",
    )(atm_state, ocean_state, land_sea)
    rest = exchange(*rest)
    turned = [pltpu.VMEM((cols, padded * halves), F32)] * 2
    atm_next = pl.pallas_call(
        functools.partial(atm_rest_kernel, halves),
        grid=(levels - 1,),
        in_specs=[pl.BlockSpec((variables, 1, rows, cols), lambda i: (0, i + 1, 0, 0)), whole(atm_diffusion)]
        + [whole(e) for e in rest]
        + [ANY],
        out_specs=pl.BlockSpec((variables, 1, rows, cols), lambda i: (0, i + 1, 0, 0)),
        out_shape=f32(atm_state.shape),
        scratch_shapes=turned,
        input_output_aliases={6: 0},
        compiler_params=params(),
        name="atm_rest",
    )(atm_state, atm_diffusion, *rest, atm_started)
    ocean_base = pl.pallas_call(
        functools.partial(ocean_kernel, halves, variables * (levels - 1), levels),
        grid=(variables,),
        in_specs=[pl.BlockSpec((1, levels, rows, cols), lambda i: (i, 0, 0, 0)), whole(land_sea)]
        + [whole(e) for e in rest],
        out_specs=pl.BlockSpec((1, levels, rows, cols), lambda i: (i, 0, 0, 0)),
        out_shape=f32(ocean_state.shape),
        scratch_shapes=[pltpu.VMEM((rows, cols), F32)] + turned,
        compiler_params=params(),
        name="ocean_base",
    )(ocean_state, land_sea, *rest)
    target = jax.ShapeDtypeStruct((8, width), jnp.int32)
    flux_target, surface_target = pl.pallas_call(
        functools.partial(arrivals_kernel, devices, capacity),
        grid_spec=pltpu.PrefetchScalarGridSpec(
            num_scalar_prefetch=1,
            grid=(1,),
            in_specs=[whole(gathered)],
            out_specs=[whole(target)] * 2,
        ),
        out_shape=[target, target],
        compiler_params=params(),
        name="arrivals",
    )(me, gathered)

    back_shape = f32((width * 3, cols))
    ocean_next, back = pl.pallas_call(
        functools.partial(forced_kernel, devices, capacity),
        grid_spec=pltpu.PrefetchScalarGridSpec(
            num_scalar_prefetch=1,
            grid=(1,),
            in_specs=[whole(arrived), whole(flux_target), whole(land_sea), level_zero(ocean_base), ANY],
            out_specs=[level_zero(ocean_base), whole(back_shape)],
            scratch_shapes=work,
        ),
        out_shape=[f32(ocean_state.shape), back_shape],
        input_output_aliases={4: 0},
        compiler_params=params(),
        name="forced",
    )(surface_slots, arrived, flux_target, land_sea, ocean_base, surface_weight)
    returned = lax.all_to_all(
        back.reshape(devices, capacity * 3, cols), AXES, split_axis=0, concat_axis=0, tiled=True
    ).reshape(width * 3, cols)
    surface_next = pl.pallas_call(
        functools.partial(surface_kernel, devices, capacity),
        grid=(1,),
        in_specs=[whole(returned), whole(surface_target)],
        out_specs=whole(surface_state),
        out_shape=f32(surface_state.shape),
        compiler_params=params(),
        name="surface",
    )(returned, surface_target)
    return (atm_next, ocean_next, surface_next)


def solution(mesh):
    in_specs = (
        P(None, None, "comp", "lon"),
        P(None, None, "comp", "lon"),
        P(None, "comp", "lon"),
        P("comp", "lon"),
        P("comp", "lon"),
        P(("comp", "lon"), None),
        P(("comp", "lon")),
        P(("comp", "lon"), None, None),
        P(("comp", "lon"), None),
        P(("comp", "lon")),
        P(("comp", "lon"), None, None),
    )
    out_specs = (P(None, None, "comp", "lon"), P(None, None, "comp", "lon"), P(None, "comp", "lon"))
    return jax.shard_map(body, mesh=mesh, in_specs=in_specs, out_specs=out_specs, check_vma=False)
```

```python
import functools

import jax
import jax.numpy as jnp
from jax import lax
from jax.experimental import pallas as pl
from jax.experimental.pallas import tpu as pltpu
from jax.sharding import PartitionSpec as P

time_step = 0.1
ocean_diffusion = 0.2
vertical_mixing = 0.2
drag_coef = 0.4
heat_coef = 0.5
moisture_coef = 0.3
rain_coef = 0.2
forcing_gain = 0.5

AXES = ("comp", "lon")
LANES = 128
CHUNKS = 4
F32 = jnp.float32
BF16 = jnp.bfloat16
VMEM_LIMIT = 24 << 20


def cost(microseconds):
    return pl.CostEstimate(flops=int(microseconds * 1e9), bytes_accessed=1 << 20, transcendentals=0)


def params(**kw):
    return pltpu.CompilerParams(vmem_limit_bytes=VMEM_LIMIT, **kw)


def shift(x, axis, up, wrap):
    devices = lax.axis_size(axis)
    pairs = [(i, (i + 1) % devices) for i in range(devices if wrap else devices - 1)]
    if not up:
        pairs = [(j, i) for i, j in pairs]
    return lax.ppermute(x, axis, pairs)


def exchange(first_rows, last_rows, first_cols, last_cols):
    north = shift(first_rows, "comp", False, False)
    south = shift(last_rows, "comp", True, False)
    east = shift(first_cols, "lon", False, True)
    west = shift(last_cols, "lon", True, True)
    return north, south, east, west


def put_edges(field, at, halves, refs):
    first_rows, last_rows, first_cols, last_cols = refs
    rows = field.shape[0]
    first_rows[at : at + 1, :] = field[0:1, :]
    last_rows[at : at + 1, :] = field[rows - 1 : rows, :]
    for h in range(halves):
        turned = jnp.transpose(field[h * LANES : (h + 1) * LANES, :])
        row = at * halves + h
        first_cols[row : row + 1, :] = turned[0:1, :]
        last_cols[row : row + 1, :] = turned[LANES - 1 : LANES, :]


def neighbours(x, north, south, east, west):
    rows, cols = x.shape
    row = lax.broadcasted_iota(jnp.int32, x.shape, 0)
    col = lax.broadcasted_iota(jnp.int32, x.shape, 1)
    n = jnp.where(row == rows - 1, north, pltpu.roll(x, rows - 1, 0))
    s = jnp.where(row == 0, south, pltpu.roll(x, 1, 0))
    e = jnp.where(col == cols - 1, east, pltpu.roll(x, cols - 1, 1))
    w = jnp.where(col == 0, west, pltpu.roll(x, 1, 1))
    return n, s, e, w


def column(turned, at, halves):
    parts = [turned[:, at * halves + h : at * halves + h + 1] for h in range(halves)]
    return jnp.concatenate(parts, axis=0)


def atm_edges_kernel(halves, count, atm, held, first_rows, last_rows, first_cols, last_cols, sem):
    copy = pltpu.make_async_copy(atm.at[:, 0], held, sem)
    copy.start()
    copy.wait()
    for at in range(count):
        put_edges(held[at], at, halves, (first_rows, last_rows, first_cols, last_cols))


def rest_edges_kernel(halves, variables, levels, atm, ocean, land, *outs):
    at = 0
    for v in range(variables):
        for level in range(1, levels):
            put_edges(atm[v, level], at, halves, outs)
            at += 1
    mask = land[...].astype(F32)
    for v in range(variables):
        for level in range(levels):
            put_edges(ocean[v, level] * mask, at, halves, outs)
            at += 1
    put_edges(mask, at, halves, outs)
    for ref in outs:
        used = (at + 1) * (ref.shape[0] // outs[0].shape[0])
        if used < ref.shape[0]:
            ref[used:, :] = jnp.zeros((ref.shape[0] - used, LANES), F32)


def atm_step(a, u, v, diffusion, sides):
    n, s, e, w = sides
    laplace = n + s + e + w - 4.0 * a
    advection = u * (e - w) + v * (n - s)
    return a + diffusion * laplace - 0.5 * time_step * advection


def put_split(fields, high_ref, low_ref):
    rows = fields[0].shape[0]
    for i in range(4):
        if i < len(fields):
            high = fields[i].astype(BF16).astype(F32)
            low = fields[i] - high
        else:
            high = low = jnp.zeros((rows, LANES), F32)
        high_ref[pl.ds(i, rows, stride=4), :] = high
        low_ref[pl.ds(i, rows, stride=4), :] = low


def start_weights(weight, held, sems):
    part = held.shape[0] // CHUNKS
    for c in range(CHUNKS):
        rows = pl.ds(c * part, part)
        pltpu.make_async_copy(weight.at[rows], held.at[rows], sems.at[c]).start()


def product_rows(slots, weight, held, sems, high_ref, low_ref, placed, channels):
    part = held.shape[0] // CHUNKS

    def some(c, carry):
        rows = pl.ds(c * part, part)
        pltpu.make_async_copy(weight.at[rows], held.at[rows], sems.at[c]).wait()
        for i in range(0, part, 2):
            r = c * part + i
            at = pl.ds(pl.multiple_of(r * 4, 8), 8)
            left = jnp.concatenate([high_ref[at, :].astype(BF16), low_ref[at, :].astype(BF16)], axis=0)
            right = jnp.concatenate([held[r], held[r + 1]], axis=1)
            both = jnp.dot(left, right, preferred_element_type=F32)
            both = both[:8] + both[8:]
            placed[pl.ds(slots[r] * channels, channels), :] = both[:channels, :LANES]
            placed[pl.ds(slots[r + 1] * channels, channels), :] = both[4 : 4 + channels, LANES:]
        return carry

    lax.fori_loop(0, CHUNKS, some, 0)


def flux_kernel(halves, slots_in, atm, diffusion, surface, north, south, east, west, weight, next_ref, sent, slots, held, high_ref, low_ref, placed, sems, weight_sems):
    start_weights(weight, held, weight_sems)
    read = pltpu.make_async_copy(slots_in, slots, sems.at[0])
    read.start()
    placed[...] = jnp.zeros(placed.shape, F32)
    east_turned, west_turned = jnp.transpose(east[...]), jnp.transpose(west[...])
    u, v, coef = atm[0], atm[1], diffusion[...]
    after = []
    for i in range(4):
        sides = neighbours(
            atm[i], north[i : i + 1, :], south[i : i + 1, :], column(east_turned, i, halves), column(west_turned, i, halves)
        )
        after.append(atm_step(atm[i], u, v, coef, sides))
        next_ref[i, 0] = after[i]
    du, dv = after[0] - surface[1], after[1] - surface[2]
    speed = jnp.sqrt(1.0 + du * du + dv * dv)
    sst, humidity = surface[0], after[3]
    moisture = moisture_coef * speed * (sst - humidity) - rain_coef * humidity * humidity
    put_split(
        [heat_coef * speed * (after[2] - sst), moisture, drag_coef * speed * du, drag_coef * speed * dv],
        high_ref,
        low_ref,
    )
    read.wait()
    product_rows(slots, weight, held, weight_sems, high_ref, low_ref, placed, 4)
    write = pltpu.make_async_copy(placed, sent, sems.at[1])
    write.start()
    write.wait()


def atm_rest_kernel(halves, per_variable, atm, diffusion, north, south, east, west, started, out, turned_e, turned_w):
    level = pl.program_id(0)

    @pl.when(level == 0)
    def _():
        turn_columns(east, west, turned_e, turned_w)

    u, v, coef = atm[0, 0], atm[1, 0], diffusion[...]
    te, tw = turned_e[...], turned_w[...]
    for i in range(4):
        at = i * per_variable + level
        a = atm[i, 0]
        sides = neighbours(
            a, north[pl.ds(at, 1), :], south[pl.ds(at, 1), :], picked(te, at, halves), picked(tw, at, halves)
        )
        out[i, 0] = atm_step(a, u, v, coef, sides)


def turn_columns(east, west, turned_e, turned_w):
    turned_e[...] = jnp.transpose(east[...])
    turned_w[...] = jnp.transpose(west[...])


def picked(turned, at, halves):
    lane = lax.broadcasted_iota(jnp.int32, turned.shape, 1)
    parts = [jnp.sum(jnp.where(lane == at * halves + h, turned, 0.0), axis=1, keepdims=True) for h in range(halves)]
    return jnp.concatenate(parts, axis=0)


def sea_count(at, halves, mask, north, south, te, tw):
    row = slice(at, at + 1)
    n, s, e, w = neighbours(mask, north[row, :], south[row, :], column(te, at, halves), column(tw, at, halves))
    return n + s + e + w


def ocean_step(o, above, below, mask, count, sides):
    n, s, e, w = sides
    lateral = n + s + e + w - count * o
    vertical = above + below - 2.0 * o
    return mask * (o + ocean_diffusion * lateral + vertical_mixing * vertical)


def ocean_top_kernel(halves, base, levels, ocean, land, north, south, east, west, out):
    mask = land[...].astype(F32)
    te, tw = jnp.transpose(east[...]), jnp.transpose(west[...])
    count = sea_count(base + 4 * levels, halves, mask, north, south, te, tw)
    for var in range(4):
        at = base + var * levels
        o = ocean[var, 0]
        sides = neighbours(
            o * mask, north[at : at + 1, :], south[at : at + 1, :], column(te, at, halves), column(tw, at, halves)
        )
        out[var] = ocean_step(o, o, ocean[var, min(1, levels - 1)], mask, count, sides)


def ocean_rest_kernel(halves, base, levels, ocean, land, north, south, east, west, started, out, sem, made, count, turned_e, turned_w):
    var = pl.program_id(0)
    mask = land[...].astype(F32)

    @pl.when(var == 0)
    def _():
        turn_columns(east, west, turned_e, turned_w)
        count[...] = sea_count(base + 4 * levels, halves, mask, north, south, turned_e[...], turned_w[...])

    te, tw = turned_e[...], turned_w[...]
    for level in range(1, levels):
        at = base + var * levels + level
        o = ocean[0, level]
        sides = neighbours(
            o * mask, north[pl.ds(at, 1), :], south[pl.ds(at, 1), :], picked(te, at, halves), picked(tw, at, halves)
        )
        made[level - 1] = ocean_step(
            o, ocean[0, level - 1], ocean[0, min(level + 1, levels - 1)], mask, count[...], sides
        )
    write = pltpu.make_async_copy(made, out.at[var, pl.ds(1, levels - 1)], sem)
    write.start()
    write.wait()


def all_lists(lists):
    devices = lax.axis_size("comp") * lax.axis_size("lon")
    held, bit = lists[None], 1
    while bit < devices:
        other = lax.ppermute(held, AXES, [(i, i ^ bit) for i in range(devices)])
        held, bit = jnp.concatenate([held, other], axis=0), 2 * bit
    return held


def arrivals_kernel(devices, capacity, me, lists, first, second, sorted_ref):
    kinds, rows = lists.shape[1:]
    for s in range(devices):
        block = lists[me[0] ^ s]
        for kind in range(kinds):
            sorted_ref[kind, s : s + 1, :] = block[kind : kind + 1]
    j = lax.broadcasted_iota(jnp.int32, (rows, rows), 0)
    i = lax.broadcasted_iota(jnp.int32, (rows, rows), 1)
    before = jnp.where(j < i, 1.0, 0.0).astype(BF16)
    for which, out in enumerate((first, second)):
        named = sorted_ref[2 * which] == me[0]
        target = sorted_ref[2 * which + 1]
        rank = jnp.dot(jnp.where(named, 1.0, 0.0).astype(BF16), before, preferred_element_type=F32)
        row = jnp.where(named, (target + 1).astype(F32), 0.0)
        parts = [jnp.where(rank == float(k), row, 0.0) for k in range(capacity)]
        table = jnp.concatenate(parts, axis=0).astype(BF16)
        total = lax.dot_general(
            jnp.ones((8, rows), BF16), table, (((1,), (1,)), ((), ())), preferred_element_type=F32
        )
        out[...] = total.astype(jnp.int32) - 1


def summed_rows(devices, capacity, rows, arrived, target, channels):
    width = devices * capacity
    row = lax.broadcasted_iota(jnp.int32, (rows, width), 0)
    chosen = jnp.where(row == target[0:1, :], 1.0, 0.0).astype(BF16)
    columns = []
    for i in range(channels):
        parts = [
            arrived[pl.ds(k * channels + i, devices, stride=capacity * channels), :] for k in range(capacity)
        ]
        x = jnp.concatenate(parts, axis=0)
        high = x.astype(BF16)
        columns += [high, (x - high.astype(F32)).astype(BF16)]
    total = jnp.dot(chosen, jnp.concatenate(columns, axis=1), preferred_element_type=F32)
    return [
        total[:, 2 * i * LANES : (2 * i + 1) * LANES] + total[:, (2 * i + 1) * LANES : (2 * i + 2) * LANES]
        for i in range(channels)
    ]


def forced_kernel(devices, capacity, slots_in, arrived, target, land, base, weight, next_ref, sent, slots, held, high_ref, low_ref, placed, sems, weight_sems, base_held):
    base_read = pltpu.make_async_copy(base, base_held, sems.at[2])
    base_read.start()
    start_weights(weight, held, weight_sems)
    read = pltpu.make_async_copy(slots_in, slots, sems.at[0])
    read.start()
    placed[...] = jnp.zeros(placed.shape, F32)
    mask = land[...].astype(F32)
    forcing = summed_rows(devices, capacity, land.shape[0], arrived, target, 4)
    base_read.wait()
    after = []
    for i in range(4):
        after.append(base_held[i] + mask * (forcing_gain * forcing[i]))
        next_ref[i, 0] = after[i]
    put_split([after[0], after[2], after[3]], high_ref, low_ref)
    read.wait()
    product_rows(slots, weight, held, weight_sems, high_ref, low_ref, placed, 3)
    write = pltpu.make_async_copy(placed, sent, sems.at[1])
    write.start()
    write.wait()


def surface_kernel(devices, capacity, arrived, target, out):
    for i, total in enumerate(summed_rows(devices, capacity, out.shape[1], arrived, target, 3)):
        out[i] = total


def slots_of(destination, capacity):
    owner = destination[:, 0]
    positions = jnp.arange(owner.shape[0], dtype=jnp.int32)
    earlier = (owner[:, None] == owner[None, :]) & (positions[None, :] < positions[:, None])
    return owner * capacity + jnp.sum(earlier.astype(jnp.int32), axis=1)


def whole(x):
    return pl.BlockSpec(x.shape, lambda *_: (0,) * len(x.shape))


def level_zero(x):
    return pl.BlockSpec((x.shape[0], 1) + x.shape[2:], lambda *_: (0, 0, 0, 0))


ANY = pl.BlockSpec(memory_space=pl.ANY)


def in_hbm(x):
    return pltpu.with_memory_space_constraint(x, pltpu.HBM)


def body(
    atm_state, ocean_state, surface_state, atm_diffusion, land_sea, flux_dest, flux_row, flux_weight, surface_dest,
    surface_row, surface_weight,
):
    variables, levels, rows, cols = atm_state.shape
    devices = lax.axis_size("comp") * lax.axis_size("lon")
    capacity = max(2, 2 * rows // devices)
    width = devices * capacity
    halves = rows // LANES
    f32 = functools.partial(jax.ShapeDtypeStruct, dtype=F32)
    flux_slots, surface_slots = slots_of(flux_dest, capacity), slots_of(surface_dest, capacity)

    top = f32((variables, rows, cols))
    top_rows, top_cols = f32((variables, cols)), f32((variables * halves, cols))
    atm_top, *edges = pl.pallas_call(
        functools.partial(atm_edges_kernel, halves, variables),
        grid=(1,),
        in_specs=[ANY],
        out_specs=[whole(e) for e in (top, top_rows, top_rows, top_cols, top_cols)],
        out_shape=[top, top_rows, top_rows, top_cols, top_cols],
        scratch_shapes=[pltpu.SemaphoreType.DMA(())],
        compiler_params=params(),
        cost_estimate=cost(8),
        name="atm_edges",
    )(in_hbm(atm_state))
    sides = exchange(*edges)

    def work(channels):
        return [
            pltpu.SMEM((rows,), jnp.int32),
            pltpu.VMEM((rows, cols, cols), BF16),
            pltpu.VMEM((rows * 4, cols), F32),
            pltpu.VMEM((rows * 4, cols), F32),
            pltpu.VMEM((width * channels, cols), F32),
            pltpu.SemaphoreType.DMA((3,)),
            pltpu.SemaphoreType.DMA((CHUNKS,)),
        ]

    atm_started, sent = pl.pallas_call(
        functools.partial(flux_kernel, halves),
        grid=(1,),
        in_specs=[ANY]
        + [whole(e) for e in (atm_top, atm_diffusion, surface_state, *sides)]
        + [ANY],
        out_specs=[level_zero(atm_state), ANY],
        scratch_shapes=work(4),
        out_shape=[f32(atm_state.shape), pltpu.HBM((width * 4, cols), F32)],
        compiler_params=params(),
        cost_estimate=cost(5),
        name="fluxes",
    )(in_hbm(flux_slots), atm_top, atm_diffusion, surface_state, *sides, in_hbm(flux_weight))
    arrived = lax.all_to_all(
        sent.reshape(devices, capacity * 4, cols), AXES, split_axis=0, concat_axis=0, tiled=True
    ).reshape(width * 4, cols)

    lists = jnp.stack([flux_dest[:, 0], flux_row, surface_dest[:, 0], surface_row])
    lists, land, _ = lax.optimization_barrier((lists, land_sea, sent))
    count = variables * (levels - 1) + variables * levels + 1
    padded = -(-count // 8) * 8
    rest_rows, rest_cols = f32((padded, cols)), f32((padded * halves, cols))
    rest = pl.pallas_call(
        functools.partial(rest_edges_kernel, halves, variables, levels),
        grid=(1,),
        in_specs=[whole(atm_state), whole(ocean_state), whole(land_sea)],
        out_specs=[whole(e) for e in (rest_rows, rest_rows, rest_cols, rest_cols)],
        out_shape=[rest_rows, rest_rows, rest_cols, rest_cols],
        compiler_params=params(),
        cost_estimate=cost(8),
        name="rest_edges",
    )(atm_state, ocean_state, land)
    rest = exchange(*rest)
    base = variables * (levels - 1)
    ocean_top = pl.pallas_call(
        functools.partial(ocean_top_kernel, halves, base, levels),
        grid=(1,),
        in_specs=[pl.BlockSpec((variables, min(2, levels), rows, cols), lambda i: (0, 0, 0, 0)), whole(land_sea)]
        + [whole(e) for e in rest],
        out_specs=whole(top),
        out_shape=pltpu.HBM(top.shape, F32),
        compiler_params=params(),
        cost_estimate=cost(4),
        name="ocean_top",
    )(ocean_state, land_sea, *rest)
    gathered = all_lists(lists)
    me = (lax.axis_index("comp") * lax.axis_size("lon") + lax.axis_index("lon")).reshape(1)
    target = jax.ShapeDtypeStruct((8, width), jnp.int32)
    flux_target, surface_target = pl.pallas_call(
        functools.partial(arrivals_kernel, devices, capacity),
        grid_spec=pltpu.PrefetchScalarGridSpec(
            num_scalar_prefetch=1,
            grid=(1,),
            in_specs=[whole(gathered)],
            out_specs=[whole(target)] * 2,
            scratch_shapes=[pltpu.VMEM((gathered.shape[1], devices, rows), jnp.int32)],
        ),
        out_shape=[target, target],
        compiler_params=params(),
        cost_estimate=cost(1),
        name="arrivals",
    )(me, gathered)

    ocean_started, back = pl.pallas_call(
        functools.partial(forced_kernel, devices, capacity),
        grid=(1,),
        in_specs=[ANY] + [whole(e) for e in (arrived, flux_target, land_sea)] + [ANY, ANY],
        out_specs=[level_zero(ocean_state), ANY],
        scratch_shapes=work(3) + [pltpu.VMEM(top.shape, F32)],
        out_shape=[f32(ocean_state.shape), pltpu.HBM((width * 3, cols), F32)],
        compiler_params=params(),
        cost_estimate=cost(5),
        name="forced",
    )(in_hbm(surface_slots), arrived, flux_target, land_sea, in_hbm(ocean_top), in_hbm(surface_weight))
    returned = lax.all_to_all(
        back.reshape(devices, capacity * 3, cols), AXES, split_axis=0, concat_axis=0, tiled=True
    ).reshape(width * 3, cols)

    turned = [pltpu.VMEM((cols, padded * halves), F32)] * 2
    one_level = pl.BlockSpec((variables, 1, rows, cols), lambda i: (0, i + 1, 0, 0))
    atm_next = pl.pallas_call(
        functools.partial(atm_rest_kernel, halves, levels - 1),
        grid=(levels - 1,),
        in_specs=[one_level, whole(atm_diffusion)] + [whole(e) for e in rest] + [ANY],
        out_specs=one_level,
        out_shape=f32(atm_state.shape),
        scratch_shapes=turned,
        input_output_aliases={6: 0},
        compiler_params=params(),
        cost_estimate=cost(5),
        name="atm_rest",
    )(atm_state, atm_diffusion, *rest, atm_started)
    ocean_next = pl.pallas_call(
        functools.partial(ocean_rest_kernel, halves, base, levels),
        grid=(variables,),
        in_specs=[pl.BlockSpec((1, levels, rows, cols), lambda i: (i, 0, 0, 0)), whole(land_sea)]
        + [whole(e) for e in rest]
        + [ANY],
        out_specs=ANY,
        out_shape=f32(ocean_state.shape),
        scratch_shapes=[
            pltpu.SemaphoreType.DMA(()),
            pltpu.VMEM((levels - 1, rows, cols), F32),
            pltpu.VMEM((rows, cols), F32),
        ]
        + turned,
        input_output_aliases={6: 0},
        compiler_params=params(),
        cost_estimate=cost(6),
        name="ocean_rest",
    )(ocean_state, land_sea, *rest, ocean_started)
    surface_next = pl.pallas_call(
        functools.partial(surface_kernel, devices, capacity),
        grid=(1,),
        in_specs=[whole(returned), whole(surface_target)],
        out_specs=whole(surface_state),
        out_shape=f32(surface_state.shape),
        compiler_params=params(),
        cost_estimate=cost(1),
        name="surface",
    )(returned, surface_target)
    return (atm_next, ocean_next, surface_next)


def solution(mesh):
    in_specs = (
        P(None, None, "comp", "lon"),
        P(None, None, "comp", "lon"),
        P(None, "comp", "lon"),
        P("comp", "lon"),
        P("comp", "lon"),
        P(("comp", "lon"), None),
        P(("comp", "lon")),
        P(("comp", "lon"), None, None),
        P(("comp", "lon"), None),
        P(("comp", "lon")),
        P(("comp", "lon"), None, None),
    )
    out_specs = (P(None, None, "comp", "lon"), P(None, None, "comp", "lon"), P(None, "comp", "lon"))
    return jax.shard_map(body, mesh=mesh, in_specs=in_specs, out_specs=out_specs, check_vma=False)
```

```python
import functools

import jax
import jax.numpy as jnp
from jax import lax
from jax.experimental import pallas as pl
from jax.experimental.pallas import tpu as pltpu
from jax.sharding import PartitionSpec as P

time_step = 0.1
ocean_diffusion = 0.2
vertical_mixing = 0.2
drag_coef = 0.4
heat_coef = 0.5
moisture_coef = 0.3
rain_coef = 0.2
forcing_gain = 0.5

AXES = ("comp", "lon")
LANES = 128
CHUNKS = 4
F32 = jnp.float32
BF16 = jnp.bfloat16
VMEM_LIMIT = 24 << 20


def cost(microseconds):
    return pl.CostEstimate(flops=int(microseconds * 1e9), bytes_accessed=1 << 20, transcendentals=0)


def params(**kw):
    return pltpu.CompilerParams(vmem_limit_bytes=VMEM_LIMIT, **kw)


def shift(x, axis, up):
    devices = lax.axis_size(axis)
    pairs = [(i, (i + 1) % devices) for i in range(devices)]
    if not up:
        pairs = [(j, i) for i, j in pairs]
    return lax.ppermute(x, axis, pairs)


def exchange(first_rows, last_rows, first_cols, last_cols):
    north = shift(first_rows, "comp", False)
    south = shift(last_rows, "comp", True)
    east = shift(first_cols, "lon", False)
    west = shift(last_cols, "lon", True)
    return north, south, east, west


def inside():
    at = lax.axis_index("comp")
    return at < lax.axis_size("comp") - 1, at > 0


def cleared(north, south):
    has_north, has_south = inside()
    return jnp.where(has_north, north[...], 0.0), jnp.where(has_south, south[...], 0.0)


def put_edges(field, at, halves, refs):
    first_rows, last_rows, first_cols, last_cols = refs
    rows = field.shape[0]
    first_rows[at : at + 1, :] = field[0:1, :]
    last_rows[at : at + 1, :] = field[rows - 1 : rows, :]
    for h in range(halves):
        turned = jnp.transpose(field[h * LANES : (h + 1) * LANES, :])
        row = at * halves + h
        first_cols[row : row + 1, :] = turned[0:1, :]
        last_cols[row : row + 1, :] = turned[LANES - 1 : LANES, :]


def neighbours(x, north, south, east, west):
    rows, cols = x.shape
    row = lax.broadcasted_iota(jnp.int32, x.shape, 0)
    col = lax.broadcasted_iota(jnp.int32, x.shape, 1)
    n = jnp.where(row == rows - 1, north, pltpu.roll(x, rows - 1, 0))
    s = jnp.where(row == 0, south, pltpu.roll(x, 1, 0))
    e = jnp.where(col == cols - 1, east, pltpu.roll(x, cols - 1, 1))
    w = jnp.where(col == 0, west, pltpu.roll(x, 1, 1))
    return n, s, e, w


def column(turned, at, halves):
    parts = [turned[:, at * halves + h : at * halves + h + 1] for h in range(halves)]
    return jnp.concatenate(parts, axis=0)


def atm_edges_kernel(halves, count, atm, held, first_rows, last_rows, first_cols, last_cols, sem):
    copy = pltpu.make_async_copy(atm.at[:, 0], held, sem)
    copy.start()
    copy.wait()
    for at in range(count):
        put_edges(held[at], at, halves, (first_rows, last_rows, first_cols, last_cols))


def rest_edges_kernel(halves, variables, levels, atm, ocean, land, *outs):
    at = 0
    for v in range(variables):
        for level in range(1, levels):
            put_edges(atm[v, level], at, halves, outs)
            at += 1
    mask = land[...].astype(F32)
    for v in range(variables):
        for level in range(levels):
            put_edges(ocean[v, level] * mask, at, halves, outs)
            at += 1
    put_edges(mask, at, halves, outs)
    for ref in outs:
        used = (at + 1) * (ref.shape[0] // outs[0].shape[0])
        if used < ref.shape[0]:
            ref[used:, :] = jnp.zeros((ref.shape[0] - used, LANES), F32)


def atm_step(a, u, v, diffusion, sides):
    n, s, e, w = sides
    laplace = n + s + e + w - 4.0 * a
    advection = u * (e - w) + v * (n - s)
    return a + diffusion * laplace - 0.5 * time_step * advection


def put_split(fields, high_ref, low_ref):
    rows = fields[0].shape[0]
    for i in range(4):
        if i < len(fields):
            high = fields[i].astype(BF16).astype(F32)
            low = fields[i] - high
        else:
            high = low = jnp.zeros((rows, LANES), F32)
        high_ref[pl.ds(i, rows, stride=4), :] = high
        low_ref[pl.ds(i, rows, stride=4), :] = low


def start_weights(weight, held, sems):
    part = held.shape[0] // CHUNKS
    for c in range(CHUNKS):
        rows = pl.ds(c * part, part)
        pltpu.make_async_copy(weight.at[rows], held.at[rows], sems.at[c]).start()


def product_rows(slots, weight, high_ref, low_ref, placed, channels, ready=None):
    part = weight.shape[0] // CHUNKS

    def some(c, carry):
        if ready is not None:
            ready(c)
        for i in range(0, part, 2):
            r = c * part + i
            at = pl.ds(pl.multiple_of(r * 4, 8), 8)
            left = jnp.concatenate([high_ref[at, :].astype(BF16), low_ref[at, :].astype(BF16)], axis=0)
            right = jnp.concatenate([weight[r], weight[r + 1]], axis=1)
            both = jnp.dot(left, right, preferred_element_type=F32)
            both = both[:8] + both[8:]
            placed[pl.ds(slots[0, r] * channels, channels), :] = both[:channels, :LANES]
            placed[pl.ds(slots[0, r + 1] * channels, channels), :] = both[4 : 4 + channels, LANES:]
        return carry

    lax.fori_loop(0, CHUNKS, some, 0)


def slot_row(destination, capacity):
    rows = destination.shape[1]
    wide = jnp.broadcast_to(destination.astype(F32), (8, rows))
    column_of = jnp.concatenate([jnp.transpose(wide[:, i : i + LANES]) for i in range(0, rows, LANES)], axis=0)[:, 0:1]
    j = lax.broadcasted_iota(jnp.int32, (rows, rows), 0)
    i = lax.broadcasted_iota(jnp.int32, (rows, rows), 1)
    earlier = (column_of == wide[0:1, :]) & (j < i)
    rank = jnp.sum(jnp.where(earlier, 1.0, 0.0), axis=0, keepdims=True)
    return destination * capacity + rank.astype(jnp.int32)


def prepare_kernel(capacity, flux_dest, flux_row, surface_dest, surface_row, weight, edge, held, flux_slots, surface_slots, lists, sem):
    read = pltpu.make_async_copy(weight, held, sem)
    read.start()
    for i, ref in enumerate((flux_dest, flux_row, surface_dest, surface_row)):
        lists[i : i + 1, :] = ref[...]
    flux_slots[...] = slot_row(flux_dest[...], capacity)
    surface_slots[...] = slot_row(surface_dest[...], capacity)
    read.wait()


def flux_kernel(halves, slots_in, atm, diffusion, surface, north, south, east, west, weight, next_ref, sent, slots, high_ref, low_ref, placed, sems):
    read = pltpu.make_async_copy(slots_in, slots, sems.at[0])
    read.start()
    placed[...] = jnp.zeros(placed.shape, F32)
    east_turned, west_turned = jnp.transpose(east[...]), jnp.transpose(west[...])
    u, v, coef = atm[0], atm[1], diffusion[...]
    norths, souths = cleared(north, south)
    after = []
    for i in range(4):
        sides = neighbours(
            atm[i], norths[i : i + 1, :], souths[i : i + 1, :], column(east_turned, i, halves), column(west_turned, i, halves)
        )
        after.append(atm_step(atm[i], u, v, coef, sides))
        next_ref[i, 0] = after[i]
    du, dv = after[0] - surface[1], after[1] - surface[2]
    speed = jnp.sqrt(1.0 + du * du + dv * dv)
    sst, humidity = surface[0], after[3]
    moisture = moisture_coef * speed * (sst - humidity) - rain_coef * humidity * humidity
    put_split(
        [heat_coef * speed * (after[2] - sst), moisture, drag_coef * speed * du, drag_coef * speed * dv],
        high_ref,
        low_ref,
    )
    read.wait()
    product_rows(slots, weight, high_ref, low_ref, placed, 4)
    write = pltpu.make_async_copy(placed, sent, sems.at[1])
    write.start()
    write.wait()


def atm_rest_kernel(halves, per_variable, atm, diffusion, north, south, east, west, started, out, turned_e, turned_w):
    level = pl.program_id(0)

    @pl.when(level == 0)
    def _():
        turn_columns(east, west, turned_e, turned_w)

    u, v, coef = atm[0, 0], atm[1, 0], diffusion[...]
    te, tw = turned_e[...], turned_w[...]
    has_north, has_south = inside()
    for i in range(4):
        at = i * per_variable + level
        a = atm[i, 0]
        n = jnp.where(has_north, north[pl.ds(at, 1), :], 0.0)
        s = jnp.where(has_south, south[pl.ds(at, 1), :], 0.0)
        sides = neighbours(a, n, s, picked(te, at, halves), picked(tw, at, halves))
        out[i, 0] = atm_step(a, u, v, coef, sides)


def turn_columns(east, west, turned_e, turned_w):
    turned_e[...] = jnp.transpose(east[...])
    turned_w[...] = jnp.transpose(west[...])


def picked(turned, at, halves):
    lane = lax.broadcasted_iota(jnp.int32, turned.shape, 1)
    parts = [jnp.sum(jnp.where(lane == at * halves + h, turned, 0.0), axis=1, keepdims=True) for h in range(halves)]
    return jnp.concatenate(parts, axis=0)


def sea_count(at, halves, mask, north, south, te, tw):
    norths, souths = cleared(north, south)
    row = slice(at, at + 1)
    n, s, e, w = neighbours(mask, norths[row, :], souths[row, :], column(te, at, halves), column(tw, at, halves))
    return n + s + e + w


def ocean_step(o, above, below, mask, count, sides):
    n, s, e, w = sides
    lateral = n + s + e + w - count * o
    vertical = above + below - 2.0 * o
    return mask * (o + ocean_diffusion * lateral + vertical_mixing * vertical)


def ocean_top_kernel(halves, base, levels, ocean, land, north, south, east, west, out):
    mask = land[...].astype(F32)
    te, tw = jnp.transpose(east[...]), jnp.transpose(west[...])
    count = sea_count(base + 4 * levels, halves, mask, north, south, te, tw)
    norths, souths = cleared(north, south)
    for var in range(4):
        at = base + var * levels
        o = ocean[var, 0]
        sides = neighbours(
            o * mask, norths[at : at + 1, :], souths[at : at + 1, :], column(te, at, halves), column(tw, at, halves)
        )
        out[var] = ocean_step(o, o, ocean[var, min(1, levels - 1)], mask, count, sides)


def ocean_rest_kernel(halves, base, levels, ocean, land, north, south, east, west, started, out, sem, made, count, turned_e, turned_w):
    var = pl.program_id(0)
    mask = land[...].astype(F32)

    @pl.when(var == 0)
    def _():
        turn_columns(east, west, turned_e, turned_w)
        count[...] = sea_count(base + 4 * levels, halves, mask, north, south, turned_e[...], turned_w[...])

    te, tw = turned_e[...], turned_w[...]
    has_north, has_south = inside()
    for level in range(1, levels):
        at = base + var * levels + level
        o = ocean[0, level]
        n = jnp.where(has_north, north[pl.ds(at, 1), :], 0.0)
        s = jnp.where(has_south, south[pl.ds(at, 1), :], 0.0)
        sides = neighbours(o * mask, n, s, picked(te, at, halves), picked(tw, at, halves))
        made[level - 1] = ocean_step(
            o, ocean[0, level - 1], ocean[0, min(level + 1, levels - 1)], mask, count[...], sides
        )
    write = pltpu.make_async_copy(made, out.at[var, pl.ds(1, levels - 1)], sem)
    write.start()
    write.wait()


def all_lists(lists):
    devices = lax.axis_size("comp") * lax.axis_size("lon")
    held, bit, early = lists[None], 1, lists
    while bit < devices:
        if bit == 4:
            early = held
        other = lax.ppermute(held, AXES, [(i, i ^ bit) for i in range(devices)])
        held, bit = jnp.concatenate([held, other], axis=0), 2 * bit
    return held, early


def arrivals_kernel(devices, capacity, lists, first, second, sorted_ref):
    kinds, rows = lists.shape[1:]
    me = lax.axis_index("comp") * lax.axis_size("lon") + lax.axis_index("lon")
    for s in range(devices):
        block = lists[me ^ s]
        for kind in range(kinds):
            sorted_ref[kind, s : s + 1, :] = block[kind : kind + 1]
    j = lax.broadcasted_iota(jnp.int32, (rows, rows), 0)
    i = lax.broadcasted_iota(jnp.int32, (rows, rows), 1)
    before = jnp.where(j < i, 1.0, 0.0).astype(BF16)
    for which, out in enumerate((first, second)):
        named = sorted_ref[2 * which] == me
        target = sorted_ref[2 * which + 1]
        rank = jnp.dot(jnp.where(named, 1.0, 0.0).astype(BF16), before, preferred_element_type=F32)
        row = jnp.where(named, (target + 1).astype(F32), 0.0)
        parts = [jnp.where(rank == float(k), row, 0.0) for k in range(capacity)]
        table = jnp.concatenate(parts, axis=0).astype(BF16)
        total = lax.dot_general(
            jnp.ones((8, rows), BF16), table, (((1,), (1,)), ((), ())), preferred_element_type=F32
        )
        wanted = lax.broadcasted_iota(jnp.int32, out.shape, 0).astype(F32) + 1.0
        out[...] = jnp.where(wanted == total[0:1, :], 1.0, 0.0).astype(BF16)


def summed_rows(devices, capacity, arrived, chosen, channels, read):
    columns = []
    for i in range(channels):
        parts = [
            arrived[pl.ds(k * channels + i, devices, stride=capacity * channels), :] for k in range(capacity)
        ]
        x = jnp.concatenate(parts, axis=0)
        high = x.astype(BF16)
        columns += [high, (x - high.astype(F32)).astype(BF16)]
    read.wait()
    total = jnp.dot(chosen[...], jnp.concatenate(columns, axis=1), preferred_element_type=F32)
    return [
        total[:, 2 * i * LANES : (2 * i + 1) * LANES] + total[:, (2 * i + 1) * LANES : (2 * i + 2) * LANES]
        for i in range(channels)
    ]


def forced_kernel(devices, capacity, slots_in, arrived, target, land, base, weight, next_ref, sent, slots, high_ref, low_ref, placed, sems, held, weight_sems, base_held, chosen):
    chosen_read = pltpu.make_async_copy(target, chosen, sems.at[3])
    chosen_read.start()
    base_read = pltpu.make_async_copy(base, base_held, sems.at[2])
    base_read.start()
    start_weights(weight, held, weight_sems)
    read = pltpu.make_async_copy(slots_in, slots, sems.at[0])
    read.start()
    placed[...] = jnp.zeros(placed.shape, F32)
    mask = land[...].astype(F32)
    forcing = summed_rows(devices, capacity, arrived, chosen, 4, chosen_read)
    base_read.wait()
    after = []
    for i in range(4):
        after.append(base_held[i] + mask * (forcing_gain * forcing[i]))
        next_ref[i, 0] = after[i]
    put_split([after[0], after[2], after[3]], high_ref, low_ref)
    read.wait()

    def ready(c):
        rows = pl.ds(c * (held.shape[0] // CHUNKS), held.shape[0] // CHUNKS)
        pltpu.make_async_copy(weight.at[rows], held.at[rows], weight_sems.at[c]).wait()

    product_rows(slots, held, high_ref, low_ref, placed, 3, ready)
    write = pltpu.make_async_copy(placed, sent, sems.at[1])
    write.start()
    write.wait()


def surface_kernel(devices, capacity, arrived, target, out, chosen, sem):
    read = pltpu.make_async_copy(target, chosen, sem)
    read.start()
    for i, total in enumerate(summed_rows(devices, capacity, arrived, chosen, 3, read)):
        out[i] = total


def whole(x):
    return pl.BlockSpec(x.shape, lambda *_: (0,) * len(x.shape))


def level_zero(x):
    return pl.BlockSpec((x.shape[0], 1) + x.shape[2:], lambda *_: (0, 0, 0, 0))


ANY = pl.BlockSpec(memory_space=pl.ANY)


def in_hbm(x):
    return pltpu.with_memory_space_constraint(x, pltpu.HBM)


def body(
    atm_state, ocean_state, surface_state, atm_diffusion, land_sea, flux_dest, flux_row, flux_weight, surface_dest,
    surface_row, surface_weight,
):
    variables, levels, rows, cols = atm_state.shape
    devices = lax.axis_size("comp") * lax.axis_size("lon")
    capacity = max(2, 2 * rows // devices)
    width = devices * capacity
    halves = rows // LANES
    f32 = functools.partial(jax.ShapeDtypeStruct, dtype=F32)
    top = f32((variables, rows, cols))
    top_rows, top_cols = f32((variables, cols)), f32((variables * halves, cols))
    atm_top, *edges = pl.pallas_call(
        functools.partial(atm_edges_kernel, halves, variables),
        grid=(1,),
        in_specs=[ANY],
        out_specs=[whole(e) for e in (top, top_rows, top_rows, top_cols, top_cols)],
        out_shape=[top, top_rows, top_rows, top_cols, top_cols],
        scratch_shapes=[pltpu.SemaphoreType.DMA(())],
        compiler_params=params(),
        cost_estimate=cost(8),
        name="atm_edges",
    )(in_hbm(atm_state))
    sides = exchange(*edges)
    line = jax.ShapeDtypeStruct((1, rows), jnp.int32)
    own_lists = jax.ShapeDtypeStruct((4, rows), jnp.int32)
    held, flux_slots, surface_slots, lists = pl.pallas_call(
        functools.partial(prepare_kernel, capacity),
        grid=(1,),
        in_specs=[whole(line)] * 4 + [ANY, ANY],
        out_specs=[pl.BlockSpec(memory_space=pltpu.VMEM)] + [whole(x) for x in (line, line, own_lists)],
        out_shape=[pltpu.VMEM(flux_weight.shape, BF16), pltpu.HBM(line.shape, jnp.int32), pltpu.HBM(line.shape, jnp.int32), own_lists],
        scratch_shapes=[pltpu.SemaphoreType.DMA(())],
        compiler_params=params(),
        cost_estimate=cost(4),
        name="prepare",
    )(*(x.reshape(1, rows) for x in (flux_dest, flux_row, surface_dest, surface_row)), in_hbm(flux_weight), edges[0])

    def work(channels):
        return [
            pltpu.SMEM((1, rows), jnp.int32),
            pltpu.VMEM((rows * 4, cols), F32),
            pltpu.VMEM((rows * 4, cols), F32),
            pltpu.VMEM((width * channels, cols), F32),
            pltpu.SemaphoreType.DMA((4,)),
        ]

    atm_started, sent = pl.pallas_call(
        functools.partial(flux_kernel, halves),
        grid=(1,),
        in_specs=[ANY]
        + [whole(e) for e in (atm_top, atm_diffusion, surface_state, *sides)]
        + [pl.BlockSpec(memory_space=pltpu.VMEM)],
        out_specs=[level_zero(atm_state), ANY],
        scratch_shapes=work(4),
        out_shape=[f32(atm_state.shape), pltpu.HBM((width * 4, cols), F32)],
        compiler_params=params(),
        cost_estimate=cost(5),
        name="fluxes",
    )(in_hbm(flux_slots), atm_top, atm_diffusion, surface_state, *sides, pltpu.with_memory_space_constraint(held, pltpu.VMEM))
    arrived = lax.all_to_all(
        sent.reshape(devices, capacity * 4, cols), AXES, split_axis=0, concat_axis=0, tiled=True
    ).reshape(width * 4, cols)

    lists, _ = lax.optimization_barrier((lists, sent))
    gathered, early = all_lists(lists)
    land, _ = lax.optimization_barrier((land_sea, early))
    count = variables * (levels - 1) + variables * levels + 1
    padded = -(-count // 8) * 8
    rest_rows, rest_cols = f32((padded, cols)), f32((padded * halves, cols))
    rest = pl.pallas_call(
        functools.partial(rest_edges_kernel, halves, variables, levels),
        grid=(1,),
        in_specs=[whole(atm_state), whole(ocean_state), whole(land_sea)],
        out_specs=[whole(e) for e in (rest_rows, rest_rows, rest_cols, rest_cols)],
        out_shape=[rest_rows, rest_rows, rest_cols, rest_cols],
        compiler_params=params(),
        cost_estimate=cost(8),
        name="rest_edges",
    )(atm_state, ocean_state, land)
    rest = exchange(*rest)
    base = variables * (levels - 1)
    ocean_top = pl.pallas_call(
        functools.partial(ocean_top_kernel, halves, base, levels),
        grid=(1,),
        in_specs=[pl.BlockSpec((variables, min(2, levels), rows, cols), lambda i: (0, 0, 0, 0)), whole(land_sea)]
        + [whole(e) for e in rest],
        out_specs=whole(top),
        out_shape=pltpu.HBM(top.shape, F32),
        compiler_params=params(),
        cost_estimate=cost(4),
        name="ocean_top",
    )(ocean_state, land_sea, *rest)
    target = jax.ShapeDtypeStruct((rows, width), BF16)
    flux_target, surface_target = pl.pallas_call(
        functools.partial(arrivals_kernel, devices, capacity),
        grid=(1,),
        in_specs=[whole(gathered)],
        out_specs=[whole(target)] * 2,
        scratch_shapes=[pltpu.VMEM((gathered.shape[1], devices, rows), jnp.int32)],
        out_shape=[pltpu.HBM(target.shape, BF16)] * 2,
        compiler_params=params(),
        cost_estimate=cost(1),
        name="arrivals",
    )(gathered)

    ocean_started, back = pl.pallas_call(
        functools.partial(forced_kernel, devices, capacity),
        grid=(1,),
        in_specs=[ANY, whole(arrived), ANY, whole(land_sea), ANY, ANY],
        out_specs=[level_zero(ocean_state), ANY],
        scratch_shapes=work(3)
        + [
            pltpu.VMEM(surface_weight.shape, BF16),
            pltpu.SemaphoreType.DMA((CHUNKS,)),
            pltpu.VMEM(top.shape, F32),
            pltpu.VMEM(target.shape, BF16),
        ],
        out_shape=[f32(ocean_state.shape), pltpu.HBM((width * 3, cols), F32)],
        compiler_params=params(),
        cost_estimate=cost(5),
        name="forced",
    )(in_hbm(surface_slots), arrived, in_hbm(flux_target), land_sea, in_hbm(ocean_top), in_hbm(surface_weight))
    returned = lax.all_to_all(
        back.reshape(devices, capacity * 3, cols), AXES, split_axis=0, concat_axis=0, tiled=True
    ).reshape(width * 3, cols)

    turned = [pltpu.VMEM((cols, padded * halves), F32)] * 2
    one_level = pl.BlockSpec((variables, 1, rows, cols), lambda i: (0, i + 1, 0, 0))
    atm_next = pl.pallas_call(
        functools.partial(atm_rest_kernel, halves, levels - 1),
        grid=(levels - 1,),
        in_specs=[one_level, whole(atm_diffusion)] + [whole(e) for e in rest] + [ANY],
        out_specs=one_level,
        out_shape=f32(atm_state.shape),
        scratch_shapes=turned,
        input_output_aliases={6: 0},
        compiler_params=params(),
        cost_estimate=cost(5),
        name="atm_rest",
    )(atm_state, atm_diffusion, *rest, atm_started)
    ocean_next = pl.pallas_call(
        functools.partial(ocean_rest_kernel, halves, base, levels),
        grid=(variables,),
        in_specs=[pl.BlockSpec((1, levels, rows, cols), lambda i: (i, 0, 0, 0)), whole(land_sea)]
        + [whole(e) for e in rest]
        + [ANY],
        out_specs=ANY,
        out_shape=f32(ocean_state.shape),
        scratch_shapes=[
            pltpu.SemaphoreType.DMA(()),
            pltpu.VMEM((levels - 1, rows, cols), F32),
            pltpu.VMEM((rows, cols), F32),
        ]
        + turned,
        input_output_aliases={6: 0},
        compiler_params=params(),
        cost_estimate=cost(6),
        name="ocean_rest",
    )(ocean_state, land_sea, *rest, ocean_started)
    surface_next = pl.pallas_call(
        functools.partial(surface_kernel, devices, capacity),
        grid=(1,),
        in_specs=[whole(returned), ANY],
        out_specs=whole(surface_state),
        out_shape=f32(surface_state.shape),
        scratch_shapes=[pltpu.VMEM(target.shape, BF16), pltpu.SemaphoreType.DMA(())],
        compiler_params=params(),
        cost_estimate=cost(1),
        name="surface",
    )(returned, in_hbm(surface_target))
    return (atm_next, ocean_next, surface_next)


def solution(mesh):
    in_specs = (
        P(None, None, "comp", "lon"),
        P(None, None, "comp", "lon"),
        P(None, "comp", "lon"),
        P("comp", "lon"),
        P("comp", "lon"),
        P(("comp", "lon"), None),
        P(("comp", "lon")),
        P(("comp", "lon"), None, None),
        P(("comp", "lon"), None),
        P(("comp", "lon")),
        P(("comp", "lon"), None, None),
    )
    out_specs = (P(None, None, "comp", "lon"), P(None, None, "comp", "lon"), P(None, "comp", "lon"))
    return jax.shard_map(body, mesh=mesh, in_specs=in_specs, out_specs=out_specs, check_vma=False)
```

```python
import functools

import jax
import jax.numpy as jnp
from jax import lax
from jax.experimental import pallas as pl
from jax.experimental.pallas import tpu as pltpu
from jax.sharding import PartitionSpec as P

time_step = 0.1
ocean_diffusion = 0.2
vertical_mixing = 0.2
drag_coef = 0.4
heat_coef = 0.5
moisture_coef = 0.3
rain_coef = 0.2
forcing_gain = 0.5

AXES = ("comp", "lon")
LANES = 128
CHUNKS = 8
LOOPS = 4
PARTS = 4
F32 = jnp.float32
BF16 = jnp.bfloat16
VMEM_LIMIT = 24 << 20


def cost(microseconds):
    return pl.CostEstimate(flops=int(microseconds * 1e9), bytes_accessed=1 << 20, transcendentals=0)


def params(**kw):
    return pltpu.CompilerParams(vmem_limit_bytes=VMEM_LIMIT, **kw)


def shift(x, axis, up):
    devices = lax.axis_size(axis)
    pairs = [(i, (i + 1) % devices) for i in range(devices)]
    if not up:
        pairs = [(j, i) for i, j in pairs]
    return lax.ppermute(x, axis, pairs)


def exchange(first_rows, last_rows, first_cols, last_cols):
    north = shift(first_rows, "comp", False)
    south = shift(last_rows, "comp", True)
    east = shift(first_cols, "lon", False)
    west = shift(last_cols, "lon", True)
    return north, south, east, west


def inside():
    at = lax.axis_index("comp")
    return at < lax.axis_size("comp") - 1, at > 0


def cleared(north, south):
    has_north, has_south = inside()
    return jnp.where(has_north, north[...], 0.0), jnp.where(has_south, south[...], 0.0)


def put_edges(field, at, halves, refs):
    first_rows, last_rows, first_cols, last_cols = refs
    rows = field.shape[0]
    first_rows[at : at + 1, :] = field[0:1, :]
    last_rows[at : at + 1, :] = field[rows - 1 : rows, :]
    for h in range(halves):
        turned = jnp.transpose(field[h * LANES : (h + 1) * LANES, :])
        row = at * halves + h
        first_cols[row : row + 1, :] = turned[0:1, :]
        last_cols[row : row + 1, :] = turned[LANES - 1 : LANES, :]


def neighbours(x, north, south, east, west):
    rows, cols = x.shape
    row = lax.broadcasted_iota(jnp.int32, x.shape, 0)
    col = lax.broadcasted_iota(jnp.int32, x.shape, 1)
    n = jnp.where(row == rows - 1, north, pltpu.roll(x, rows - 1, 0))
    s = jnp.where(row == 0, south, pltpu.roll(x, 1, 0))
    e = jnp.where(col == cols - 1, east, pltpu.roll(x, cols - 1, 1))
    w = jnp.where(col == 0, west, pltpu.roll(x, 1, 1))
    return n, s, e, w


def column(turned, at, halves):
    parts = [turned[:, at * halves + h : at * halves + h + 1] for h in range(halves)]
    return jnp.concatenate(parts, axis=0)


def atm_edges_kernel(halves, count, atm, flux_dest, flux_row, surface_dest, surface_row, held, first_rows, last_rows, first_cols, last_cols, lists, lines, sems):
    copies = [pltpu.make_async_copy(atm.at[at, 0], held.at[at], sems.at[at]) for at in range(count)]
    for copy in copies:
        copy.start()
    reads = []
    for i, ref in enumerate((flux_dest, flux_row, surface_dest, surface_row)):
        reads.append(pltpu.make_async_copy(ref, lines.at[i], sems.at[count + i]))
        reads[i].start()
    for at in range(count):
        copies[at].wait()
        put_edges(held[at], at, halves, (first_rows, last_rows, first_cols, last_cols))
    for i, read in enumerate(reads):
        read.wait()
        lists[0, i : i + 1, :] = lines[i]


def rest_edges_kernel(halves, variables, levels, atm, ocean, land, *outs):
    at = 0
    for v in range(variables):
        for level in range(1, levels):
            put_edges(atm[v, level], at, halves, outs)
            at += 1
    mask = land[...].astype(F32)
    for v in range(variables):
        for level in range(levels):
            put_edges(ocean[v, level] * mask, at, halves, outs)
            at += 1
    put_edges(mask, at, halves, outs)
    for ref in outs:
        used = (at + 1) * (ref.shape[0] // outs[0].shape[0])
        if used < ref.shape[0]:
            ref[used:, :] = jnp.zeros((ref.shape[0] - used, LANES), F32)


def atm_step(a, u, v, diffusion, sides):
    n, s, e, w = sides
    laplace = n + s + e + w - 4.0 * a
    advection = u * (e - w) + v * (n - s)
    return a + diffusion * laplace - 0.5 * time_step * advection


def put_split(fields, high_ref, low_ref):
    rows = fields[0].shape[0]
    for i in range(4):
        if i < len(fields):
            high = fields[i].astype(BF16).astype(F32)
            low = fields[i] - high
        else:
            high = low = jnp.zeros((rows, LANES), F32)
        high_ref[pl.ds(i, rows, stride=4), :] = high
        low_ref[pl.ds(i, rows, stride=4), :] = low


def weight_copies(weight, held, sems):
    part = held.shape[0] // CHUNKS
    for c in range(CHUNKS):
        rows = pl.ds(c * part, part)
        yield pltpu.make_async_copy(weight.at[rows], held.at[rows], sems.at[c])


def start_weights(weight, held, sems):
    for copy in weight_copies(weight, held, sems):
        copy.start()


def wait_weights(weight, held, sems):
    for copy in weight_copies(weight, held, sems):
        copy.wait()


def product_rows(slots, weight, high_ref, low_ref, placed, channels, ready=None):
    part = weight.shape[0] // LOOPS

    def some(c, carry):
        if ready is not None:
            ready(c)
        for i in range(0, part, 2):
            r = c * part + i
            at = pl.ds(pl.multiple_of(r * 4, 8), 8)
            left = jnp.concatenate([high_ref[at, :].astype(BF16), low_ref[at, :].astype(BF16)], axis=0)
            right = jnp.concatenate([weight[r], weight[r + 1]], axis=1)
            both = jnp.dot(left, right, preferred_element_type=F32)
            both = both[:8] + both[8:]
            placed[pl.ds(slots[0, r] * channels, channels), :] = both[:channels, :LANES]
            placed[pl.ds(slots[0, r + 1] * channels, channels), :] = both[4 : 4 + channels, LANES:]
        return carry

    lax.fori_loop(0, LOOPS, some, 0)


def slot_row(destination, capacity):
    rows = destination.shape[1]
    wide = jnp.broadcast_to(destination.astype(F32), (8, rows))
    column_of = jnp.concatenate([jnp.transpose(wide[:, i : i + LANES]) for i in range(0, rows, LANES)], axis=0)[:, 0:1]
    j = lax.broadcasted_iota(jnp.int32, (rows, rows), 0)
    i = lax.broadcasted_iota(jnp.int32, (rows, rows), 1)
    earlier = (column_of == wide[0:1, :]) & (j < i)
    rank = jnp.sum(jnp.where(earlier, 1.0, 0.0), axis=0, keepdims=True)
    return destination * capacity + rank.astype(jnp.int32)


def prepare_kernel(capacity, lists, weight, held, flux_slots, surface_slots, sems):
    start_weights(weight, held, sems)
    flux_slots[...] = slot_row(lists[0, 0:1, :], capacity)
    surface_slots[...] = slot_row(lists[0, 2:3, :], capacity)
    wait_weights(weight, held, sems)


def copies_of(source, target, sems, first):
    part = source.shape[0] // PARTS
    copies = []
    for c in range(PARTS):
        rows = pl.ds(c * part, part)
        copies.append(pltpu.make_async_copy(source.at[rows], target.at[rows], sems.at[first + c]))
        copies[-1].start()
    return copies


def wait_all(copies):
    for copy in copies:
        copy.wait()


def flux_kernel(halves, slots_in, atm, diffusion, surface, north, south, east, west, weight, ahead, next_ref, sent, slots, high_ref, low_ref, placed, made, sems):
    read = pltpu.make_async_copy(slots_in, slots, sems.at[0])
    read.start()
    placed[...] = jnp.zeros(placed.shape, F32)
    east_turned, west_turned = jnp.transpose(east[...]), jnp.transpose(west[...])
    u, v, coef = atm[0], atm[1], diffusion[...]
    norths, souths = cleared(north, south)
    after = []
    for i in range(4):
        sides = neighbours(
            atm[i], norths[i : i + 1, :], souths[i : i + 1, :], column(east_turned, i, halves), column(west_turned, i, halves)
        )
        after.append(atm_step(atm[i], u, v, coef, sides))
        made[i] = after[i]
    writes = copies_of(made, next_ref.at[:, 0], sems, 1)
    du, dv = after[0] - surface[1], after[1] - surface[2]
    speed = jnp.sqrt(1.0 + du * du + dv * dv)
    sst, humidity = surface[0], after[3]
    moisture = moisture_coef * speed * (sst - humidity) - rain_coef * humidity * humidity
    put_split(
        [heat_coef * speed * (after[2] - sst), moisture, drag_coef * speed * du, drag_coef * speed * dv],
        high_ref,
        low_ref,
    )
    read.wait()
    product_rows(slots, weight, high_ref, low_ref, placed, 4)
    wait_all(writes + copies_of(placed, sent, sems, 1 + PARTS))


def atm_rest_kernel(halves, per_variable, atm, diffusion, north, south, east, west, started, out, turned_e, turned_w):
    level = pl.program_id(0)

    @pl.when(level == 0)
    def _():
        turn_columns(east, west, turned_e, turned_w)

    u, v, coef = atm[0, 0], atm[1, 0], diffusion[...]
    te, tw = turned_e[...], turned_w[...]
    has_north, has_south = inside()
    for i in range(4):
        at = i * per_variable + level
        a = atm[i, 0]
        n = jnp.where(has_north, north[pl.ds(at, 1), :], 0.0)
        s = jnp.where(has_south, south[pl.ds(at, 1), :], 0.0)
        sides = neighbours(a, n, s, picked(te, at, halves), picked(tw, at, halves))
        out[i, 0] = atm_step(a, u, v, coef, sides)


def turn_columns(east, west, turned_e, turned_w):
    turned_e[...] = jnp.transpose(east[...])
    turned_w[...] = jnp.transpose(west[...])


def picked(turned, at, halves):
    lane = lax.broadcasted_iota(jnp.int32, turned.shape, 1)
    parts = [jnp.sum(jnp.where(lane == at * halves + h, turned, 0.0), axis=1, keepdims=True) for h in range(halves)]
    return jnp.concatenate(parts, axis=0)


def sea_count(at, halves, mask, north, south, te, tw):
    norths, souths = cleared(north, south)
    row = slice(at, at + 1)
    n, s, e, w = neighbours(mask, norths[row, :], souths[row, :], column(te, at, halves), column(tw, at, halves))
    return n + s + e + w


def ocean_step(o, above, below, mask, count, sides):
    n, s, e, w = sides
    lateral = n + s + e + w - count * o
    vertical = above + below - 2.0 * o
    return mask * (o + ocean_diffusion * lateral + vertical_mixing * vertical)


def ocean_top_kernel(halves, base, levels, ocean, land, north, south, east, west, out):
    mask = land[...].astype(F32)
    te, tw = jnp.transpose(east[...]), jnp.transpose(west[...])
    count = sea_count(base + 4 * levels, halves, mask, north, south, te, tw)
    norths, souths = cleared(north, south)
    for var in range(4):
        at = base + var * levels
        o = ocean[var, 0]
        sides = neighbours(
            o * mask, norths[at : at + 1, :], souths[at : at + 1, :], column(te, at, halves), column(tw, at, halves)
        )
        out[var] = ocean_step(o, o, ocean[var, min(1, levels - 1)], mask, count, sides)


def ocean_rest_kernel(halves, base, levels, ocean, land, north, south, east, west, started, out, sem, made, count, turned_e, turned_w):
    var = pl.program_id(0)
    mask = land[...].astype(F32)

    @pl.when(var == 0)
    def _():
        turn_columns(east, west, turned_e, turned_w)
        count[...] = sea_count(base + 4 * levels, halves, mask, north, south, turned_e[...], turned_w[...])

    te, tw = turned_e[...], turned_w[...]
    has_north, has_south = inside()
    for level in range(1, levels):
        at = base + var * levels + level
        o = ocean[0, level]
        n = jnp.where(has_north, north[pl.ds(at, 1), :], 0.0)
        s = jnp.where(has_south, south[pl.ds(at, 1), :], 0.0)
        sides = neighbours(o * mask, n, s, picked(te, at, halves), picked(tw, at, halves))
        made[level - 1] = ocean_step(
            o, ocean[0, level - 1], ocean[0, min(level + 1, levels - 1)], mask, count[...], sides
        )
    write = pltpu.make_async_copy(made, out.at[var, pl.ds(1, levels - 1)], sem)
    write.start()
    write.wait()


def list_steps(lists):
    comp, lon = lax.axis_size("comp"), lax.axis_size("lon")
    bits = [lon << k for k in range(comp.bit_length() - 1)] + [1 << k for k in range(lon.bit_length() - 1)]
    pieces = [lists]
    held = lists
    for bit in bits:
        held = yield held
        pieces.append(lax.ppermute(held, AXES, [(i, i ^ bit) for i in range(comp * lon)]))
        held = jnp.concatenate([held, pieces[-1]], axis=0)
    return pieces


def arrivals_kernel(devices, capacity, *refs):
    *pieces, first, second, all_ref, sorted_ref = refs
    kinds, rows = pieces[0].shape[1:]
    comp, lon = lax.axis_size("comp"), lax.axis_size("lon")
    my_comp, my_lon = lax.axis_index("comp"), lax.axis_index("lon")
    me = my_comp * lon + my_lon
    place = 0
    for piece in pieces:
        all_ref[place : place + piece.shape[0]] = piece[...]
        place += piece.shape[0]
    for s in range(devices):
        block = all_ref[(my_comp ^ (s // lon)) + (my_lon ^ (s % lon)) * comp]
        for kind in range(kinds):
            sorted_ref[kind, s : s + 1, :] = block[kind : kind + 1]
    j = lax.broadcasted_iota(jnp.int32, (rows, rows), 0)
    i = lax.broadcasted_iota(jnp.int32, (rows, rows), 1)
    before = jnp.where(j < i, 1.0, 0.0).astype(BF16)
    for which, out in enumerate((first, second)):
        named = sorted_ref[2 * which] == me
        target = sorted_ref[2 * which + 1]
        rank = jnp.dot(jnp.where(named, 1.0, 0.0).astype(BF16), before, preferred_element_type=F32)
        row = jnp.where(named, (target + 1).astype(F32), 0.0)
        parts = [jnp.where(rank == float(k), row, 0.0) for k in range(capacity)]
        table = jnp.concatenate(parts, axis=0).astype(BF16)
        total = lax.dot_general(
            jnp.ones((8, rows), BF16), table, (((1,), (1,)), ((), ())), preferred_element_type=F32
        )
        wanted = lax.broadcasted_iota(jnp.int32, out.shape, 0).astype(F32) + 1.0
        out[...] = jnp.where(wanted == total[0:1, :], 1.0, 0.0).astype(BF16)


def summed_rows(devices, capacity, arrived, chosen, channels, read=None):
    columns = []
    for i in range(channels):
        parts = [
            arrived[pl.ds(k * channels + i, devices, stride=capacity * channels), :] for k in range(capacity)
        ]
        x = jnp.concatenate(parts, axis=0)
        high = x.astype(BF16)
        columns += [high, (x - high.astype(F32)).astype(BF16)]
    if read is not None:
        read.wait()
    total = jnp.dot(chosen[...], jnp.concatenate(columns, axis=1), preferred_element_type=F32)
    return [
        total[:, 2 * i * LANES : (2 * i + 1) * LANES] + total[:, (2 * i + 1) * LANES : (2 * i + 2) * LANES]
        for i in range(channels)
    ]


def forced_kernel(devices, capacity, slots_in, arrived, target, land, base, weight, next_ref, sent, slots, high_ref, low_ref, placed, made, sems, chosen, held, weight_sems):
    chosen_read = pltpu.make_async_copy(target, chosen, sems.at[1 + 2 * PARTS])
    chosen_read.start()
    reads = copies_of(base, made, sems, 1)
    slots_read = pltpu.make_async_copy(slots_in, slots, sems.at[0])
    slots_read.start()
    start_weights(weight, held, weight_sems)
    placed[...] = jnp.zeros(placed.shape, F32)
    mask = land[...].astype(F32)
    forcing = summed_rows(devices, capacity, arrived, chosen, 4, chosen_read)
    wait_all(reads)
    after = []
    for i in range(4):
        after.append(made[i] + mask * (forcing_gain * forcing[i]))
        made[i] = after[i]
    writes = copies_of(made, next_ref.at[:, 0], sems, 1)
    put_split([after[0], after[2], after[3]], high_ref, low_ref)
    slots_read.wait()
    per_loop, part = CHUNKS // LOOPS, held.shape[0] // CHUNKS

    def ready(c):
        for i in range(per_loop):
            rows = pl.ds((c * per_loop + i) * part, part)
            pltpu.make_async_copy(weight.at[rows], held.at[rows], weight_sems.at[c * per_loop + i]).wait()

    product_rows(slots, held, high_ref, low_ref, placed, 3, ready)
    wait_all(writes + copies_of(placed, sent, sems, 1 + PARTS))


def surface_kernel(devices, capacity, arrived, chosen, out):
    for i, total in enumerate(summed_rows(devices, capacity, arrived, chosen, 3)):
        out[i] = total


def whole(x):
    return pl.BlockSpec(x.shape, lambda *_: (0,) * len(x.shape))


def level_zero(x):
    return pl.BlockSpec((x.shape[0], 1) + x.shape[2:], lambda *_: (0, 0, 0, 0))


ANY = pl.BlockSpec(memory_space=pl.ANY)


def in_hbm(x):
    return pltpu.with_memory_space_constraint(x, pltpu.HBM)


def in_vmem(x):
    return pltpu.with_memory_space_constraint(x, pltpu.VMEM)


def body(
    atm_state, ocean_state, surface_state, atm_diffusion, land_sea, flux_dest, flux_row, flux_weight, surface_dest,
    surface_row, surface_weight,
):
    variables, levels, rows, cols = atm_state.shape
    devices = lax.axis_size("comp") * lax.axis_size("lon")
    capacity = max(2, 2 * rows // devices)
    width = devices * capacity
    halves = rows // LANES
    f32 = functools.partial(jax.ShapeDtypeStruct, dtype=F32)
    top = f32((variables, rows, cols))
    top_rows, top_cols = f32((variables, cols)), f32((variables * halves, cols))
    line = jax.ShapeDtypeStruct((1, rows), jnp.int32)
    made = [top, top_rows, top_rows, top_cols, top_cols, jax.ShapeDtypeStruct((1, 4, rows), jnp.int32)]
    atm_top, *edges, lists = pl.pallas_call(
        functools.partial(atm_edges_kernel, halves, variables),
        grid=(1,),
        in_specs=[ANY] * 5,
        out_specs=[whole(e) for e in made],
        out_shape=made,
        scratch_shapes=[pltpu.VMEM((4, 1, rows), jnp.int32), pltpu.SemaphoreType.DMA((variables + 4,))],
        compiler_params=params(),
        cost_estimate=cost(8),
        name="atm_edges",
    )(in_hbm(atm_state), *(in_hbm(x.reshape(1, rows)) for x in (flux_dest, flux_row, surface_dest, surface_row)))
    sides = exchange(*edges)
    steps = list_steps(lists)
    step = steps.send(None)
    step = steps.send(step)
    in_memory = pl.BlockSpec(memory_space=pltpu.VMEM)
    held, flux_slots, surface_slots = pl.pallas_call(
        functools.partial(prepare_kernel, capacity),
        grid=(1,),
        in_specs=[whole(lists), ANY],
        out_specs=[in_memory, whole(line), whole(line)],
        out_shape=[pltpu.VMEM(flux_weight.shape, BF16)] + [pltpu.HBM(line.shape, jnp.int32)] * 2,
        scratch_shapes=[pltpu.SemaphoreType.DMA((CHUNKS,))],
        compiler_params=params(),
        cost_estimate=cost(4),
        name="prepare",
    )(lists, in_hbm(flux_weight))
    step, flux_slots = lax.optimization_barrier((step, flux_slots))
    step = steps.send(step)

    def work(channels):
        return [
            pltpu.SMEM((1, rows), jnp.int32),
            pltpu.VMEM((rows * 4, cols), F32),
            pltpu.VMEM((rows * 4, cols), F32),
            pltpu.VMEM((width * channels, cols), F32),
            pltpu.VMEM(top.shape, F32),
            pltpu.SemaphoreType.DMA((2 + 2 * PARTS,)),
        ]

    atm_started, sent = pl.pallas_call(
        functools.partial(flux_kernel, halves),
        grid=(1,),
        in_specs=[ANY]
        + [whole(e) for e in (atm_top, atm_diffusion, surface_state, *sides)]
        + [in_memory, ANY],
        out_specs=[ANY, ANY],
        scratch_shapes=work(4),
        out_shape=[f32(atm_state.shape), pltpu.HBM((width * 4, cols), F32)],
        compiler_params=params(),
        cost_estimate=cost(5),
        name="fluxes",
    )(in_hbm(flux_slots), atm_top, atm_diffusion, surface_state, *sides, in_vmem(held), in_hbm(flux_slots))
    arrived = lax.all_to_all(
        sent.reshape(devices, capacity * 4, cols), AXES, split_axis=0, concat_axis=0, tiled=True
    ).reshape(width * 4, cols)

    step, land, _ = lax.optimization_barrier((step, land_sea, sent))
    while True:
        try:
            step = steps.send(step)
        except StopIteration as stop:
            pieces = stop.value
            break
    count = variables * (levels - 1) + variables * levels + 1
    padded = -(-count // 8) * 8
    rest_rows, rest_cols = f32((padded, cols)), f32((padded * halves, cols))
    rest = pl.pallas_call(
        functools.partial(rest_edges_kernel, halves, variables, levels),
        grid=(1,),
        in_specs=[whole(atm_state), whole(ocean_state), whole(land_sea)],
        out_specs=[whole(e) for e in (rest_rows, rest_rows, rest_cols, rest_cols)],
        out_shape=[rest_rows, rest_rows, rest_cols, rest_cols],
        compiler_params=params(),
        cost_estimate=cost(8),
        name="rest_edges",
    )(atm_state, ocean_state, land)
    rest = exchange(*rest)
    base = variables * (levels - 1)
    ocean_top = pl.pallas_call(
        functools.partial(ocean_top_kernel, halves, base, levels),
        grid=(1,),
        in_specs=[pl.BlockSpec((variables, min(2, levels), rows, cols), lambda i: (0, 0, 0, 0)), whole(land_sea)]
        + [whole(e) for e in rest],
        out_specs=whole(top),
        out_shape=pltpu.HBM(top.shape, F32),
        compiler_params=params(),
        cost_estimate=cost(4),
        name="ocean_top",
    )(ocean_state, land_sea, *rest)
    target = jax.ShapeDtypeStruct((rows, width), BF16)
    flux_target, surface_target = pl.pallas_call(
        functools.partial(arrivals_kernel, devices, capacity),
        grid=(1,),
        in_specs=[whole(piece) for piece in pieces],
        out_specs=[whole(target)] * 2,
        scratch_shapes=[pltpu.VMEM((devices, 4, rows), jnp.int32), pltpu.VMEM((4, devices, rows), jnp.int32)],
        out_shape=[pltpu.HBM(target.shape, BF16), target],
        compiler_params=params(),
        cost_estimate=cost(1),
        name="arrivals",
    )(*pieces)

    ocean_started, back = pl.pallas_call(
        functools.partial(forced_kernel, devices, capacity),
        grid=(1,),
        in_specs=[ANY, whole(arrived), ANY, whole(land_sea), ANY, ANY],
        out_specs=[ANY, ANY],
        scratch_shapes=work(3)
        + [
            pltpu.VMEM(target.shape, BF16),
            pltpu.VMEM(surface_weight.shape, BF16),
            pltpu.SemaphoreType.DMA((CHUNKS,)),
        ],
        out_shape=[f32(ocean_state.shape), pltpu.HBM((width * 3, cols), F32)],
        compiler_params=params(),
        cost_estimate=cost(5),
        name="forced",
    )(in_hbm(surface_slots), arrived, in_hbm(flux_target), land_sea, in_hbm(ocean_top), in_hbm(surface_weight))
    returned = lax.all_to_all(
        back.reshape(devices, capacity * 3, cols), AXES, split_axis=0, concat_axis=0, tiled=True
    ).reshape(width * 3, cols)

    turned = [pltpu.VMEM((cols, padded * halves), F32)] * 2
    one_level = pl.BlockSpec((variables, 1, rows, cols), lambda i: (0, i + 1, 0, 0))
    atm_next = pl.pallas_call(
        functools.partial(atm_rest_kernel, halves, levels - 1),
        grid=(levels - 1,),
        in_specs=[one_level, whole(atm_diffusion)] + [whole(e) for e in rest] + [ANY],
        out_specs=one_level,
        out_shape=f32(atm_state.shape),
        scratch_shapes=turned,
        input_output_aliases={6: 0},
        compiler_params=params(),
        cost_estimate=cost(5),
        name="atm_rest",
    )(atm_state, atm_diffusion, *rest, atm_started)
    ocean_next = pl.pallas_call(
        functools.partial(ocean_rest_kernel, halves, base, levels),
        grid=(variables,),
        in_specs=[pl.BlockSpec((1, levels, rows, cols), lambda i: (i, 0, 0, 0)), whole(land_sea)]
        + [whole(e) for e in rest]
        + [ANY],
        out_specs=ANY,
        out_shape=f32(ocean_state.shape),
        scratch_shapes=[
            pltpu.SemaphoreType.DMA(()),
            pltpu.VMEM((levels - 1, rows, cols), F32),
            pltpu.VMEM((rows, cols), F32),
        ]
        + turned,
        input_output_aliases={6: 0},
        compiler_params=params(),
        cost_estimate=cost(6),
        name="ocean_rest",
    )(ocean_state, land_sea, *rest, ocean_started)
    surface_next = pl.pallas_call(
        functools.partial(surface_kernel, devices, capacity),
        grid=(1,),
        in_specs=[whole(returned), whole(surface_target)],
        out_specs=whole(surface_state),
        out_shape=f32(surface_state.shape),
        compiler_params=params(),
        cost_estimate=cost(1),
        name="surface",
    )(returned, surface_target)
    return (atm_next, ocean_next, surface_next)


def solution(mesh):
    in_specs = (
        P(None, None, "comp", "lon"),
        P(None, None, "comp", "lon"),
        P(None, "comp", "lon"),
        P("comp", "lon"),
        P("comp", "lon"),
        P(("comp", "lon"), None),
        P(("comp", "lon")),
        P(("comp", "lon"), None, None),
        P(("comp", "lon"), None),
        P(("comp", "lon")),
        P(("comp", "lon"), None, None),
    )
    out_specs = (P(None, None, "comp", "lon"), P(None, None, "comp", "lon"), P(None, "comp", "lon"))
    return jax.shard_map(body, mesh=mesh, in_specs=in_specs, out_specs=out_specs, check_vma=False)
```

```python
import functools

import jax
import jax.numpy as jnp
from jax import lax
from jax.experimental import pallas as pl
from jax.experimental.pallas import tpu as pltpu
from jax.sharding import PartitionSpec as P

time_step = 0.1
ocean_diffusion = 0.2
vertical_mixing = 0.2
drag_coef = 0.4
heat_coef = 0.5
moisture_coef = 0.3
rain_coef = 0.2
forcing_gain = 0.5

AXES = ("comp", "lon")
LANES = 128
CHUNKS = 8
LOOPS = 4
PARTS = 4
F32 = jnp.float32
BF16 = jnp.bfloat16
VMEM_LIMIT = 24 << 20


def cost(microseconds):
    return pl.CostEstimate(flops=int(microseconds * 1e9), bytes_accessed=1 << 20, transcendentals=0)


def params(**kw):
    return pltpu.CompilerParams(vmem_limit_bytes=VMEM_LIMIT, **kw)


def shift(x, axis, up):
    devices = lax.axis_size(axis)
    pairs = [(i, (i + 1) % devices) for i in range(devices)]
    if not up:
        pairs = [(j, i) for i, j in pairs]
    return lax.ppermute(x, axis, pairs)


def exchange_rows(first_rows, last_rows):
    return shift(first_rows, "comp", False), shift(last_rows, "comp", True)


def exchange_columns(first_cols, last_cols):
    return shift(first_cols, "lon", False), shift(last_cols, "lon", True)


def inside():
    at = lax.axis_index("comp")
    return at < lax.axis_size("comp") - 1, at > 0


def cleared(north, south):
    has_north, has_south = inside()
    return jnp.where(has_north, north[...], 0.0), jnp.where(has_south, south[...], 0.0)


def put_columns(field, at, halves, first_cols, last_cols):
    for h in range(halves):
        turned = jnp.transpose(field[h * LANES : (h + 1) * LANES, :])
        row = at * halves + h
        first_cols[row : row + 1, :] = turned[0:1, :]
        last_cols[row : row + 1, :] = turned[LANES - 1 : LANES, :]


def neighbours(x, north, south, east, west):
    rows, cols = x.shape
    row = lax.broadcasted_iota(jnp.int32, x.shape, 0)
    col = lax.broadcasted_iota(jnp.int32, x.shape, 1)
    n = jnp.where(row == rows - 1, north, pltpu.roll(x, rows - 1, 0))
    s = jnp.where(row == 0, south, pltpu.roll(x, 1, 0))
    e = jnp.where(col == cols - 1, east, pltpu.roll(x, cols - 1, 1))
    w = jnp.where(col == 0, west, pltpu.roll(x, 1, 1))
    return n, s, e, w


def column(turned, at, halves):
    parts = [turned[:, at * halves + h : at * halves + h + 1] for h in range(halves)]
    return jnp.concatenate(parts, axis=0)


def edges_kernel(halves, variables, levels, rows, atm, ocean, land, *refs):
    list_refs = refs[:4]
    held, first_rows, last_rows, first_cols, last_cols, lists, atm_ends, ocean_ends, land_ends, lines, sems = refs[4:]
    copies = [pltpu.make_async_copy(atm.at[v, 0], held.at[v], sems.at[v]) for v in range(variables)]
    ends = (pl.ds(0, 8), pl.ds(rows - 8, 8))
    for side in range(2):
        copies.append(pltpu.make_async_copy(atm.at[:, :, ends[side]], atm_ends.at[side], sems.at[variables + side]))
        copies.append(pltpu.make_async_copy(ocean.at[:, :, ends[side]], ocean_ends.at[side], sems.at[variables + 2 + side]))
        copies.append(pltpu.make_async_copy(land.at[ends[side]], land_ends.at[side], sems.at[variables + 4 + side]))
    for i, ref in enumerate(list_refs):
        copies.append(pltpu.make_async_copy(ref, lines.at[i], sems.at[variables + 6 + i]))
    for copy in copies:
        copy.start()
    for v in range(variables):
        copies[v].wait()
        put_columns(held[v], v, halves, first_cols, last_cols)
    wait_all(copies[variables:])
    for side, out in enumerate((first_rows, last_rows)):
        row = slice(0, 1) if side == 0 else slice(7, 8)
        mask = land_ends[side, row, :].astype(F32)
        at = 0
        for v in range(variables):
            for level in range(levels):
                out[at : at + 1, :] = atm_ends[side, v, level, row, :]
                at += 1
        for v in range(variables):
            for level in range(levels):
                out[at : at + 1, :] = ocean_ends[side, v, level, row, :] * mask
                at += 1
        out[at : at + 1, :] = mask
        out[at + 1 :, :] = jnp.zeros((out.shape[0] - at - 1, LANES), F32)
    for i in range(4):
        for h in range(halves):
            line = lines[i, :, h * LANES : (h + 1) * LANES].astype(F32)
            for out, at in ((first_rows, first_rows.shape[0] - 4 * halves), (last_rows, first_rows.shape[0] - 4 * halves), (lists, 0)):
                out[at + i * halves + h : at + i * halves + h + 1, :] = line


def rest_edges_kernel(halves, variables, levels, atm, ocean, land, first_cols, last_cols):
    at = 0
    for v in range(variables):
        for level in range(1, levels):
            put_columns(atm[v, level], at, halves, first_cols, last_cols)
            at += 1
    mask = land[...].astype(F32)
    for v in range(variables):
        for level in range(levels):
            put_columns(ocean[v, level] * mask, at, halves, first_cols, last_cols)
            at += 1
    put_columns(mask, at, halves, first_cols, last_cols)
    used = (at + 1) * halves
    for ref in (first_cols, last_cols):
        if used < ref.shape[0]:
            ref[used:, :] = jnp.zeros((ref.shape[0] - used, LANES), F32)


def atm_step(a, u, v, diffusion, sides):
    n, s, e, w = sides
    laplace = n + s + e + w - 4.0 * a
    advection = u * (e - w) + v * (n - s)
    return a + diffusion * laplace - 0.5 * time_step * advection


def put_split(fields, high_ref, low_ref):
    rows = fields[0].shape[0]
    for i in range(4):
        if i < len(fields):
            high = fields[i].astype(BF16).astype(F32)
            low = fields[i] - high
        else:
            high = low = jnp.zeros((rows, LANES), F32)
        high_ref[pl.ds(i, rows, stride=4), :] = high
        low_ref[pl.ds(i, rows, stride=4), :] = low


def weight_copies(weight, held, sems):
    part = held.shape[0] // CHUNKS
    for c in range(CHUNKS):
        rows = pl.ds(c * part, part)
        yield pltpu.make_async_copy(weight.at[rows], held.at[rows], sems.at[c])


def start_weights(weight, held, sems):
    for copy in weight_copies(weight, held, sems):
        copy.start()


def wait_weights(weight, held, sems):
    for copy in weight_copies(weight, held, sems):
        copy.wait()


def product_rows(slots, weight, high_ref, low_ref, placed, channels, ready=None):
    part = weight.shape[0] // LOOPS

    def some(c, carry):
        if ready is not None:
            ready(c)
        for i in range(0, part, 2):
            r = c * part + i
            at = pl.ds(pl.multiple_of(r * 4, 8), 8)
            left = jnp.concatenate([high_ref[at, :].astype(BF16), low_ref[at, :].astype(BF16)], axis=0)
            right = jnp.concatenate([weight[r], weight[r + 1]], axis=1)
            both = jnp.dot(left, right, preferred_element_type=F32)
            both = both[:8] + both[8:]
            placed[pl.ds(slots[0, r] * channels, channels), :] = both[:channels, :LANES]
            placed[pl.ds(slots[0, r + 1] * channels, channels), :] = both[4 : 4 + channels, LANES:]
        return carry

    lax.fori_loop(0, LOOPS, some, 0)


def joined(rows, i, halves):
    return jnp.concatenate([rows[i * halves + h : i * halves + h + 1, :] for h in range(halves)], axis=1)


def slot_row(destination, capacity):
    rows = destination.shape[1]
    wide = jnp.broadcast_to(destination, (8, rows))
    column_of = jnp.concatenate([jnp.transpose(wide[:, i : i + LANES]) for i in range(0, rows, LANES)], axis=0)[:, 0:1]
    j = lax.broadcasted_iota(jnp.int32, (rows, rows), 0)
    i = lax.broadcasted_iota(jnp.int32, (rows, rows), 1)
    earlier = (column_of == wide[0:1, :]) & (j < i)
    rank = jnp.sum(jnp.where(earlier, 1.0, 0.0), axis=0, keepdims=True)
    return (destination * float(capacity) + rank).astype(jnp.int32)


def prepare_kernel(capacity, lists, weight, held, flux_slots, surface_slots, sems):
    start_weights(weight, held, sems)
    halves = lists.shape[0] // 4
    flux_slots[...] = slot_row(joined(lists, 0, halves), capacity)
    surface_slots[...] = slot_row(joined(lists, 2, halves), capacity)
    wait_weights(weight, held, sems)


def copies_of(source, target, sems, first):
    part = source.shape[0] // PARTS
    copies = []
    for c in range(PARTS):
        rows = pl.ds(c * part, part)
        copies.append(pltpu.make_async_copy(source.at[rows], target.at[rows], sems.at[first + c]))
        copies[-1].start()
    return copies


def wait_all(copies):
    for copy in copies:
        copy.wait()


def flux_kernel(halves, levels, slots_in, atm, diffusion, surface, north, south, east, west, weight, next_ref, sent, slots, high_ref, low_ref, placed, made, sems):
    read = pltpu.make_async_copy(slots_in, slots, sems.at[0])
    read.start()
    placed[...] = jnp.zeros(placed.shape, F32)
    east_turned, west_turned = jnp.transpose(east[...]), jnp.transpose(west[...])
    u, v, coef = atm[0], atm[1], diffusion[...]
    norths, souths = cleared(north, south)
    after = []
    for i in range(4):
        row = slice(i * levels, i * levels + 1)
        sides = neighbours(
            atm[i], norths[row, :], souths[row, :], column(east_turned, i, halves), column(west_turned, i, halves)
        )
        after.append(atm_step(atm[i], u, v, coef, sides))
        made[i] = after[i]
    writes = copies_of(made, next_ref.at[:, 0], sems, 1)
    du, dv = after[0] - surface[1], after[1] - surface[2]
    speed = jnp.sqrt(1.0 + du * du + dv * dv)
    sst, humidity = surface[0], after[3]
    moisture = moisture_coef * speed * (sst - humidity) - rain_coef * humidity * humidity
    put_split(
        [heat_coef * speed * (after[2] - sst), moisture, drag_coef * speed * du, drag_coef * speed * dv],
        high_ref,
        low_ref,
    )
    read.wait()
    product_rows(slots, weight, high_ref, low_ref, placed, 4)
    wait_all(writes + copies_of(placed, sent, sems, 1 + PARTS))


def atm_rest_kernel(halves, per_variable, atm, diffusion, north, south, east, west, started, out, turned_e, turned_w):
    level = pl.program_id(0)

    @pl.when(level == 0)
    def _():
        turn_columns(east, west, turned_e, turned_w)

    u, v, coef = atm[0, 0], atm[1, 0], diffusion[...]
    te, tw = turned_e[...], turned_w[...]
    has_north, has_south = inside()
    for i in range(4):
        at = i * per_variable + level
        row = pl.ds(i * (per_variable + 1) + level + 1, 1)
        a = atm[i, 0]
        n = jnp.where(has_north, north[row, :], 0.0)
        s = jnp.where(has_south, south[row, :], 0.0)
        sides = neighbours(a, n, s, picked(te, at, halves), picked(tw, at, halves))
        out[i, 0] = atm_step(a, u, v, coef, sides)


def turn_columns(east, west, turned_e, turned_w):
    turned_e[...] = jnp.transpose(east[...])
    turned_w[...] = jnp.transpose(west[...])


def picked(turned, at, halves):
    lane = lax.broadcasted_iota(jnp.int32, turned.shape, 1)
    parts = [jnp.sum(jnp.where(lane == at * halves + h, turned, 0.0), axis=1, keepdims=True) for h in range(halves)]
    return jnp.concatenate(parts, axis=0)


def sea_count(at, row, halves, mask, north, south, te, tw):
    norths, souths = cleared(north, south)
    row = slice(row, row + 1)
    n, s, e, w = neighbours(mask, norths[row, :], souths[row, :], column(te, at, halves), column(tw, at, halves))
    return n + s + e + w


def ocean_step(o, above, below, mask, count, sides):
    n, s, e, w = sides
    lateral = n + s + e + w - count * o
    vertical = above + below - 2.0 * o
    return mask * (o + ocean_diffusion * lateral + vertical_mixing * vertical)


def ocean_top_kernel(halves, base, levels, ocean, land, north, south, east, west, out):
    mask = land[...].astype(F32)
    te, tw = jnp.transpose(east[...]), jnp.transpose(west[...])
    count = sea_count(base + 4 * levels, 8 * levels, halves, mask, north, south, te, tw)
    norths, souths = cleared(north, south)
    for var in range(4):
        at = base + var * levels
        row = slice((4 + var) * levels, (4 + var) * levels + 1)
        o = ocean[var, 0]
        sides = neighbours(
            o * mask, norths[row, :], souths[row, :], column(te, at, halves), column(tw, at, halves)
        )
        out[var] = ocean_step(o, o, ocean[var, min(1, levels - 1)], mask, count, sides)


def ocean_rest_kernel(halves, base, levels, ocean, land, north, south, east, west, started, out, sem, made, count, turned_e, turned_w):
    var = pl.program_id(0)
    mask = land[...].astype(F32)

    @pl.when(var == 0)
    def _():
        turn_columns(east, west, turned_e, turned_w)
        count[...] = sea_count(base + 4 * levels, 8 * levels, halves, mask, north, south, turned_e[...], turned_w[...])

    te, tw = turned_e[...], turned_w[...]
    has_north, has_south = inside()
    for level in range(1, levels):
        at = base + var * levels + level
        row = pl.ds((4 + var) * levels + level, 1)
        o = ocean[0, level]
        n = jnp.where(has_north, north[row, :], 0.0)
        s = jnp.where(has_south, south[row, :], 0.0)
        sides = neighbours(o * mask, n, s, picked(te, at, halves), picked(tw, at, halves))
        made[level - 1] = ocean_step(
            o, ocean[0, level - 1], ocean[0, min(level + 1, levels - 1)], mask, count[...], sides
        )
    write = pltpu.make_async_copy(made, out.at[var, pl.ds(1, levels - 1)], sem)
    write.start()
    write.wait()


def far_lists(lists):
    size = lax.axis_size("comp")
    return [lax.ppermute(lists, "comp", [(i, (i - q) % size) for i in range(size)]) for q in range(2, size - 1)]


def lists_along_comp(lists, north, south, far):
    first = north.shape[0] - lists.shape[0]
    return jnp.stack([lists, north[first:], *far, south[first:]])


def lists_along_lon(held):
    size, bit, pieces = lax.axis_size("lon"), 1, [held]
    while bit < size:
        pieces.append(lax.ppermute(held, "lon", [(i, i ^ bit) for i in range(size)]))
        held, bit = jnp.concatenate([held, pieces[-1]], axis=0), 2 * bit
    return pieces


def arrivals_kernel(devices, capacity, *refs):
    *pieces, first, second, all_ref, sorted_ref = refs
    halves = pieces[0].shape[1] // 4
    rows = halves * LANES
    comp, lon = lax.axis_size("comp"), lax.axis_size("lon")
    my_comp, my_lon = lax.axis_index("comp"), lax.axis_index("lon")
    me = (my_comp * lon + my_lon).astype(F32)
    place = 0
    for piece in pieces:
        all_ref[place : place + piece.shape[0]] = piece[...]
        place += piece.shape[0]
    for s in range(devices):
        block = all_ref[lax.rem(s // lon - my_comp + comp, comp) + (my_lon ^ (s % lon)) * comp]
        for i in range(4):
            sorted_ref[i, s : s + 1, :] = joined(block, i, halves)
    j = lax.broadcasted_iota(jnp.int32, (rows, rows), 0)
    i = lax.broadcasted_iota(jnp.int32, (rows, rows), 1)
    before = jnp.where(j < i, 1.0, 0.0).astype(BF16)
    for which, out in enumerate((first, second)):
        named = sorted_ref[2 * which] == me
        target = sorted_ref[2 * which + 1]
        rank = jnp.dot(jnp.where(named, 1.0, 0.0).astype(BF16), before, preferred_element_type=F32)
        row = jnp.where(named, target + 1.0, 0.0)
        parts = [jnp.where(rank == float(k), row, 0.0) for k in range(capacity)]
        table = jnp.concatenate(parts, axis=0).astype(BF16)
        total = lax.dot_general(
            jnp.ones((8, rows), BF16), table, (((1,), (1,)), ((), ())), preferred_element_type=F32
        )
        wanted = lax.broadcasted_iota(jnp.int32, out.shape, 0).astype(F32) + 1.0
        out[...] = jnp.where(wanted == total[0:1, :], 1.0, 0.0).astype(BF16)


def summed_rows(devices, capacity, arrived, chosen, channels, read=None):
    columns = []
    for i in range(channels):
        parts = [
            arrived[pl.ds(k * channels + i, devices, stride=capacity * channels), :] for k in range(capacity)
        ]
        x = jnp.concatenate(parts, axis=0)
        high = x.astype(BF16)
        columns += [high, (x - high.astype(F32)).astype(BF16)]
    if read is not None:
        read.wait()
    total = jnp.dot(chosen[...], jnp.concatenate(columns, axis=1), preferred_element_type=F32)
    return [
        total[:, 2 * i * LANES : (2 * i + 1) * LANES] + total[:, (2 * i + 1) * LANES : (2 * i + 2) * LANES]
        for i in range(channels)
    ]


def forced_kernel(devices, capacity, slots_in, arrived, target, land, base, weight, next_ref, sent, slots, high_ref, low_ref, placed, made, sems, chosen, held, weight_sems, land_held):
    chosen_read = pltpu.make_async_copy(target, chosen, sems.at[1 + 2 * PARTS])
    chosen_read.start()
    reads = copies_of(base, made, sems, 1)
    reads += copies_of(land, land_held, sems, 1 + PARTS)
    slots_read = pltpu.make_async_copy(slots_in, slots, sems.at[0])
    slots_read.start()
    start_weights(weight, held, weight_sems)
    placed[...] = jnp.zeros(placed.shape, F32)
    forcing = summed_rows(devices, capacity, arrived, chosen, 4, chosen_read)
    wait_all(reads)
    mask = land_held[...].astype(F32)
    after = []
    for i in range(4):
        after.append(made[i] + mask * (forcing_gain * forcing[i]))
        made[i] = after[i]
    writes = copies_of(made, next_ref.at[:, 0], sems, 1)
    put_split([after[0], after[2], after[3]], high_ref, low_ref)
    slots_read.wait()
    per_loop, part = CHUNKS // LOOPS, held.shape[0] // CHUNKS

    def ready(c):
        for i in range(per_loop):
            rows = pl.ds((c * per_loop + i) * part, part)
            pltpu.make_async_copy(weight.at[rows], held.at[rows], weight_sems.at[c * per_loop + i]).wait()

    product_rows(slots, held, high_ref, low_ref, placed, 3, ready)
    wait_all(writes + copies_of(placed, sent, sems, 1 + PARTS))


def surface_kernel(devices, capacity, arrived, chosen, out):
    for i, total in enumerate(summed_rows(devices, capacity, arrived, chosen, 3)):
        out[i] = total


def whole(x):
    return pl.BlockSpec(x.shape, lambda *_: (0,) * len(x.shape))


def level_zero(x):
    return pl.BlockSpec((x.shape[0], 1) + x.shape[2:], lambda *_: (0, 0, 0, 0))


ANY = pl.BlockSpec(memory_space=pl.ANY)


def in_hbm(x):
    return pltpu.with_memory_space_constraint(x, pltpu.HBM)


def in_vmem(x):
    return pltpu.with_memory_space_constraint(x, pltpu.VMEM)


def body(
    atm_state, ocean_state, surface_state, atm_diffusion, land_sea, flux_dest, flux_row, flux_weight, surface_dest,
    surface_row, surface_weight,
):
    variables, levels, rows, cols = atm_state.shape
    devices = lax.axis_size("comp") * lax.axis_size("lon")
    capacity = max(2, 2 * rows // devices)
    width = devices * capacity
    halves = rows // LANES
    f32 = functools.partial(jax.ShapeDtypeStruct, dtype=F32)
    top = f32((variables, rows, cols))
    line = jax.ShapeDtypeStruct((1, rows), jnp.int32)
    all_rows = f32((-(-(2 * variables * levels + 1 + 4 * halves) // 8) * 8, cols))
    top_cols, own_lists = f32((variables * halves, cols)), f32((4 * halves, cols))
    made = [top, all_rows, all_rows, top_cols, top_cols, own_lists]
    atm_top, first_rows, last_rows, first_cols, last_cols, lists = pl.pallas_call(
        functools.partial(edges_kernel, halves, variables, levels, rows),
        grid=(1,),
        in_specs=[ANY] * 7,
        out_specs=[whole(e) for e in made],
        out_shape=made,
        scratch_shapes=[
            pltpu.VMEM((2, variables, levels, 8, cols), F32),
            pltpu.VMEM((2, variables, levels, 8, cols), F32),
            pltpu.VMEM((2, 8, cols), jnp.int32),
            pltpu.VMEM((4, 1, rows), jnp.int32),
            pltpu.SemaphoreType.DMA((variables + 10,)),
        ],
        compiler_params=params(),
        cost_estimate=cost(8),
        name="edges",
    )(
        *(in_hbm(x) for x in (atm_state, ocean_state, land_sea)),
        *(in_hbm(x.reshape(1, rows)) for x in (flux_dest, flux_row, surface_dest, surface_row)),
    )
    north, south = exchange_rows(first_rows, last_rows)
    sides = (north, south, *exchange_columns(first_cols, last_cols))
    far = far_lists(lists)
    in_memory = pl.BlockSpec(memory_space=pltpu.VMEM)
    held, flux_slots, surface_slots = pl.pallas_call(
        functools.partial(prepare_kernel, capacity),
        grid=(1,),
        in_specs=[whole(lists), ANY],
        out_specs=[in_memory, whole(line), whole(line)],
        out_shape=[pltpu.VMEM(flux_weight.shape, BF16)] + [pltpu.HBM(line.shape, jnp.int32)] * 2,
        scratch_shapes=[pltpu.SemaphoreType.DMA((CHUNKS,))],
        compiler_params=params(),
        cost_estimate=cost(4),
        name="prepare",
    )(lists, in_hbm(flux_weight))

    far, flux_slots = lax.optimization_barrier((far, flux_slots))

    def work(channels):
        return [
            pltpu.SMEM((1, rows), jnp.int32),
            pltpu.VMEM((rows * 4, cols), F32),
            pltpu.VMEM((rows * 4, cols), F32),
            pltpu.VMEM((width * channels, cols), F32),
            pltpu.VMEM(top.shape, F32),
            pltpu.SemaphoreType.DMA((2 + 2 * PARTS,)),
        ]

    atm_started, sent = pl.pallas_call(
        functools.partial(flux_kernel, halves, levels),
        grid=(1,),
        in_specs=[ANY]
        + [whole(e) for e in (atm_top, atm_diffusion, surface_state, *sides)]
        + [in_memory],
        out_specs=[ANY, ANY],
        scratch_shapes=work(4),
        out_shape=[f32(atm_state.shape), pltpu.HBM((width * 4, cols), F32)],
        compiler_params=params(),
        cost_estimate=cost(5),
        name="fluxes",
    )(in_hbm(flux_slots), atm_top, atm_diffusion, surface_state, *sides, in_vmem(held))
    arrived = lax.all_to_all(
        sent.reshape(devices, capacity * 4, cols), AXES, split_axis=0, concat_axis=0, tiled=True
    ).reshape(width * 4, cols)

    along_comp = lists_along_comp(lists, north, south, far)
    along_comp, land, _ = lax.optimization_barrier((along_comp, land_sea, sent))
    pieces = lists_along_lon(along_comp)
    count = variables * (levels - 1) + variables * levels + 1
    padded = -(-count // 8) * 8
    rest_cols = f32((padded * halves, cols))
    rest = pl.pallas_call(
        functools.partial(rest_edges_kernel, halves, variables, levels),
        grid=(1,),
        in_specs=[whole(atm_state), whole(ocean_state), whole(land_sea)],
        out_specs=[whole(rest_cols)] * 2,
        out_shape=[rest_cols, rest_cols],
        compiler_params=params(),
        cost_estimate=cost(8),
        name="rest_edges",
    )(atm_state, ocean_state, land)
    rest = (north, south, *exchange_columns(*rest))
    base = variables * (levels - 1)
    ocean_top = pl.pallas_call(
        functools.partial(ocean_top_kernel, halves, base, levels),
        grid=(1,),
        in_specs=[pl.BlockSpec((variables, min(2, levels), rows, cols), lambda i: (0, 0, 0, 0)), whole(land_sea)]
        + [whole(e) for e in rest],
        out_specs=whole(top),
        out_shape=pltpu.HBM(top.shape, F32),
        compiler_params=params(),
        cost_estimate=cost(4),
        name="ocean_top",
    )(ocean_state, land_sea, *rest)
    target = jax.ShapeDtypeStruct((rows, width), BF16)
    flux_target, surface_target = pl.pallas_call(
        functools.partial(arrivals_kernel, devices, capacity),
        grid=(1,),
        in_specs=[whole(piece) for piece in pieces],
        out_specs=[whole(target)] * 2,
        scratch_shapes=[pltpu.VMEM((devices, 4 * halves, cols), F32), pltpu.VMEM((4, devices, rows), F32)],
        out_shape=[pltpu.HBM(target.shape, BF16), target],
        compiler_params=params(),
        cost_estimate=cost(1),
        name="arrivals",
    )(*pieces)

    ocean_started, back = pl.pallas_call(
        functools.partial(forced_kernel, devices, capacity),
        grid=(1,),
        in_specs=[ANY, whole(arrived), ANY, ANY, ANY, ANY],
        out_specs=[ANY, ANY],
        scratch_shapes=work(3)
        + [
            pltpu.VMEM(target.shape, BF16),
            pltpu.VMEM(surface_weight.shape, BF16),
            pltpu.SemaphoreType.DMA((CHUNKS,)),
            pltpu.VMEM((rows, cols), jnp.int32),
        ],
        out_shape=[f32(ocean_state.shape), pltpu.HBM((width * 3, cols), F32)],
        compiler_params=params(),
        cost_estimate=cost(5),
        name="forced",
    )(in_hbm(surface_slots), arrived, in_hbm(flux_target), in_hbm(land_sea), in_hbm(ocean_top), in_hbm(surface_weight))
    returned = lax.all_to_all(
        back.reshape(devices, capacity * 3, cols), AXES, split_axis=0, concat_axis=0, tiled=True
    ).reshape(width * 3, cols)

    turned = [pltpu.VMEM((cols, padded * halves), F32)] * 2
    one_level = pl.BlockSpec((variables, 1, rows, cols), lambda i: (0, i + 1, 0, 0))
    atm_next = pl.pallas_call(
        functools.partial(atm_rest_kernel, halves, levels - 1),
        grid=(levels - 1,),
        in_specs=[one_level, whole(atm_diffusion)] + [whole(e) for e in rest] + [ANY],
        out_specs=one_level,
        out_shape=f32(atm_state.shape),
        scratch_shapes=turned,
        input_output_aliases={6: 0},
        compiler_params=params(),
        cost_estimate=cost(5),
        name="atm_rest",
    )(atm_state, atm_diffusion, *rest, atm_started)
    ocean_next = pl.pallas_call(
        functools.partial(ocean_rest_kernel, halves, base, levels),
        grid=(variables,),
        in_specs=[pl.BlockSpec((1, levels, rows, cols), lambda i: (i, 0, 0, 0)), whole(land_sea)]
        + [whole(e) for e in rest]
        + [ANY],
        out_specs=ANY,
        out_shape=f32(ocean_state.shape),
        scratch_shapes=[
            pltpu.SemaphoreType.DMA(()),
            pltpu.VMEM((levels - 1, rows, cols), F32),
            pltpu.VMEM((rows, cols), F32),
        ]
        + turned,
        input_output_aliases={6: 0},
        compiler_params=params(),
        cost_estimate=cost(6),
        name="ocean_rest",
    )(ocean_state, land_sea, *rest, ocean_started)
    surface_next = pl.pallas_call(
        functools.partial(surface_kernel, devices, capacity),
        grid=(1,),
        in_specs=[whole(returned), whole(surface_target)],
        out_specs=whole(surface_state),
        out_shape=f32(surface_state.shape),
        compiler_params=params(),
        cost_estimate=cost(1),
        name="surface",
    )(returned, surface_target)
    return (atm_next, ocean_next, surface_next)


def solution(mesh):
    in_specs = (
        P(None, None, "comp", "lon"),
        P(None, None, "comp", "lon"),
        P(None, "comp", "lon"),
        P("comp", "lon"),
        P("comp", "lon"),
        P(("comp", "lon"), None),
        P(("comp", "lon")),
        P(("comp", "lon"), None, None),
        P(("comp", "lon"), None),
        P(("comp", "lon")),
        P(("comp", "lon"), None, None),
    )
    out_specs = (P(None, None, "comp", "lon"), P(None, None, "comp", "lon"), P(None, "comp", "lon"))
    return jax.shard_map(body, mesh=mesh, in_specs=in_specs, out_specs=out_specs, check_vma=False)
```

```python
import functools

import jax
import jax.numpy as jnp
from jax import lax
from jax.experimental import pallas as pl
from jax.experimental.pallas import tpu as pltpu
from jax.sharding import PartitionSpec as P

time_step = 0.1
ocean_diffusion = 0.2
vertical_mixing = 0.2
drag_coef = 0.4
heat_coef = 0.5
moisture_coef = 0.3
rain_coef = 0.2
forcing_gain = 0.5

AXES = ("comp", "lon")
LANES = 128
CHUNKS = 8
LOOPS = 2
PARTS = 4
F32 = jnp.float32
BF16 = jnp.bfloat16
VMEM_LIMIT = 24 << 20


def cost(microseconds):
    return pl.CostEstimate(flops=int(microseconds * 1e9), bytes_accessed=1 << 20, transcendentals=0)


def params(**kw):
    return pltpu.CompilerParams(vmem_limit_bytes=VMEM_LIMIT, **kw)


def shift(x, axis, up):
    devices = lax.axis_size(axis)
    pairs = [(i, (i + 1) % devices) for i in range(devices)]
    if not up:
        pairs = [(j, i) for i, j in pairs]
    return lax.ppermute(x, axis, pairs)


def exchange_rows(first_rows, last_rows):
    return shift(first_rows, "comp", False), shift(last_rows, "comp", True)


def exchange_columns(first_cols, last_cols):
    return shift(first_cols, "lon", False), shift(last_cols, "lon", True)


def inside():
    at = lax.axis_index("comp")
    return at < lax.axis_size("comp") - 1, at > 0


def cleared(north, south):
    has_north, has_south = inside()
    return jnp.where(has_north, north[...], 0.0), jnp.where(has_south, south[...], 0.0)


def put_columns(field, at, halves, first_cols, last_cols):
    for h in range(halves):
        turned = jnp.transpose(field[h * LANES : (h + 1) * LANES, :])
        row = at * halves + h
        first_cols[row : row + 1, :] = turned[0:1, :]
        last_cols[row : row + 1, :] = turned[LANES - 1 : LANES, :]


def neighbours(x, north, south, east, west):
    rows, cols = x.shape
    row = lax.broadcasted_iota(jnp.int32, x.shape, 0)
    col = lax.broadcasted_iota(jnp.int32, x.shape, 1)
    n = jnp.where(row == rows - 1, north, pltpu.roll(x, rows - 1, 0))
    s = jnp.where(row == 0, south, pltpu.roll(x, 1, 0))
    e = jnp.where(col == cols - 1, east, pltpu.roll(x, cols - 1, 1))
    w = jnp.where(col == 0, west, pltpu.roll(x, 1, 1))
    return n, s, e, w


def column(turned, at, halves):
    parts = [turned[:, at * halves + h : at * halves + h + 1] for h in range(halves)]
    return jnp.concatenate(parts, axis=0)


def edges_kernel(halves, variables, levels, rows, atm, ocean, land, *refs):
    list_refs = refs[:4]
    held, first_rows, last_rows, first_cols, last_cols, lists, atm_ends, ocean_ends, land_ends, lines, sems = refs[4:]
    copies = [pltpu.make_async_copy(atm.at[v, 0], held.at[v], sems.at[v]) for v in range(variables)]
    ends = (pl.ds(0, 8), pl.ds(rows - 8, 8))
    for side in range(2):
        copies.append(pltpu.make_async_copy(atm.at[:, :, ends[side]], atm_ends.at[side], sems.at[variables + side]))
        copies.append(pltpu.make_async_copy(ocean.at[:, :, ends[side]], ocean_ends.at[side], sems.at[variables + 2 + side]))
        copies.append(pltpu.make_async_copy(land.at[ends[side]], land_ends.at[side], sems.at[variables + 4 + side]))
    for i, ref in enumerate(list_refs):
        copies.append(pltpu.make_async_copy(ref, lines.at[i], sems.at[variables + 6 + i]))
    for copy in copies:
        copy.start()
    for v in range(variables):
        copies[v].wait()
        put_columns(held[v], v, halves, first_cols, last_cols)
    wait_all(copies[variables:])
    for side, out in enumerate((first_rows, last_rows)):
        row = slice(0, 1) if side == 0 else slice(7, 8)
        mask = land_ends[side, row, :].astype(F32)
        at = 0
        for v in range(variables):
            for level in range(levels):
                out[at : at + 1, :] = atm_ends[side, v, level, row, :]
                at += 1
        for v in range(variables):
            for level in range(levels):
                out[at : at + 1, :] = ocean_ends[side, v, level, row, :] * mask
                at += 1
        out[at : at + 1, :] = mask
        out[at + 1 :, :] = jnp.zeros((out.shape[0] - at - 1, LANES), F32)
    for i in range(4):
        for h in range(halves):
            line = lines[i, :, h * LANES : (h + 1) * LANES].astype(F32)
            for out, at in ((first_rows, first_rows.shape[0] - 4 * halves), (last_rows, first_rows.shape[0] - 4 * halves), (lists, 0)):
                out[at + i * halves + h : at + i * halves + h + 1, :] = line


def rest_edges_kernel(halves, variables, levels, atm, ocean, land, first_cols, last_cols):
    at = 0
    for v in range(variables):
        for level in range(1, levels):
            put_columns(atm[v, level], at, halves, first_cols, last_cols)
            at += 1
    mask = land[...].astype(F32)
    for v in range(variables):
        for level in range(levels):
            put_columns(ocean[v, level] * mask, at, halves, first_cols, last_cols)
            at += 1
    put_columns(mask, at, halves, first_cols, last_cols)
    used = (at + 1) * halves
    for ref in (first_cols, last_cols):
        if used < ref.shape[0]:
            ref[used:, :] = jnp.zeros((ref.shape[0] - used, LANES), F32)


def atm_step(a, u, v, diffusion, sides):
    n, s, e, w = sides
    laplace = n + s + e + w - 4.0 * a
    advection = u * (e - w) + v * (n - s)
    return a + diffusion * laplace - 0.5 * time_step * advection


def put_split(fields, high_ref, low_ref):
    rows = fields[0].shape[0]
    for i in range(4):
        if i < len(fields):
            high = fields[i].astype(BF16).astype(F32)
            low = fields[i] - high
        else:
            high = low = jnp.zeros((rows, LANES), F32)
        high_ref[pl.ds(i, rows, stride=4), :] = high
        low_ref[pl.ds(i, rows, stride=4), :] = low


def weight_copies(weight, held, sems):
    part = held.shape[0] // CHUNKS
    for c in range(CHUNKS):
        rows = pl.ds(c * part, part)
        yield pltpu.make_async_copy(weight.at[rows], held.at[rows], sems.at[c])


def start_weights(weight, held, sems):
    for copy in weight_copies(weight, held, sems):
        copy.start()


def wait_weights(weight, held, sems):
    for copy in weight_copies(weight, held, sems):
        copy.wait()


def product_rows(slots, weight, high_ref, low_ref, placed, channels, ready=None):
    part = weight.shape[0] // LOOPS

    def some(c, carry):
        if ready is not None:
            ready(c)
        for i in range(0, part, 2):
            r = c * part + i
            at = pl.ds(pl.multiple_of(r * 4, 8), 8)
            left = jnp.concatenate([high_ref[at, :].astype(BF16), low_ref[at, :].astype(BF16)], axis=0)
            right = jnp.concatenate([weight[r], weight[r + 1]], axis=1)
            both = jnp.dot(left, right, preferred_element_type=F32)
            both = both[:8] + both[8:]
            placed[pl.ds(slots[0, r] * channels, channels), :] = both[:channels, :LANES]
            placed[pl.ds(slots[0, r + 1] * channels, channels), :] = both[4 : 4 + channels, LANES:]
        return carry

    lax.fori_loop(0, LOOPS, some, 0)


def joined(rows, i, halves):
    return jnp.concatenate([rows[i * halves + h : i * halves + h + 1, :] for h in range(halves)], axis=1)


def slot_row(destination, capacity):
    rows = destination.shape[1]
    wide = jnp.broadcast_to(destination, (8, rows))
    column_of = jnp.concatenate([jnp.transpose(wide[:, i : i + LANES]) for i in range(0, rows, LANES)], axis=0)[:, 0:1]
    j = lax.broadcasted_iota(jnp.int32, (rows, rows), 0)
    i = lax.broadcasted_iota(jnp.int32, (rows, rows), 1)
    earlier = (column_of == wide[0:1, :]) & (j < i)
    rank = jnp.sum(jnp.where(earlier, 1.0, 0.0), axis=0, keepdims=True)
    return (destination * float(capacity) + rank).astype(jnp.int32)


def prepare_kernel(capacity, lists, weight, held, flux_slots, surface_slots, sems):
    start_weights(weight, held, sems)
    halves = lists.shape[0] // 4
    flux_slots[...] = slot_row(joined(lists, 0, halves), capacity)
    surface_slots[...] = slot_row(joined(lists, 2, halves), capacity)
    wait_weights(weight, held, sems)


def copies_of(source, target, sems, first):
    part = source.shape[0] // PARTS
    copies = []
    for c in range(PARTS):
        rows = pl.ds(c * part, part)
        copies.append(pltpu.make_async_copy(source.at[rows], target.at[rows], sems.at[first + c]))
        copies[-1].start()
    return copies


def wait_all(copies):
    for copy in copies:
        copy.wait()


def flux_kernel(halves, levels, slots_in, atm, diffusion, surface, north, south, east, west, weight, next_ref, sent, slots, high_ref, low_ref, made, sems, placed):
    read = pltpu.make_async_copy(slots_in, slots, sems.at[0])
    read.start()
    placed[...] = jnp.zeros(placed.shape, F32)
    east_turned, west_turned = jnp.transpose(east[...]), jnp.transpose(west[...])
    u, v, coef = atm[0], atm[1], diffusion[...]
    norths, souths = cleared(north, south)
    after = []
    for i in range(4):
        row = slice(i * levels, i * levels + 1)
        sides = neighbours(
            atm[i], norths[row, :], souths[row, :], column(east_turned, i, halves), column(west_turned, i, halves)
        )
        after.append(atm_step(atm[i], u, v, coef, sides))
        made[i] = after[i]
    writes = copies_of(made, next_ref.at[:, 0], sems, 1)
    du, dv = after[0] - surface[1], after[1] - surface[2]
    speed = jnp.sqrt(1.0 + du * du + dv * dv)
    sst, humidity = surface[0], after[3]
    moisture = moisture_coef * speed * (sst - humidity) - rain_coef * humidity * humidity
    put_split(
        [heat_coef * speed * (after[2] - sst), moisture, drag_coef * speed * du, drag_coef * speed * dv],
        high_ref,
        low_ref,
    )
    read.wait()
    product_rows(slots, weight, high_ref, low_ref, placed, 4)
    wait_all(writes + copies_of(placed, sent, sems, 1 + PARTS))


def atm_rest_kernel(halves, levels, atm, diffusion, north, south, east, west, started, out, made, sems):
    coef = diffusion[...]
    te, tw = jnp.transpose(east[...]), jnp.transpose(west[...])
    norths, souths = cleared(north, south)
    writes = []
    for level in range(1, levels):
        u, v = atm[0, level], atm[1, level]
        for i in range(4):
            at = i * (levels - 1) + level - 1
            row = slice(i * levels + level, i * levels + level + 1)
            a = atm[i, level]
            sides = neighbours(a, norths[row, :], souths[row, :], column(te, at, halves), column(tw, at, halves))
            made[at] = atm_step(a, u, v, coef, sides)
            writes.append(pltpu.make_async_copy(made.at[at], out.at[i, level], sems.at[at]))
            writes[-1].start()
    wait_all(writes)


def ocean_kernel(halves, base, levels, ocean, land, north, south, east, west, out, made, sems):
    mask = land[...].astype(F32)
    te, tw = jnp.transpose(east[...]), jnp.transpose(west[...])
    norths, souths = cleared(north, south)
    row, at = slice(8 * levels, 8 * levels + 1), base + 4 * levels
    n, s, e, w = neighbours(mask, norths[row, :], souths[row, :], column(te, at, halves), column(tw, at, halves))
    count = n + s + e + w
    writes = []
    for var in range(4):
        for level in range(levels):
            place = var * levels + level
            at = base + place
            row = slice(4 * levels + place, 4 * levels + place + 1)
            o = ocean[var, level]
            n, s, e, w = neighbours(
                o * mask, norths[row, :], souths[row, :], column(te, at, halves), column(tw, at, halves)
            )
            lateral = n + s + e + w - count * o
            vertical = ocean[var, max(level - 1, 0)] + ocean[var, min(level + 1, levels - 1)] - 2.0 * o
            made[place] = mask * (o + ocean_diffusion * lateral + vertical_mixing * vertical)
            writes.append(pltpu.make_async_copy(made.at[place], out.at[var, level], sems.at[place]))
            writes[-1].start()
    wait_all(writes)


def far_lists(lists):
    size = lax.axis_size("comp")
    return [lax.ppermute(lists, "comp", [(i, (i - q) % size) for i in range(size)]) for q in range(2, size - 1)]


def lists_along_comp(lists, north, south, far):
    first = north.shape[0] - lists.shape[0]
    return jnp.stack([lists, north[first:], *far, south[first:]])


def lists_along_lon(held):
    size, bit, pieces = lax.axis_size("lon"), 1, [held]
    while bit < size:
        pieces.append(lax.ppermute(held, "lon", [(i, i ^ bit) for i in range(size)]))
        held, bit = jnp.concatenate([held, pieces[-1]], axis=0), 2 * bit
    return pieces


def arrivals_kernel(devices, capacity, *refs):
    *pieces, first, second, all_ref, sorted_ref = refs
    halves = pieces[0].shape[1] // 4
    rows = halves * LANES
    comp, lon = lax.axis_size("comp"), lax.axis_size("lon")
    my_comp, my_lon = lax.axis_index("comp"), lax.axis_index("lon")
    me = (my_comp * lon + my_lon).astype(F32)
    place = 0
    for piece in pieces:
        all_ref[place : place + piece.shape[0]] = piece[...]
        place += piece.shape[0]
    for s in range(devices):
        block = all_ref[lax.rem(s // lon - my_comp + comp, comp) + (my_lon ^ (s % lon)) * comp]
        for i in range(4):
            sorted_ref[i, s : s + 1, :] = joined(block, i, halves)
    j = lax.broadcasted_iota(jnp.int32, (rows, rows), 0)
    i = lax.broadcasted_iota(jnp.int32, (rows, rows), 1)
    before = jnp.where(j < i, 1.0, 0.0).astype(BF16)
    for which, out in enumerate((first, second)):
        named = sorted_ref[2 * which] == me
        target = sorted_ref[2 * which + 1]
        rank = jnp.dot(jnp.where(named, 1.0, 0.0).astype(BF16), before, preferred_element_type=F32)
        row = jnp.where(named, target + 1.0, 0.0)
        parts = [jnp.where(rank == float(k), row, 0.0) for k in range(capacity)]
        table = jnp.concatenate(parts, axis=0).astype(BF16)
        total = lax.dot_general(
            jnp.ones((8, rows), BF16), table, (((1,), (1,)), ((), ())), preferred_element_type=F32
        )
        wanted = lax.broadcasted_iota(jnp.int32, out.shape, 0).astype(F32) + 1.0
        out[...] = jnp.where(wanted == total[0:1, :], 1.0, 0.0).astype(BF16)


def summed_channel(devices, capacity, arrived, chosen, channels, i):
    parts = [arrived[pl.ds(k * channels + i, devices, stride=capacity * channels), :] for k in range(capacity)]
    x = jnp.concatenate(parts, axis=0)
    high = x.astype(BF16)
    low = (x - high.astype(F32)).astype(BF16)
    total = jnp.dot(chosen[...], jnp.concatenate([high, low], axis=1), preferred_element_type=F32)
    return total[:, :LANES] + total[:, LANES:]


def forced_kernel(devices, capacity, slots_in, arrived, target, land, base, weight, after_this, next_ref, placed, slots, high_ref, low_ref, made, sems, chosen, held, weight_sems, land_held):
    chosen_read = pltpu.make_async_copy(target, chosen, sems.at[1 + 2 * PARTS])
    chosen_read.start()
    reads = copies_of(base.at[:, 0], made, sems, 1)
    reads += copies_of(land, land_held, sems, 1 + PARTS)
    slots_read = pltpu.make_async_copy(slots_in, slots, sems.at[0])
    slots_read.start()
    start_weights(weight, held, weight_sems)
    placed[...] = jnp.zeros(placed.shape, F32)
    chosen_read.wait()
    forcing = [summed_channel(devices, capacity, arrived, chosen, 4, i) for i in range(4)]
    wait_all(reads)
    mask = land_held[...].astype(F32)
    after = []
    for i in range(4):
        after.append(made[i] + mask * (forcing_gain * forcing[i]))
        made[i] = after[i]
    writes = copies_of(made, next_ref.at[:, 0], sems, 1)
    put_split([after[0], after[2], after[3]], high_ref, low_ref)
    slots_read.wait()
    per_loop, part = CHUNKS // LOOPS, held.shape[0] // CHUNKS

    def ready(c):
        for i in range(per_loop):
            rows = pl.ds((c * per_loop + i) * part, part)
            pltpu.make_async_copy(weight.at[rows], held.at[rows], weight_sems.at[c * per_loop + i]).wait()

    product_rows(slots, held, high_ref, low_ref, placed, 3, ready)
    wait_all(writes)


def surface_kernel(devices, capacity, arrived, chosen, out, made, sems):
    writes = []
    for i in range(3):
        made[i] = summed_channel(devices, capacity, arrived, chosen, 3, i)
        writes.append(pltpu.make_async_copy(made.at[i], out.at[i], sems.at[i]))
        writes[i].start()
    wait_all(writes)


def whole(x):
    return pl.BlockSpec(x.shape, lambda *_: (0,) * len(x.shape))


def level_zero(x):
    return pl.BlockSpec((x.shape[0], 1) + x.shape[2:], lambda *_: (0, 0, 0, 0))


ANY = pl.BlockSpec(memory_space=pl.ANY)


def in_hbm(x):
    return pltpu.with_memory_space_constraint(x, pltpu.HBM)


def in_vmem(x):
    return pltpu.with_memory_space_constraint(x, pltpu.VMEM)


def body(
    atm_state, ocean_state, surface_state, atm_diffusion, land_sea, flux_dest, flux_row, flux_weight, surface_dest,
    surface_row, surface_weight,
):
    variables, levels, rows, cols = atm_state.shape
    devices = lax.axis_size("comp") * lax.axis_size("lon")
    capacity = max(2, 2 * rows // devices)
    width = devices * capacity
    halves = rows // LANES
    f32 = functools.partial(jax.ShapeDtypeStruct, dtype=F32)
    top = f32((variables, rows, cols))
    line = jax.ShapeDtypeStruct((1, rows), jnp.int32)
    all_rows = f32((-(-(2 * variables * levels + 1 + 4 * halves) // 8) * 8, cols))
    top_cols, own_lists = f32((variables * halves, cols)), f32((4 * halves, cols))
    made = [top, all_rows, all_rows, top_cols, top_cols, own_lists]
    atm_top, first_rows, last_rows, first_cols, last_cols, lists = pl.pallas_call(
        functools.partial(edges_kernel, halves, variables, levels, rows),
        grid=(1,),
        in_specs=[ANY] * 7,
        out_specs=[whole(e) for e in made],
        out_shape=made,
        scratch_shapes=[
            pltpu.VMEM((2, variables, levels, 8, cols), F32),
            pltpu.VMEM((2, variables, levels, 8, cols), F32),
            pltpu.VMEM((2, 8, cols), jnp.int32),
            pltpu.VMEM((4, 1, rows), jnp.int32),
            pltpu.SemaphoreType.DMA((variables + 10,)),
        ],
        compiler_params=params(),
        cost_estimate=cost(8),
        name="edges",
    )(
        *(in_hbm(x) for x in (atm_state, ocean_state, land_sea)),
        *(in_hbm(x.reshape(1, rows)) for x in (flux_dest, flux_row, surface_dest, surface_row)),
    )
    north, south = exchange_rows(first_rows, last_rows)
    sides = (north, south, *exchange_columns(first_cols, last_cols))
    far = far_lists(lists)
    in_memory = pl.BlockSpec(memory_space=pltpu.VMEM)
    held, flux_slots, surface_slots = pl.pallas_call(
        functools.partial(prepare_kernel, capacity),
        grid=(1,),
        in_specs=[whole(lists), ANY],
        out_specs=[in_memory, whole(line), whole(line)],
        out_shape=[pltpu.VMEM(flux_weight.shape, BF16)] + [pltpu.HBM(line.shape, jnp.int32)] * 2,
        scratch_shapes=[pltpu.SemaphoreType.DMA((CHUNKS,))],
        compiler_params=params(),
        cost_estimate=cost(4),
        name="prepare",
    )(lists, in_hbm(flux_weight))

    far, flux_slots = lax.optimization_barrier((far, flux_slots))

    work = [
        pltpu.SMEM((1, rows), jnp.int32),
        pltpu.VMEM((rows * 4, cols), F32),
        pltpu.VMEM((rows * 4, cols), F32),
        pltpu.VMEM(top.shape, F32),
        pltpu.SemaphoreType.DMA((2 + 2 * PARTS,)),
    ]
    atm_started, sent = pl.pallas_call(
        functools.partial(flux_kernel, halves, levels),
        grid=(1,),
        in_specs=[ANY]
        + [whole(e) for e in (atm_top, atm_diffusion, surface_state, *sides)]
        + [in_memory],
        out_specs=[ANY, ANY],
        scratch_shapes=[*work, pltpu.VMEM((width * 4, cols), F32)],
        out_shape=[f32(atm_state.shape), pltpu.HBM((width * 4, cols), F32)],
        compiler_params=params(),
        cost_estimate=cost(5),
        name="fluxes",
    )(in_hbm(flux_slots), atm_top, atm_diffusion, surface_state, *sides, in_vmem(held))
    arrived = lax.all_to_all(
        sent.reshape(devices, capacity * 4, cols), AXES, split_axis=0, concat_axis=0, tiled=True
    ).reshape(width * 4, cols)

    along_comp = lists_along_comp(lists, north, south, far)
    along_comp, land, _ = lax.optimization_barrier((along_comp, land_sea, sent))
    pieces = lists_along_lon(along_comp)
    count = variables * (levels - 1) + variables * levels + 1
    padded = -(-count // 8) * 8
    rest_cols = f32((padded * halves, cols))
    rest = pl.pallas_call(
        functools.partial(rest_edges_kernel, halves, variables, levels),
        grid=(1,),
        in_specs=[whole(atm_state), whole(ocean_state), whole(land_sea)],
        out_specs=[whole(rest_cols)] * 2,
        out_shape=[rest_cols, rest_cols],
        compiler_params=params(),
        cost_estimate=cost(8),
        name="rest_edges",
    )(atm_state, ocean_state, land)
    rest = (north, south, *exchange_columns(*rest))
    base = variables * (levels - 1)
    atm_next = pl.pallas_call(
        functools.partial(atm_rest_kernel, halves, levels),
        grid=(1,),
        in_specs=[whole(atm_state), whole(atm_diffusion)] + [whole(e) for e in rest] + [ANY],
        out_specs=ANY,
        out_shape=f32(atm_state.shape),
        scratch_shapes=[pltpu.VMEM((base, rows, cols), F32), pltpu.SemaphoreType.DMA((base,))],
        input_output_aliases={6: 0},
        compiler_params=params(),
        cost_estimate=cost(4),
        name="atm_rest",
    )(atm_state, atm_diffusion, *rest, atm_started)
    fields = variables * levels
    ocean_base = pl.pallas_call(
        functools.partial(ocean_kernel, halves, base, levels),
        grid=(1,),
        in_specs=[whole(ocean_state), whole(land_sea)] + [whole(e) for e in rest],
        out_specs=ANY,
        out_shape=pltpu.HBM(ocean_state.shape, F32),
        scratch_shapes=[pltpu.VMEM((fields, rows, cols), F32), pltpu.SemaphoreType.DMA((fields,))],
        compiler_params=params(),
        cost_estimate=cost(5),
        name="ocean_base",
    )(ocean_state, land_sea, *rest)
    target = jax.ShapeDtypeStruct((rows, width), BF16)
    flux_target, surface_target = pl.pallas_call(
        functools.partial(arrivals_kernel, devices, capacity),
        grid=(1,),
        in_specs=[whole(piece) for piece in pieces],
        out_specs=[whole(target)] * 2,
        scratch_shapes=[pltpu.VMEM((devices, 4 * halves, cols), F32), pltpu.VMEM((4, devices, rows), F32)],
        out_shape=[pltpu.HBM(target.shape, BF16), target],
        compiler_params=params(),
        cost_estimate=cost(1),
        name="arrivals",
    )(*pieces)

    back_shape = f32((width * 3, cols))
    ocean_next, back = pl.pallas_call(
        functools.partial(forced_kernel, devices, capacity),
        grid=(1,),
        in_specs=[ANY, whole(arrived), ANY, ANY, ANY, ANY, ANY],
        out_specs=[ANY, whole(back_shape)],
        scratch_shapes=[
            *work,
            pltpu.VMEM(target.shape, BF16),
            pltpu.VMEM(surface_weight.shape, BF16),
            pltpu.SemaphoreType.DMA((CHUNKS,)),
            pltpu.VMEM((rows, cols), jnp.int32),
        ],
        out_shape=[f32(ocean_state.shape), back_shape],
        input_output_aliases={4: 0},
        compiler_params=params(),
        cost_estimate=cost(5),
        name="forced",
    )(in_hbm(surface_slots), arrived, in_hbm(flux_target), in_hbm(land_sea), ocean_base, in_hbm(surface_weight), in_hbm(atm_next))
    returned = lax.all_to_all(
        back.reshape(devices, capacity * 3, cols), AXES, split_axis=0, concat_axis=0, tiled=True
    ).reshape(width * 3, cols)

    surface_next = pl.pallas_call(
        functools.partial(surface_kernel, devices, capacity),
        grid=(1,),
        in_specs=[whole(returned), whole(surface_target)],
        out_specs=ANY,
        out_shape=f32(surface_state.shape),
        scratch_shapes=[pltpu.VMEM(surface_state.shape, F32), pltpu.SemaphoreType.DMA((3,))],
        compiler_params=params(),
        cost_estimate=cost(1),
        name="surface",
    )(returned, surface_target)
    return (atm_next, ocean_next, surface_next)


def solution(mesh):
    in_specs = (
        P(None, None, "comp", "lon"),
        P(None, None, "comp", "lon"),
        P(None, "comp", "lon"),
        P("comp", "lon"),
        P("comp", "lon"),
        P(("comp", "lon"), None),
        P(("comp", "lon")),
        P(("comp", "lon"), None, None),
        P(("comp", "lon"), None),
        P(("comp", "lon")),
        P(("comp", "lon"), None, None),
    )
    out_specs = (P(None, None, "comp", "lon"), P(None, None, "comp", "lon"), P(None, "comp", "lon"))
    return jax.shard_map(body, mesh=mesh, in_specs=in_specs, out_specs=out_specs, check_vma=False)
```

```python
import functools
import math

import jax
import jax.numpy as jnp
from jax import lax
from jax.experimental import pallas as pl
from jax.experimental.pallas import tpu as pltpu
from jax.sharding import PartitionSpec as P

time_step = 0.1
ocean_diffusion = 0.2
vertical_mixing = 0.2
drag_coef = 0.4
heat_coef = 0.5
moisture_coef = 0.3
rain_coef = 0.2
forcing_gain = 0.5

AXES = ("comp", "lon")
LANES = 128
CHUNKS = 8
EARLY = 2
STEP = 128
LATE = 3
PARTS = 4
F32 = jnp.float32
BF16 = jnp.bfloat16
VMEM_LIMIT = 24 << 20


def cost(microseconds):
    return pl.CostEstimate(flops=int(microseconds * 1e9), bytes_accessed=1 << 20, transcendentals=0)


def params(**kw):
    return pltpu.CompilerParams(vmem_limit_bytes=VMEM_LIMIT, **kw)


def shift(x, axis, up):
    devices = lax.axis_size(axis)
    pairs = [(i, (i + 1) % devices) for i in range(devices)]
    if not up:
        pairs = [(j, i) for i, j in pairs]
    return lax.ppermute(x, axis, pairs)


def exchange_rows(first_rows, last_rows):
    return shift(first_rows, "comp", False), shift(last_rows, "comp", True)


def exchange_columns(first_cols, last_cols):
    return shift(first_cols, "lon", False), shift(last_cols, "lon", True)


def inside():
    at = lax.axis_index("comp")
    return at < lax.axis_size("comp") - 1, at > 0


def cleared(north, south):
    has_north, has_south = inside()
    return jnp.where(has_north, north[...], 0.0), jnp.where(has_south, south[...], 0.0)


def put_columns(field, at, halves, first_cols, last_cols):
    for h in range(halves):
        turned = jnp.transpose(field[h * LANES : (h + 1) * LANES, :])
        row = at * halves + h
        first_cols[row : row + 1, :] = turned[0:1, :]
        last_cols[row : row + 1, :] = turned[LANES - 1 : LANES, :]


def neighbours(x, north, south, east, west):
    rows, cols = x.shape
    row = lax.broadcasted_iota(jnp.int32, x.shape, 0)
    col = lax.broadcasted_iota(jnp.int32, x.shape, 1)
    n = jnp.where(row == rows - 1, north, pltpu.roll(x, rows - 1, 0))
    s = jnp.where(row == 0, south, pltpu.roll(x, 1, 0))
    e = jnp.where(col == cols - 1, east, pltpu.roll(x, cols - 1, 1))
    w = jnp.where(col == 0, west, pltpu.roll(x, 1, 1))
    return n, s, e, w


def column(turned, at, halves):
    parts = [turned[:, at * halves + h : at * halves + h + 1] for h in range(halves)]
    return jnp.concatenate(parts, axis=0)


def edges_kernel(halves, variables, levels, rows, atm, ocean, land, *refs):
    list_refs = refs[:4]
    held, first_rows, last_rows, first_cols, last_cols, lists, atm_ends, ocean_ends, land_ends, lines, sems = refs[4:]
    copies = [pltpu.make_async_copy(atm.at[v, 0], held.at[v], sems.at[v]) for v in range(variables)]
    ends = (pl.ds(0, 8), pl.ds(rows - 8, 8))
    for side in range(2):
        copies.append(pltpu.make_async_copy(atm.at[:, :, ends[side]], atm_ends.at[side], sems.at[variables + side]))
        copies.append(pltpu.make_async_copy(ocean.at[:, :, ends[side]], ocean_ends.at[side], sems.at[variables + 2 + side]))
        copies.append(pltpu.make_async_copy(land.at[ends[side]], land_ends.at[side], sems.at[variables + 4 + side]))
    for i, ref in enumerate(list_refs):
        copies.append(pltpu.make_async_copy(ref, lines.at[i], sems.at[variables + 6 + i]))
    for copy in copies:
        copy.start()
    for v in range(variables):
        copies[v].wait()
        put_columns(held[v], v, halves, first_cols, last_cols)
    wait_all(copies[variables:])
    for side, out in enumerate((first_rows, last_rows)):
        row = slice(0, 1) if side == 0 else slice(7, 8)
        mask = land_ends[side, row, :].astype(F32)
        at = 0
        for v in range(variables):
            for level in range(levels):
                out[at : at + 1, :] = atm_ends[side, v, level, row, :]
                at += 1
        for v in range(variables):
            for level in range(levels):
                out[at : at + 1, :] = ocean_ends[side, v, level, row, :] * mask
                at += 1
        out[at : at + 1, :] = mask
        out[at + 1 :, :] = jnp.zeros((out.shape[0] - at - 1, LANES), F32)
    for i in range(4):
        for h in range(halves):
            line = lines[i, :, h * LANES : (h + 1) * LANES].astype(F32)
            for out, at in ((first_rows, first_rows.shape[0] - 4 * halves), (last_rows, first_rows.shape[0] - 4 * halves), (lists, 0)):
                out[at + i * halves + h : at + i * halves + h + 1, :] = line


def rest_edges_kernel(halves, variables, levels, atm, ocean, land, first_cols, last_cols):
    at = 0
    for v in range(variables):
        for level in range(1, levels):
            put_columns(atm[v, level], at, halves, first_cols, last_cols)
            at += 1
    mask = land[...].astype(F32)
    for v in range(variables):
        for level in range(levels):
            put_columns(ocean[v, level] * mask, at, halves, first_cols, last_cols)
            at += 1
    put_columns(mask, at, halves, first_cols, last_cols)
    used = (at + 1) * halves
    for ref in (first_cols, last_cols):
        if used < ref.shape[0]:
            ref[used:, :] = jnp.zeros((ref.shape[0] - used, LANES), F32)


def atm_step(a, u, v, diffusion, sides):
    n, s, e, w = sides
    laplace = n + s + e + w - 4.0 * a
    advection = u * (e - w) + v * (n - s)
    return a + diffusion * laplace - 0.5 * time_step * advection


def put_split(fields, high_ref, low_ref):
    rows = fields[0].shape[0]
    for i in range(4):
        if i < len(fields):
            high = fields[i].astype(BF16).astype(F32)
            low = fields[i] - high
        else:
            high = low = jnp.zeros((rows, LANES), F32)
        high_ref[pl.ds(i, rows, stride=4), :] = high
        low_ref[pl.ds(i, rows, stride=4), :] = low


def weight_copies(weight, held, sems):
    part = held.shape[0] // CHUNKS
    for c in range(CHUNKS):
        rows = pl.ds(c * part, part)
        yield pltpu.make_async_copy(weight.at[rows], held.at[rows], sems.at[c])


def start_weights(weight, held, sems):
    for copy in weight_copies(weight, held, sems):
        copy.start()


def wait_weights(weight, held, sems):
    for copy in weight_copies(weight, held, sems):
        copy.wait()


def product_rows(slots, weight, high_ref, low_ref, placed, channels, first=0):
    step = weight.shape[0] if weight.shape[0] <= STEP else math.gcd(weight.shape[0], STEP)

    def some(c, carry):
        for i in range(0, step, 2):
            own = c * step + i
            r = first + own
            at = pl.ds(pl.multiple_of(r * 4, 8), 8)
            left = jnp.concatenate([high_ref[at, :].astype(BF16), low_ref[at, :].astype(BF16)], axis=0)
            right = jnp.concatenate([weight[own], weight[own + 1]], axis=1)
            both = jnp.dot(left, right, preferred_element_type=F32)
            both = both[:8] + both[8:]
            placed[pl.ds(slots[0, r] * channels, channels), :] = both[:channels, :LANES]
            placed[pl.ds(slots[0, r + 1] * channels, channels), :] = both[4 : 4 + channels, LANES:]
        return carry

    lax.fori_loop(0, weight.shape[0] // step, some, 0)


def joined(rows, i, halves):
    return jnp.concatenate([rows[i * halves + h : i * halves + h + 1, :] for h in range(halves)], axis=1)


def slot_row(destination, capacity):
    rows = destination.shape[1]
    wide = jnp.broadcast_to(destination, (8, rows))
    column_of = jnp.concatenate([jnp.transpose(wide[:, i : i + LANES]) for i in range(0, rows, LANES)], axis=0)[:, 0:1]
    j = lax.broadcasted_iota(jnp.int32, (rows, rows), 0)
    i = lax.broadcasted_iota(jnp.int32, (rows, rows), 1)
    earlier = (column_of == wide[0:1, :]) & (j < i)
    rank = jnp.sum(jnp.where(earlier, 1.0, 0.0), axis=0, keepdims=True)
    return (destination * float(capacity) + rank).astype(jnp.int32)


def prepare_kernel(capacity, lists, weight, held, flux_slots, surface_slots, sems):
    start_weights(weight, held, sems)
    halves = lists.shape[0] // 4
    flux_slots[...] = slot_row(joined(lists, 0, halves), capacity)
    surface_slots[...] = slot_row(joined(lists, 2, halves), capacity)
    wait_weights(weight, held, sems)


def copies_of(source, target, sems, first):
    part = source.shape[0] // PARTS
    copies = []
    for c in range(PARTS):
        rows = pl.ds(c * part, part)
        copies.append(pltpu.make_async_copy(source.at[rows], target.at[rows], sems.at[first + c]))
        copies[-1].start()
    return copies


def wait_all(copies):
    for copy in copies:
        copy.wait()


def flux_kernel(halves, levels, slots_in, atm, diffusion, surface, north, south, east, west, weight, next_ref, sent, slots, high_ref, low_ref, made, sems, placed):
    read = pltpu.make_async_copy(slots_in, slots, sems.at[0])
    read.start()
    placed[...] = jnp.zeros(placed.shape, F32)
    east_turned, west_turned = jnp.transpose(east[...]), jnp.transpose(west[...])
    u, v, coef = atm[0], atm[1], diffusion[...]
    norths, souths = cleared(north, south)
    after = []
    for i in range(4):
        row = slice(i * levels, i * levels + 1)
        sides = neighbours(
            atm[i], norths[row, :], souths[row, :], column(east_turned, i, halves), column(west_turned, i, halves)
        )
        after.append(atm_step(atm[i], u, v, coef, sides))
        made[i] = after[i]
    writes = copies_of(made, next_ref.at[:, 0], sems, 1)
    du, dv = after[0] - surface[1], after[1] - surface[2]
    speed = jnp.sqrt(1.0 + du * du + dv * dv)
    sst, humidity = surface[0], after[3]
    moisture = moisture_coef * speed * (sst - humidity) - rain_coef * humidity * humidity
    put_split(
        [heat_coef * speed * (after[2] - sst), moisture, drag_coef * speed * du, drag_coef * speed * dv],
        high_ref,
        low_ref,
    )
    read.wait()
    product_rows(slots, weight, high_ref, low_ref, placed, 4)
    wait_all(writes + copies_of(placed, sent, sems, 1 + PARTS))


def atm_rest_kernel(halves, levels, atm, diffusion, north, south, east, west, started, out, made, sems):
    coef = diffusion[...]
    te, tw = jnp.transpose(east[...]), jnp.transpose(west[...])
    norths, souths = cleared(north, south)
    writes = []
    for level in range(1, levels):
        u, v = atm[0, level], atm[1, level]
        for i in range(4):
            at = i * (levels - 1) + level - 1
            row = slice(i * levels + level, i * levels + level + 1)
            a = atm[i, level]
            sides = neighbours(a, norths[row, :], souths[row, :], column(te, at, halves), column(tw, at, halves))
            made[at] = atm_step(a, u, v, coef, sides)
            writes.append(pltpu.make_async_copy(made.at[at], out.at[i, level], sems.at[at]))
            writes[-1].start()
    wait_all(writes)


def ocean_kernel(halves, base, levels, ocean, land, north, south, east, west, out, made, sems):
    mask = land[...].astype(F32)
    te, tw = jnp.transpose(east[...]), jnp.transpose(west[...])
    norths, souths = cleared(north, south)
    row, at = slice(8 * levels, 8 * levels + 1), base + 4 * levels
    n, s, e, w = neighbours(mask, norths[row, :], souths[row, :], column(te, at, halves), column(tw, at, halves))
    count = n + s + e + w
    writes = []
    for var in range(4):
        for level in range(levels):
            place = var * levels + level
            at = base + place
            row = slice(4 * levels + place, 4 * levels + place + 1)
            o = ocean[var, level]
            n, s, e, w = neighbours(
                o * mask, norths[row, :], souths[row, :], column(te, at, halves), column(tw, at, halves)
            )
            lateral = n + s + e + w - count * o
            vertical = ocean[var, max(level - 1, 0)] + ocean[var, min(level + 1, levels - 1)] - 2.0 * o
            made[place] = mask * (o + ocean_diffusion * lateral + vertical_mixing * vertical)
            writes.append(pltpu.make_async_copy(made.at[place], out.at[var, level], sems.at[place]))
            writes[-1].start()
    wait_all(writes)


def far_lists(lists):
    size = lax.axis_size("comp")
    return [lax.ppermute(lists, "comp", [(i, (i - q) % size) for i in range(size)]) for q in range(2, size - 1)]


def lists_along_comp(lists, north, south, far):
    first = north.shape[0] - lists.shape[0]
    return jnp.stack([lists, north[first:], *far, south[first:]])


def lists_along_lon(held):
    size, bit, pieces = lax.axis_size("lon"), 1, [held]
    while bit < size:
        pieces.append(lax.ppermute(held, "lon", [(i, i ^ bit) for i in range(size)]))
        held, bit = jnp.concatenate([held, pieces[-1]], axis=0), 2 * bit
    return pieces


def arrivals_kernel(devices, capacity, *refs):
    *pieces, weight, early, first, second, all_ref, sorted_ref, sem = refs
    read = pltpu.make_async_copy(weight.at[pl.ds(0, early.shape[0])], early, sem)
    read.start()
    halves = pieces[0].shape[1] // 4
    rows = halves * LANES
    comp, lon = lax.axis_size("comp"), lax.axis_size("lon")
    my_comp, my_lon = lax.axis_index("comp"), lax.axis_index("lon")
    me = (my_comp * lon + my_lon).astype(F32)
    place = 0
    for piece in pieces:
        all_ref[place : place + piece.shape[0]] = piece[...]
        place += piece.shape[0]
    for s in range(devices):
        block = all_ref[lax.rem(s // lon - my_comp + comp, comp) + (my_lon ^ (s % lon)) * comp]
        for i in range(4):
            sorted_ref[i, s : s + 1, :] = joined(block, i, halves)
    j = lax.broadcasted_iota(jnp.int32, (rows, rows), 0)
    i = lax.broadcasted_iota(jnp.int32, (rows, rows), 1)
    before = jnp.where(j < i, 1.0, 0.0).astype(BF16)
    for which, out in enumerate((first, second)):
        named = sorted_ref[2 * which] == me
        target = sorted_ref[2 * which + 1]
        rank = jnp.dot(jnp.where(named, 1.0, 0.0).astype(BF16), before, preferred_element_type=F32)
        row = jnp.where(named, target + 1.0, 0.0)
        parts = [jnp.where(rank == float(k), row, 0.0) for k in range(capacity)]
        table = jnp.concatenate(parts, axis=0).astype(BF16)
        total = lax.dot_general(
            jnp.ones((8, rows), BF16), table, (((1,), (1,)), ((), ())), preferred_element_type=F32
        )
        wanted = lax.broadcasted_iota(jnp.int32, out.shape, 0).astype(F32) + 1.0
        out[...] = jnp.where(wanted == total[0:1, :], 1.0, 0.0).astype(BF16)
    read.wait()


def summed_channel(devices, capacity, arrived, chosen, channels, i):
    parts = [arrived[pl.ds(k * channels + i, devices, stride=capacity * channels), :] for k in range(capacity)]
    x = jnp.concatenate(parts, axis=0)
    high = x.astype(BF16)
    low = (x - high.astype(F32)).astype(BF16)
    total = jnp.dot(chosen[...], jnp.concatenate([high, low], axis=1), preferred_element_type=F32)
    return total[:, :LANES] + total[:, LANES:]


def forced_kernel(devices, capacity, slots_in, arrived, target, land, base, weight, early, after_this, next_ref, placed, slots, high_ref, low_ref, made, sems, chosen, held, weight_sems, land_held):
    chosen_read = pltpu.make_async_copy(target, chosen, sems.at[1 + 2 * PARTS])
    chosen_read.start()
    reads = copies_of(base.at[:, 0], made, sems, 1)
    reads += copies_of(land, land_held, sems, 1 + PARTS)
    slots_read = pltpu.make_async_copy(slots_in, slots, sems.at[0])
    slots_read.start()
    size = held.shape[0] // LATE
    for late in range(LATE):
        source = weight.at[pl.ds(early.shape[0] + late * size, size)]
        pltpu.make_async_copy(source, held.at[pl.ds(late * size, size)], weight_sems.at[late]).start()
    placed[...] = jnp.zeros(placed.shape, F32)
    chosen_read.wait()
    forcing = [summed_channel(devices, capacity, arrived, chosen, 4, i) for i in range(4)]
    wait_all(reads)
    mask = land_held[...].astype(F32)
    after = []
    for i in range(4):
        after.append(made[i] + mask * (forcing_gain * forcing[i]))
        made[i] = after[i]
    writes = copies_of(made, next_ref.at[:, 0], sems, 1)
    put_split([after[0], after[2], after[3]], high_ref, low_ref)
    slots_read.wait()
    product_rows(slots, early, high_ref, low_ref, placed, 3)
    first = early.shape[0]
    for late in range(LATE):
        size = held.shape[0] // LATE
        part = pl.ds(late * size, size)
        pltpu.make_async_copy(weight.at[pl.ds(first + late * size, size)], held.at[part], weight_sems.at[late]).wait()
        product_rows(slots, held.at[part], high_ref, low_ref, placed, 3, first + late * size)
    wait_all(writes)


def surface_kernel(devices, capacity, arrived, chosen, out, made, sems):
    writes = []
    for i in range(3):
        made[i] = summed_channel(devices, capacity, arrived, chosen, 3, i)
        writes.append(pltpu.make_async_copy(made.at[i], out.at[i], sems.at[i]))
        writes[i].start()
    wait_all(writes)


def whole(x):
    return pl.BlockSpec(x.shape, lambda *_: (0,) * len(x.shape))


def level_zero(x):
    return pl.BlockSpec((x.shape[0], 1) + x.shape[2:], lambda *_: (0, 0, 0, 0))


ANY = pl.BlockSpec(memory_space=pl.ANY)


def in_hbm(x):
    return pltpu.with_memory_space_constraint(x, pltpu.HBM)


def in_vmem(x):
    return pltpu.with_memory_space_constraint(x, pltpu.VMEM)


def body(
    atm_state, ocean_state, surface_state, atm_diffusion, land_sea, flux_dest, flux_row, flux_weight, surface_dest,
    surface_row, surface_weight,
):
    variables, levels, rows, cols = atm_state.shape
    devices = lax.axis_size("comp") * lax.axis_size("lon")
    capacity = max(2, 2 * rows // devices)
    width = devices * capacity
    halves = rows // LANES
    f32 = functools.partial(jax.ShapeDtypeStruct, dtype=F32)
    top = f32((variables, rows, cols))
    line = jax.ShapeDtypeStruct((1, rows), jnp.int32)
    all_rows = f32((-(-(2 * variables * levels + 1 + 4 * halves) // 8) * 8, cols))
    top_cols, own_lists = f32((variables * halves, cols)), f32((4 * halves, cols))
    made = [top, all_rows, all_rows, top_cols, top_cols, own_lists]
    atm_top, first_rows, last_rows, first_cols, last_cols, lists = pl.pallas_call(
        functools.partial(edges_kernel, halves, variables, levels, rows),
        grid=(1,),
        in_specs=[ANY] * 7,
        out_specs=[whole(e) for e in made],
        out_shape=made,
        scratch_shapes=[
            pltpu.VMEM((2, variables, levels, 8, cols), F32),
            pltpu.VMEM((2, variables, levels, 8, cols), F32),
            pltpu.VMEM((2, 8, cols), jnp.int32),
            pltpu.VMEM((4, 1, rows), jnp.int32),
            pltpu.SemaphoreType.DMA((variables + 10,)),
        ],
        compiler_params=params(),
        cost_estimate=cost(8),
        name="edges",
    )(
        *(in_hbm(x) for x in (atm_state, ocean_state, land_sea)),
        *(in_hbm(x.reshape(1, rows)) for x in (flux_dest, flux_row, surface_dest, surface_row)),
    )
    north, south = exchange_rows(first_rows, last_rows)
    sides = (north, south, *exchange_columns(first_cols, last_cols))
    far = far_lists(lists)
    in_memory = pl.BlockSpec(memory_space=pltpu.VMEM)
    held, flux_slots, surface_slots = pl.pallas_call(
        functools.partial(prepare_kernel, capacity),
        grid=(1,),
        in_specs=[whole(lists), ANY],
        out_specs=[in_memory, whole(line), whole(line)],
        out_shape=[pltpu.VMEM(flux_weight.shape, BF16)] + [pltpu.HBM(line.shape, jnp.int32)] * 2,
        scratch_shapes=[pltpu.SemaphoreType.DMA((CHUNKS,))],
        compiler_params=params(),
        cost_estimate=cost(4),
        name="prepare",
    )(lists, in_hbm(flux_weight))

    far, flux_slots = lax.optimization_barrier((far, flux_slots))

    work = [
        pltpu.SMEM((1, rows), jnp.int32),
        pltpu.VMEM((rows * 4, cols), F32),
        pltpu.VMEM((rows * 4, cols), F32),
        pltpu.VMEM(top.shape, F32),
        pltpu.SemaphoreType.DMA((2 + 2 * PARTS,)),
    ]
    atm_started, sent = pl.pallas_call(
        functools.partial(flux_kernel, halves, levels),
        grid=(1,),
        in_specs=[ANY]
        + [whole(e) for e in (atm_top, atm_diffusion, surface_state, *sides)]
        + [in_memory],
        out_specs=[ANY, ANY],
        scratch_shapes=[*work, pltpu.VMEM((width * 4, cols), F32)],
        out_shape=[f32(atm_state.shape), pltpu.HBM((width * 4, cols), F32)],
        compiler_params=params(),
        cost_estimate=cost(5),
        name="fluxes",
    )(in_hbm(flux_slots), atm_top, atm_diffusion, surface_state, *sides, in_vmem(held))
    arrived = lax.all_to_all(
        sent.reshape(devices, capacity * 4, cols), AXES, split_axis=0, concat_axis=0, tiled=True
    ).reshape(width * 4, cols)

    along_comp = lists_along_comp(lists, north, south, far)
    along_comp, land, _ = lax.optimization_barrier((along_comp, land_sea, sent))
    pieces = lists_along_lon(along_comp)
    count = variables * (levels - 1) + variables * levels + 1
    padded = -(-count // 8) * 8
    rest_cols = f32((padded * halves, cols))
    rest = pl.pallas_call(
        functools.partial(rest_edges_kernel, halves, variables, levels),
        grid=(1,),
        in_specs=[whole(atm_state), whole(ocean_state), whole(land_sea)],
        out_specs=[whole(rest_cols)] * 2,
        out_shape=[rest_cols, rest_cols],
        compiler_params=params(),
        cost_estimate=cost(8),
        name="rest_edges",
    )(atm_state, ocean_state, land)
    rest = (north, south, *exchange_columns(*rest))
    base = variables * (levels - 1)
    atm_next = pl.pallas_call(
        functools.partial(atm_rest_kernel, halves, levels),
        grid=(1,),
        in_specs=[whole(atm_state), whole(atm_diffusion)] + [whole(e) for e in rest] + [ANY],
        out_specs=ANY,
        out_shape=f32(atm_state.shape),
        scratch_shapes=[pltpu.VMEM((base, rows, cols), F32), pltpu.SemaphoreType.DMA((base,))],
        input_output_aliases={6: 0},
        compiler_params=params(),
        cost_estimate=cost(4),
        name="atm_rest",
    )(atm_state, atm_diffusion, *rest, atm_started)
    fields = variables * levels
    ocean_base = pl.pallas_call(
        functools.partial(ocean_kernel, halves, base, levels),
        grid=(1,),
        in_specs=[whole(ocean_state), whole(land_sea)] + [whole(e) for e in rest],
        out_specs=ANY,
        out_shape=pltpu.HBM(ocean_state.shape, F32),
        scratch_shapes=[pltpu.VMEM((fields, rows, cols), F32), pltpu.SemaphoreType.DMA((fields,))],
        compiler_params=params(),
        cost_estimate=cost(5),
        name="ocean_base",
    )(ocean_state, land_sea, *rest)
    target = jax.ShapeDtypeStruct((rows, width), BF16)
    early, flux_target, surface_target = pl.pallas_call(
        functools.partial(arrivals_kernel, devices, capacity),
        grid=(1,),
        in_specs=[whole(piece) for piece in pieces] + [ANY],
        out_specs=[in_memory, whole(target), whole(target)],
        scratch_shapes=[pltpu.VMEM((devices, 4 * halves, cols), F32), pltpu.VMEM((4, devices, rows), F32), pltpu.SemaphoreType.DMA(())],
        out_shape=[pltpu.VMEM((rows // CHUNKS * EARLY, cols, cols), BF16), pltpu.HBM(target.shape, BF16), target],
        compiler_params=params(),
        cost_estimate=cost(1),
        name="arrivals",
    )(*pieces, in_hbm(surface_weight))

    back_shape = f32((width * 3, cols))
    ocean_next, back = pl.pallas_call(
        functools.partial(forced_kernel, devices, capacity),
        grid=(1,),
        in_specs=[ANY, whole(arrived), ANY, ANY, ANY, ANY, in_memory, ANY],
        out_specs=[ANY, whole(back_shape)],
        scratch_shapes=[
            *work,
            pltpu.VMEM(target.shape, BF16),
            pltpu.VMEM((rows - rows // CHUNKS * EARLY, cols, cols), BF16),
            pltpu.SemaphoreType.DMA((LATE,)),
            pltpu.VMEM((rows, cols), jnp.int32),
        ],
        out_shape=[f32(ocean_state.shape), back_shape],
        input_output_aliases={4: 0},
        compiler_params=params(),
        cost_estimate=cost(5),
        name="forced",
    )(in_hbm(surface_slots), arrived, in_hbm(flux_target), in_hbm(land_sea), ocean_base, in_hbm(surface_weight), in_vmem(early), in_hbm(atm_next))
    returned = lax.all_to_all(
        back.reshape(devices, capacity * 3, cols), AXES, split_axis=0, concat_axis=0, tiled=True
    ).reshape(width * 3, cols)

    surface_next = pl.pallas_call(
        functools.partial(surface_kernel, devices, capacity),
        grid=(1,),
        in_specs=[whole(returned), whole(surface_target)],
        out_specs=ANY,
        out_shape=f32(surface_state.shape),
        scratch_shapes=[pltpu.VMEM(surface_state.shape, F32), pltpu.SemaphoreType.DMA((3,))],
        compiler_params=params(),
        cost_estimate=cost(1),
        name="surface",
    )(returned, surface_target)
    return (atm_next, ocean_next, surface_next)


def solution(mesh):
    in_specs = (
        P(None, None, "comp", "lon"),
        P(None, None, "comp", "lon"),
        P(None, "comp", "lon"),
        P("comp", "lon"),
        P("comp", "lon"),
        P(("comp", "lon"), None),
        P(("comp", "lon")),
        P(("comp", "lon"), None, None),
        P(("comp", "lon"), None),
        P(("comp", "lon")),
        P(("comp", "lon"), None, None),
    )
    out_specs = (P(None, None, "comp", "lon"), P(None, None, "comp", "lon"), P(None, "comp", "lon"))
    return jax.shard_map(body, mesh=mesh, in_specs=in_specs, out_specs=out_specs, check_vma=False)
```

```python
import functools
import math

import jax
import jax.numpy as jnp
from jax import lax
from jax.experimental import pallas as pl
from jax.experimental.pallas import tpu as pltpu
from jax.sharding import PartitionSpec as P

time_step = 0.1
ocean_diffusion = 0.2
vertical_mixing = 0.2
drag_coef = 0.4
heat_coef = 0.5
moisture_coef = 0.3
rain_coef = 0.2
forcing_gain = 0.5

AXES = ("comp", "lon")
LANES = 128
CHUNKS = 8
EARLY = 2
STEP = 128
LATE = 3
PARTS = 4
F32 = jnp.float32
BF16 = jnp.bfloat16
VMEM_LIMIT = 24 << 20


def cost(microseconds):
    return pl.CostEstimate(flops=int(microseconds * 1e9), bytes_accessed=1 << 20, transcendentals=0)


def params(**kw):
    return pltpu.CompilerParams(vmem_limit_bytes=VMEM_LIMIT, **kw)


def swap(x, axis, close):
    size = lax.axis_size(axis)
    pairs = [(i, i + 1 if i % 2 == 0 else i - 1) for i in range(size)]
    if not close:
        pairs = [(i, (i - 1 if i % 2 == 0 else i + 1) % size) for i in range(size)]
    return lax.ppermute(x, axis, pairs)


def exchange(close, other, axis):
    return swap(close, axis, True), swap(other, axis, False)


def is_even(axis):
    return lax.rem(lax.axis_index(axis), 2) == 0


def chosen_edges(first, last, axis):
    even = is_even(axis)
    return jnp.where(even, last, first), jnp.where(even, first, last)


def ahead_and_behind(close, other, axis):
    even = is_even(axis)
    return jnp.where(even, close[...], other[...]), jnp.where(even, other[...], close[...])


def inside():
    at = lax.axis_index("comp")
    return at < lax.axis_size("comp") - 1, at > 0


def edge_rows(close, other):
    north, south = ahead_and_behind(close, other, "comp")
    has_north, has_south = inside()
    return jnp.where(has_north, north, 0.0), jnp.where(has_south, south, 0.0)


def edge_columns(close, other):
    east, west = ahead_and_behind(close, other, "lon")
    return jnp.transpose(east), jnp.transpose(west)


def put_columns(field, at, halves, first_cols, last_cols):
    for h in range(halves):
        turned = jnp.transpose(field[h * LANES : (h + 1) * LANES, :])
        row = at * halves + h
        first_cols[row : row + 1, :] = turned[0:1, :]
        last_cols[row : row + 1, :] = turned[LANES - 1 : LANES, :]


def neighbours(x, north, south, east, west):
    rows, cols = x.shape
    row = lax.broadcasted_iota(jnp.int32, x.shape, 0)
    col = lax.broadcasted_iota(jnp.int32, x.shape, 1)
    n = jnp.where(row == rows - 1, north, pltpu.roll(x, rows - 1, 0))
    s = jnp.where(row == 0, south, pltpu.roll(x, 1, 0))
    e = jnp.where(col == cols - 1, east, pltpu.roll(x, cols - 1, 1))
    w = jnp.where(col == 0, west, pltpu.roll(x, 1, 1))
    return n, s, e, w


def column(turned, at, halves):
    parts = [turned[:, at * halves + h : at * halves + h + 1] for h in range(halves)]
    return jnp.concatenate(parts, axis=0)


def edges_kernel(halves, variables, levels, rows, atm, ocean, land, *refs):
    list_refs = refs[:4]
    held, close_rows, other_rows, close_cols, other_cols, lists, ends_rows, ends_cols, atm_ends, ocean_ends, land_ends, lines, sems = refs[4:]
    first_rows, last_rows = ends_rows.at[0], ends_rows.at[1]
    copies = [pltpu.make_async_copy(atm.at[v, 0], held.at[v], sems.at[v]) for v in range(variables)]
    ends = (pl.ds(0, 8), pl.ds(rows - 8, 8))
    for side in range(2):
        copies.append(pltpu.make_async_copy(atm.at[:, :, ends[side]], atm_ends.at[side], sems.at[variables + side]))
        copies.append(pltpu.make_async_copy(ocean.at[:, :, ends[side]], ocean_ends.at[side], sems.at[variables + 2 + side]))
        copies.append(pltpu.make_async_copy(land.at[ends[side]], land_ends.at[side], sems.at[variables + 4 + side]))
    for i, ref in enumerate(list_refs):
        copies.append(pltpu.make_async_copy(ref, lines.at[i], sems.at[variables + 6 + i]))
    for copy in copies:
        copy.start()
    for v in range(variables):
        copies[v].wait()
        put_columns(held[v], v, halves, ends_cols.at[0], ends_cols.at[1])
    close_cols[...], other_cols[...] = chosen_edges(ends_cols[0], ends_cols[1], "lon")
    wait_all(copies[variables:])
    for side, out in enumerate((first_rows, last_rows)):
        row = slice(0, 1) if side == 0 else slice(7, 8)
        mask = land_ends[side, row, :].astype(F32)
        at = 0
        for v in range(variables):
            for level in range(levels):
                out[at : at + 1, :] = atm_ends[side, v, level, row, :]
                at += 1
        for v in range(variables):
            for level in range(levels):
                out[at : at + 1, :] = ocean_ends[side, v, level, row, :] * mask
                at += 1
        out[at : at + 1, :] = mask
        out[at + 1 :, :] = jnp.zeros((out.shape[0] - at - 1, LANES), F32)
    for i in range(4):
        for h in range(halves):
            line = lines[i, :, h * LANES : (h + 1) * LANES].astype(F32)
            for out, at in ((first_rows, first_rows.shape[0] - 4 * halves), (last_rows, first_rows.shape[0] - 4 * halves), (lists, 0)):
                out[at + i * halves + h : at + i * halves + h + 1, :] = line
    close_rows[...], other_rows[...] = chosen_edges(ends_rows[0], ends_rows[1], "comp")


def rest_edges_kernel(halves, variables, levels, atm, ocean, land, close_cols, other_cols, ends):
    first_cols, last_cols = ends.at[0], ends.at[1]
    at = 0
    for v in range(variables):
        for level in range(1, levels):
            put_columns(atm[v, level], at, halves, first_cols, last_cols)
            at += 1
    mask = land[...].astype(F32)
    for v in range(variables):
        for level in range(levels):
            put_columns(ocean[v, level] * mask, at, halves, first_cols, last_cols)
            at += 1
    put_columns(mask, at, halves, first_cols, last_cols)
    used = (at + 1) * halves
    for ref in (first_cols, last_cols):
        if used < ref.shape[0]:
            ref[used:, :] = jnp.zeros((ref.shape[0] - used, LANES), F32)
    close_cols[...], other_cols[...] = chosen_edges(ends[0], ends[1], "lon")


def atm_step(a, u, v, diffusion, sides):
    n, s, e, w = sides
    laplace = n + s + e + w - 4.0 * a
    advection = u * (e - w) + v * (n - s)
    return a + diffusion * laplace - 0.5 * time_step * advection


def put_split(fields, high_ref, low_ref):
    rows = fields[0].shape[0]
    for i in range(4):
        if i < len(fields):
            high = fields[i].astype(BF16).astype(F32)
            low = fields[i] - high
        else:
            high = low = jnp.zeros((rows, LANES), F32)
        high_ref[pl.ds(i, rows, stride=4), :] = high
        low_ref[pl.ds(i, rows, stride=4), :] = low


def weight_copies(weight, held, sems):
    part = held.shape[0] // CHUNKS
    for c in range(CHUNKS):
        rows = pl.ds(c * part, part)
        yield pltpu.make_async_copy(weight.at[rows], held.at[rows], sems.at[c])


def start_weights(weight, held, sems):
    for copy in weight_copies(weight, held, sems):
        copy.start()


def wait_weights(weight, held, sems):
    for copy in weight_copies(weight, held, sems):
        copy.wait()


def product_rows(slots, weight, high_ref, low_ref, placed, channels, first=0):
    step = weight.shape[0] if weight.shape[0] <= STEP else math.gcd(weight.shape[0], STEP)

    def some(c, carry):
        for i in range(0, step, 2):
            own = c * step + i
            r = first + own
            at = pl.ds(pl.multiple_of(r * 4, 8), 8)
            left = jnp.concatenate([high_ref[at, :].astype(BF16), low_ref[at, :].astype(BF16)], axis=0)
            right = jnp.concatenate([weight[own], weight[own + 1]], axis=1)
            both = jnp.dot(left, right, preferred_element_type=F32)
            both = both[:8] + both[8:]
            placed[pl.ds(slots[0, r] * channels, channels), :] = both[:channels, :LANES]
            placed[pl.ds(slots[0, r + 1] * channels, channels), :] = both[4 : 4 + channels, LANES:]
        return carry

    lax.fori_loop(0, weight.shape[0] // step, some, 0)


def joined(rows, i, halves):
    return jnp.concatenate([rows[i * halves + h : i * halves + h + 1, :] for h in range(halves)], axis=1)


def slot_row(destination, capacity):
    rows = destination.shape[1]
    wide = jnp.broadcast_to(destination, (8, rows))
    column_of = jnp.concatenate([jnp.transpose(wide[:, i : i + LANES]) for i in range(0, rows, LANES)], axis=0)[:, 0:1]
    j = lax.broadcasted_iota(jnp.int32, (rows, rows), 0)
    i = lax.broadcasted_iota(jnp.int32, (rows, rows), 1)
    earlier = (column_of == wide[0:1, :]) & (j < i)
    rank = jnp.sum(jnp.where(earlier, 1.0, 0.0), axis=0, keepdims=True)
    return (destination * float(capacity) + rank).astype(jnp.int32)


def prepare_kernel(capacity, lists, weight, held, flux_slots, surface_slots, sems):
    start_weights(weight, held, sems)
    halves = lists.shape[0] // 4
    flux_slots[...] = slot_row(joined(lists, 0, halves), capacity)
    surface_slots[...] = slot_row(joined(lists, 2, halves), capacity)
    wait_weights(weight, held, sems)


def copies_of(source, target, sems, first):
    part = source.shape[0] // PARTS
    copies = []
    for c in range(PARTS):
        rows = pl.ds(c * part, part)
        copies.append(pltpu.make_async_copy(source.at[rows], target.at[rows], sems.at[first + c]))
        copies[-1].start()
    return copies


def wait_all(copies):
    for copy in copies:
        copy.wait()


def flux_kernel(halves, levels, slots_in, atm, diffusion, surface, close_rows, other_rows, close_cols, other_cols, weight, next_ref, sent, slots, high_ref, low_ref, made, sems, placed):
    read = pltpu.make_async_copy(slots_in, slots, sems.at[0])
    read.start()
    placed[...] = jnp.zeros(placed.shape, F32)
    east_turned, west_turned = edge_columns(close_cols, other_cols)
    u, v, coef = atm[0], atm[1], diffusion[...]
    norths, souths = edge_rows(close_rows, other_rows)
    after = []
    for i in range(4):
        row = slice(i * levels, i * levels + 1)
        sides = neighbours(
            atm[i], norths[row, :], souths[row, :], column(east_turned, i, halves), column(west_turned, i, halves)
        )
        after.append(atm_step(atm[i], u, v, coef, sides))
        made[i] = after[i]
    writes = copies_of(made, next_ref.at[:, 0], sems, 1)
    du, dv = after[0] - surface[1], after[1] - surface[2]
    speed = jnp.sqrt(1.0 + du * du + dv * dv)
    sst, humidity = surface[0], after[3]
    moisture = moisture_coef * speed * (sst - humidity) - rain_coef * humidity * humidity
    put_split(
        [heat_coef * speed * (after[2] - sst), moisture, drag_coef * speed * du, drag_coef * speed * dv],
        high_ref,
        low_ref,
    )
    read.wait()
    product_rows(slots, weight, high_ref, low_ref, placed, 4)
    wait_all(writes + copies_of(placed, sent, sems, 1 + PARTS))


def atm_rest_kernel(halves, levels, atm, diffusion, close_rows, other_rows, close_cols, other_cols, started, out, made, sems):
    coef = diffusion[...]
    te, tw = edge_columns(close_cols, other_cols)
    norths, souths = edge_rows(close_rows, other_rows)
    writes = []
    for level in range(1, levels):
        u, v = atm[0, level], atm[1, level]
        for i in range(4):
            at = i * (levels - 1) + level - 1
            row = slice(i * levels + level, i * levels + level + 1)
            a = atm[i, level]
            sides = neighbours(a, norths[row, :], souths[row, :], column(te, at, halves), column(tw, at, halves))
            made[at] = atm_step(a, u, v, coef, sides)
            writes.append(pltpu.make_async_copy(made.at[at], out.at[i, level], sems.at[at]))
            writes[-1].start()
    wait_all(writes)


def ocean_kernel(halves, base, levels, ocean, land, close_rows, other_rows, close_cols, other_cols, out, made, sems):
    mask = land[...].astype(F32)
    te, tw = edge_columns(close_cols, other_cols)
    norths, souths = edge_rows(close_rows, other_rows)
    row, at = slice(8 * levels, 8 * levels + 1), base + 4 * levels
    n, s, e, w = neighbours(mask, norths[row, :], souths[row, :], column(te, at, halves), column(tw, at, halves))
    count = n + s + e + w
    writes = []
    for var in range(4):
        for level in range(levels):
            place = var * levels + level
            at = base + place
            row = slice(4 * levels + place, 4 * levels + place + 1)
            o = ocean[var, level]
            n, s, e, w = neighbours(
                o * mask, norths[row, :], souths[row, :], column(te, at, halves), column(tw, at, halves)
            )
            lateral = n + s + e + w - count * o
            vertical = ocean[var, max(level - 1, 0)] + ocean[var, min(level + 1, levels - 1)] - 2.0 * o
            made[place] = mask * (o + ocean_diffusion * lateral + vertical_mixing * vertical)
            writes.append(pltpu.make_async_copy(made.at[place], out.at[var, level], sems.at[place]))
            writes[-1].start()
    wait_all(writes)


def far_lists(lists):
    size = lax.axis_size("comp")
    return [lax.ppermute(lists, "comp", [(i, (i - q) % size) for i in range(size)]) for q in range(2, size - 1)]


def lists_along_comp(lists, close, other, far):
    first = close.shape[0] - lists.shape[0]
    return jnp.stack([lists, close[first:], *far, other[first:]])


def lists_along_lon(held):
    size, bit, pieces = lax.axis_size("lon"), 1, [held]
    while bit < size:
        pieces.append(lax.ppermute(held, "lon", [(i, i ^ bit) for i in range(size)]))
        held, bit = jnp.concatenate([held, pieces[-1]], axis=0), 2 * bit
    return pieces


def arrivals_kernel(devices, capacity, *refs):
    *pieces, weight, early, first, second, all_ref, sorted_ref, sem = refs
    read = pltpu.make_async_copy(weight.at[pl.ds(0, early.shape[0])], early, sem)
    read.start()
    halves = pieces[0].shape[1] // 4
    rows = halves * LANES
    comp, lon = lax.axis_size("comp"), lax.axis_size("lon")
    my_comp, my_lon = lax.axis_index("comp"), lax.axis_index("lon")
    me = (my_comp * lon + my_lon).astype(F32)
    place = 0
    for piece in pieces:
        all_ref[place : place + piece.shape[0]] = piece[...]
        place += piece.shape[0]
    for s in range(devices):
        along = lax.rem(s // lon - my_comp + comp, comp)
        beside = (along == 1) | (along == comp - 1)
        along = jnp.where(beside & ~is_even("comp"), comp - along, along)
        block = all_ref[along + (my_lon ^ (s % lon)) * comp]
        for i in range(4):
            sorted_ref[i, s : s + 1, :] = joined(block, i, halves)
    j = lax.broadcasted_iota(jnp.int32, (rows, rows), 0)
    i = lax.broadcasted_iota(jnp.int32, (rows, rows), 1)
    before = jnp.where(j < i, 1.0, 0.0).astype(BF16)
    for which, out in enumerate((first, second)):
        named = sorted_ref[2 * which] == me
        target = sorted_ref[2 * which + 1]
        rank = jnp.dot(jnp.where(named, 1.0, 0.0).astype(BF16), before, preferred_element_type=F32)
        row = jnp.where(named, target + 1.0, 0.0)
        parts = [jnp.where(rank == float(k), row, 0.0) for k in range(capacity)]
        table = jnp.concatenate(parts, axis=0).astype(BF16)
        total = lax.dot_general(
            jnp.ones((8, rows), BF16), table, (((1,), (1,)), ((), ())), preferred_element_type=F32
        )
        wanted = lax.broadcasted_iota(jnp.int32, out.shape, 0).astype(F32) + 1.0
        out[...] = jnp.where(wanted == total[0:1, :], 1.0, 0.0).astype(BF16)
    read.wait()


def summed_channel(devices, capacity, arrived, chosen, channels, i):
    parts = [arrived[pl.ds(k * channels + i, devices, stride=capacity * channels), :] for k in range(capacity)]
    x = jnp.concatenate(parts, axis=0)
    high = x.astype(BF16)
    low = (x - high.astype(F32)).astype(BF16)
    total = jnp.dot(chosen[...], jnp.concatenate([high, low], axis=1), preferred_element_type=F32)
    return total[:, :LANES] + total[:, LANES:]


def forced_kernel(devices, capacity, slots_in, arrived, target, land, base, weight, early, after_this, next_ref, placed, slots, high_ref, low_ref, made, sems, chosen, held, weight_sems, land_held):
    chosen_read = pltpu.make_async_copy(target, chosen, sems.at[1 + 2 * PARTS])
    chosen_read.start()
    reads = copies_of(base.at[:, 0], made, sems, 1)
    reads += copies_of(land, land_held, sems, 1 + PARTS)
    slots_read = pltpu.make_async_copy(slots_in, slots, sems.at[0])
    slots_read.start()
    size = held.shape[0] // LATE
    for late in range(LATE):
        source = weight.at[pl.ds(early.shape[0] + late * size, size)]
        pltpu.make_async_copy(source, held.at[pl.ds(late * size, size)], weight_sems.at[late]).start()
    placed[...] = jnp.zeros(placed.shape, F32)
    chosen_read.wait()
    forcing = [summed_channel(devices, capacity, arrived, chosen, 4, i) for i in range(4)]
    wait_all(reads)
    mask = land_held[...].astype(F32)
    after = []
    for i in range(4):
        after.append(made[i] + mask * (forcing_gain * forcing[i]))
        made[i] = after[i]
    writes = copies_of(made, next_ref.at[:, 0], sems, 1)
    put_split([after[0], after[2], after[3]], high_ref, low_ref)
    slots_read.wait()
    product_rows(slots, early, high_ref, low_ref, placed, 3)
    first = early.shape[0]
    for late in range(LATE):
        size = held.shape[0] // LATE
        part = pl.ds(late * size, size)
        pltpu.make_async_copy(weight.at[pl.ds(first + late * size, size)], held.at[part], weight_sems.at[late]).wait()
        product_rows(slots, held.at[part], high_ref, low_ref, placed, 3, first + late * size)
    wait_all(writes)


def surface_kernel(devices, capacity, arrived, chosen, out, made, sems):
    writes = []
    for i in range(3):
        made[i] = summed_channel(devices, capacity, arrived, chosen, 3, i)
        writes.append(pltpu.make_async_copy(made.at[i], out.at[i], sems.at[i]))
        writes[i].start()
    wait_all(writes)


def whole(x):
    return pl.BlockSpec(x.shape, lambda *_: (0,) * len(x.shape))


def level_zero(x):
    return pl.BlockSpec((x.shape[0], 1) + x.shape[2:], lambda *_: (0, 0, 0, 0))


ANY = pl.BlockSpec(memory_space=pl.ANY)


def in_hbm(x):
    return pltpu.with_memory_space_constraint(x, pltpu.HBM)


def in_vmem(x):
    return pltpu.with_memory_space_constraint(x, pltpu.VMEM)


def body(
    atm_state, ocean_state, surface_state, atm_diffusion, land_sea, flux_dest, flux_row, flux_weight, surface_dest,
    surface_row, surface_weight,
):
    variables, levels, rows, cols = atm_state.shape
    devices = lax.axis_size("comp") * lax.axis_size("lon")
    capacity = max(2, 2 * rows // devices)
    width = devices * capacity
    halves = rows // LANES
    f32 = functools.partial(jax.ShapeDtypeStruct, dtype=F32)
    top = f32((variables, rows, cols))
    line = jax.ShapeDtypeStruct((1, rows), jnp.int32)
    all_rows = f32((-(-(2 * variables * levels + 1 + 4 * halves) // 8) * 8, cols))
    top_cols, own_lists = f32((variables * halves, cols)), f32((4 * halves, cols))
    made = [top, all_rows, all_rows, top_cols, top_cols, own_lists]
    atm_top, close_rows, other_rows, close_cols, other_cols, lists = pl.pallas_call(
        functools.partial(edges_kernel, halves, variables, levels, rows),
        grid=(1,),
        in_specs=[ANY] * 7,
        out_specs=[whole(e) for e in made],
        out_shape=made,
        scratch_shapes=[
            pltpu.VMEM((2, *all_rows.shape), F32),
            pltpu.VMEM((2, *top_cols.shape), F32),
            pltpu.VMEM((2, variables, levels, 8, cols), F32),
            pltpu.VMEM((2, variables, levels, 8, cols), F32),
            pltpu.VMEM((2, 8, cols), jnp.int32),
            pltpu.VMEM((4, 1, rows), jnp.int32),
            pltpu.SemaphoreType.DMA((variables + 10,)),
        ],
        compiler_params=params(),
        cost_estimate=cost(8),
        name="edges",
    )(
        *(in_hbm(x) for x in (atm_state, ocean_state, land_sea)),
        *(in_hbm(x.reshape(1, rows)) for x in (flux_dest, flux_row, surface_dest, surface_row)),
    )
    row_sides = exchange(close_rows, other_rows, "comp")
    sides = (*row_sides, *exchange(close_cols, other_cols, "lon"))
    far = far_lists(lists)
    in_memory = pl.BlockSpec(memory_space=pltpu.VMEM)
    held, flux_slots, surface_slots = pl.pallas_call(
        functools.partial(prepare_kernel, capacity),
        grid=(1,),
        in_specs=[whole(lists), ANY],
        out_specs=[in_memory, whole(line), whole(line)],
        out_shape=[pltpu.VMEM(flux_weight.shape, BF16)] + [pltpu.HBM(line.shape, jnp.int32)] * 2,
        scratch_shapes=[pltpu.SemaphoreType.DMA((CHUNKS,))],
        compiler_params=params(),
        cost_estimate=cost(4),
        name="prepare",
    )(lists, in_hbm(flux_weight))

    far, flux_slots = lax.optimization_barrier((far, flux_slots))

    work = [
        pltpu.SMEM((1, rows), jnp.int32),
        pltpu.VMEM((rows * 4, cols), F32),
        pltpu.VMEM((rows * 4, cols), F32),
        pltpu.VMEM(top.shape, F32),
        pltpu.SemaphoreType.DMA((2 + 2 * PARTS,)),
    ]
    atm_started, sent = pl.pallas_call(
        functools.partial(flux_kernel, halves, levels),
        grid=(1,),
        in_specs=[ANY]
        + [whole(e) for e in (atm_top, atm_diffusion, surface_state, *sides)]
        + [in_memory],
        out_specs=[ANY, ANY],
        scratch_shapes=[*work, pltpu.VMEM((width * 4, cols), F32)],
        out_shape=[f32(atm_state.shape), pltpu.HBM((width * 4, cols), F32)],
        compiler_params=params(),
        cost_estimate=cost(5),
        name="fluxes",
    )(in_hbm(flux_slots), atm_top, atm_diffusion, surface_state, *sides, in_vmem(held))
    arrived = lax.all_to_all(
        sent.reshape(devices, capacity * 4, cols), AXES, split_axis=0, concat_axis=0, tiled=True
    ).reshape(width * 4, cols)

    along_comp = lists_along_comp(lists, *row_sides, far)
    along_comp, land, _ = lax.optimization_barrier((along_comp, land_sea, sent))
    pieces = lists_along_lon(along_comp)
    count = variables * (levels - 1) + variables * levels + 1
    padded = -(-count // 8) * 8
    rest_cols = f32((padded * halves, cols))
    rest = pl.pallas_call(
        functools.partial(rest_edges_kernel, halves, variables, levels),
        grid=(1,),
        in_specs=[whole(atm_state), whole(ocean_state), whole(land_sea)],
        out_specs=[whole(rest_cols)] * 2,
        out_shape=[rest_cols, rest_cols],
        scratch_shapes=[pltpu.VMEM((2, *rest_cols.shape), F32)],
        compiler_params=params(),
        cost_estimate=cost(8),
        name="rest_edges",
    )(atm_state, ocean_state, land)
    rest = (*row_sides, *exchange(*rest, "lon"))
    base = variables * (levels - 1)
    atm_next = pl.pallas_call(
        functools.partial(atm_rest_kernel, halves, levels),
        grid=(1,),
        in_specs=[whole(atm_state), whole(atm_diffusion)] + [whole(e) for e in rest] + [ANY],
        out_specs=ANY,
        out_shape=f32(atm_state.shape),
        scratch_shapes=[pltpu.VMEM((base, rows, cols), F32), pltpu.SemaphoreType.DMA((base,))],
        input_output_aliases={6: 0},
        compiler_params=params(),
        cost_estimate=cost(4),
        name="atm_rest",
    )(atm_state, atm_diffusion, *rest, atm_started)
    fields = variables * levels
    ocean_base = pl.pallas_call(
        functools.partial(ocean_kernel, halves, base, levels),
        grid=(1,),
        in_specs=[whole(ocean_state), whole(land_sea)] + [whole(e) for e in rest],
        out_specs=ANY,
        out_shape=pltpu.HBM(ocean_state.shape, F32),
        scratch_shapes=[pltpu.VMEM((fields, rows, cols), F32), pltpu.SemaphoreType.DMA((fields,))],
        compiler_params=params(),
        cost_estimate=cost(5),
        name="ocean_base",
    )(ocean_state, land_sea, *rest)
    target = jax.ShapeDtypeStruct((rows, width), BF16)
    early, flux_target, surface_target = pl.pallas_call(
        functools.partial(arrivals_kernel, devices, capacity),
        grid=(1,),
        in_specs=[whole(piece) for piece in pieces] + [ANY],
        out_specs=[in_memory, whole(target), whole(target)],
        scratch_shapes=[pltpu.VMEM((devices, 4 * halves, cols), F32), pltpu.VMEM((4, devices, rows), F32), pltpu.SemaphoreType.DMA(())],
        out_shape=[pltpu.VMEM((rows // CHUNKS * EARLY, cols, cols), BF16), pltpu.HBM(target.shape, BF16), target],
        compiler_params=params(),
        cost_estimate=cost(1),
        name="arrivals",
    )(*pieces, in_hbm(surface_weight))

    back_shape = f32((width * 3, cols))
    ocean_next, back = pl.pallas_call(
        functools.partial(forced_kernel, devices, capacity),
        grid=(1,),
        in_specs=[ANY, whole(arrived), ANY, ANY, ANY, ANY, in_memory, ANY],
        out_specs=[ANY, whole(back_shape)],
        scratch_shapes=[
            *work,
            pltpu.VMEM(target.shape, BF16),
            pltpu.VMEM((rows - rows // CHUNKS * EARLY, cols, cols), BF16),
            pltpu.SemaphoreType.DMA((LATE,)),
            pltpu.VMEM((rows, cols), jnp.int32),
        ],
        out_shape=[f32(ocean_state.shape), back_shape],
        input_output_aliases={4: 0},
        compiler_params=params(),
        cost_estimate=cost(5),
        name="forced",
    )(in_hbm(surface_slots), arrived, in_hbm(flux_target), in_hbm(land_sea), ocean_base, in_hbm(surface_weight), in_vmem(early), in_hbm(atm_next))
    returned = lax.all_to_all(
        back.reshape(devices, capacity * 3, cols), AXES, split_axis=0, concat_axis=0, tiled=True
    ).reshape(width * 3, cols)

    surface_next = pl.pallas_call(
        functools.partial(surface_kernel, devices, capacity),
        grid=(1,),
        in_specs=[whole(returned), whole(surface_target)],
        out_specs=ANY,
        out_shape=f32(surface_state.shape),
        scratch_shapes=[pltpu.VMEM(surface_state.shape, F32), pltpu.SemaphoreType.DMA((3,))],
        compiler_params=params(),
        cost_estimate=cost(1),
        name="surface",
    )(returned, surface_target)
    return (atm_next, ocean_next, surface_next)


def solution(mesh):
    in_specs = (
        P(None, None, "comp", "lon"),
        P(None, None, "comp", "lon"),
        P(None, "comp", "lon"),
        P("comp", "lon"),
        P("comp", "lon"),
        P(("comp", "lon"), None),
        P(("comp", "lon")),
        P(("comp", "lon"), None, None),
        P(("comp", "lon"), None),
        P(("comp", "lon")),
        P(("comp", "lon"), None, None),
    )
    out_specs = (P(None, None, "comp", "lon"), P(None, None, "comp", "lon"), P(None, "comp", "lon"))
    return jax.shard_map(body, mesh=mesh, in_specs=in_specs, out_specs=out_specs, check_vma=False)
```

```python
import functools
import math

import jax
import jax.numpy as jnp
from jax import lax
from jax.experimental import pallas as pl
from jax.experimental.pallas import tpu as pltpu
from jax.sharding import PartitionSpec as P

time_step = 0.1
ocean_diffusion = 0.2
vertical_mixing = 0.2
drag_coef = 0.4
heat_coef = 0.5
moisture_coef = 0.3
rain_coef = 0.2
forcing_gain = 0.5

AXES = ("comp", "lon")
LANES = 128
CHUNKS = 8
EARLY = 2
STEP = 128
LATE = 3
PARTS = 4
F32 = jnp.float32
BF16 = jnp.bfloat16
VMEM_LIMIT = 24 << 20


def cost(microseconds):
    return pl.CostEstimate(flops=int(microseconds * 1e9), bytes_accessed=1 << 20, transcendentals=0)


def params(**kw):
    return pltpu.CompilerParams(vmem_limit_bytes=VMEM_LIMIT, **kw)


def swap(x, axis, close):
    size = lax.axis_size(axis)
    pairs = [(i, i + 1 if i % 2 == 0 else i - 1) for i in range(size)]
    if not close:
        pairs = [(i, (i - 1 if i % 2 == 0 else i + 1) % size) for i in range(size)]
    return lax.ppermute(x, axis, pairs)


def exchange(close, other, axis):
    return swap(close, axis, True), swap(other, axis, False)


def is_even(axis):
    return lax.rem(lax.axis_index(axis), 2) == 0


def chosen_edges(first, last, axis):
    even = is_even(axis)
    return jnp.where(even, last, first), jnp.where(even, first, last)


def ahead_and_behind(close, other, axis):
    even = is_even(axis)
    return jnp.where(even, close[...], other[...]), jnp.where(even, other[...], close[...])


def inside():
    at = lax.axis_index("comp")
    return at < lax.axis_size("comp") - 1, at > 0


def edge_rows(close, other):
    north, south = ahead_and_behind(close, other, "comp")
    has_north, has_south = inside()
    return jnp.where(has_north, north, 0.0), jnp.where(has_south, south, 0.0)


def edge_columns(close, other):
    east, west = ahead_and_behind(close, other, "lon")
    return jnp.transpose(east), jnp.transpose(west)


def put_columns(field, at, halves, first_cols, last_cols):
    for h in range(halves):
        turned = jnp.transpose(field[h * LANES : (h + 1) * LANES, :])
        row = at * halves + h
        first_cols[row : row + 1, :] = turned[0:1, :]
        last_cols[row : row + 1, :] = turned[LANES - 1 : LANES, :]


def neighbours(x, north, south, east, west):
    rows, cols = x.shape
    row = lax.broadcasted_iota(jnp.int32, x.shape, 0)
    col = lax.broadcasted_iota(jnp.int32, x.shape, 1)
    n = jnp.where(row == rows - 1, north, pltpu.roll(x, rows - 1, 0))
    s = jnp.where(row == 0, south, pltpu.roll(x, 1, 0))
    e = jnp.where(col == cols - 1, east, pltpu.roll(x, cols - 1, 1))
    w = jnp.where(col == 0, west, pltpu.roll(x, 1, 1))
    return n, s, e, w


def column(turned, at, halves):
    parts = [turned[:, at * halves + h : at * halves + h + 1] for h in range(halves)]
    return jnp.concatenate(parts, axis=0)


def edges_kernel(halves, variables, levels, rows, atm, ocean, land, *refs):
    list_refs = refs[:4]
    held, close_rows, other_rows, close_cols, other_cols, lists, ends_rows, ends_cols, atm_ends, ocean_ends, land_ends, lines, sems = refs[4:]
    first_rows, last_rows = ends_rows.at[0], ends_rows.at[1]
    copies = [pltpu.make_async_copy(atm.at[v, 0], held.at[v], sems.at[v]) for v in range(variables)]
    ends = (pl.ds(0, 8), pl.ds(rows - 8, 8))
    for side in range(2):
        copies.append(pltpu.make_async_copy(atm.at[:, :, ends[side]], atm_ends.at[side], sems.at[variables + side]))
        copies.append(pltpu.make_async_copy(ocean.at[:, :, ends[side]], ocean_ends.at[side], sems.at[variables + 2 + side]))
        copies.append(pltpu.make_async_copy(land.at[ends[side]], land_ends.at[side], sems.at[variables + 4 + side]))
    for i, ref in enumerate(list_refs):
        copies.append(pltpu.make_async_copy(ref, lines.at[i], sems.at[variables + 6 + i]))
    for copy in copies:
        copy.start()
    for v in range(variables):
        copies[v].wait()
        put_columns(held[v], v, halves, ends_cols.at[0], ends_cols.at[1])
    close_cols[...], other_cols[...] = chosen_edges(ends_cols[0], ends_cols[1], "lon")
    wait_all(copies[variables:])
    for side, out in enumerate((first_rows, last_rows)):
        row = slice(0, 1) if side == 0 else slice(7, 8)
        mask = land_ends[side, row, :].astype(F32)
        at = 0
        for v in range(variables):
            for level in range(levels):
                out[at : at + 1, :] = atm_ends[side, v, level, row, :]
                at += 1
        for v in range(variables):
            for level in range(levels):
                out[at : at + 1, :] = ocean_ends[side, v, level, row, :] * mask
                at += 1
        out[at : at + 1, :] = mask
        out[at + 1 :, :] = jnp.zeros((out.shape[0] - at - 1, LANES), F32)
    for i in range(4):
        for h in range(halves):
            line = lines[i, :, h * LANES : (h + 1) * LANES].astype(F32)
            for out, at in ((first_rows, first_rows.shape[0] - 4 * halves), (last_rows, first_rows.shape[0] - 4 * halves), (lists, 0)):
                out[at + i * halves + h : at + i * halves + h + 1, :] = line
    close_rows[...], other_rows[...] = chosen_edges(ends_rows[0], ends_rows[1], "comp")


def rest_edges_kernel(halves, variables, levels, atm, ocean, land, close_cols, other_cols, ends):
    first_cols, last_cols = ends.at[0], ends.at[1]
    at = 0
    for v in range(variables):
        for level in range(1, levels):
            put_columns(atm[v, level], at, halves, first_cols, last_cols)
            at += 1
    mask = land[...].astype(F32)
    for v in range(variables):
        for level in range(levels):
            put_columns(ocean[v, level] * mask, at, halves, first_cols, last_cols)
            at += 1
    put_columns(mask, at, halves, first_cols, last_cols)
    used = (at + 1) * halves
    for ref in (first_cols, last_cols):
        if used < ref.shape[0]:
            ref[used:, :] = jnp.zeros((ref.shape[0] - used, LANES), F32)
    close_cols[...], other_cols[...] = chosen_edges(ends[0], ends[1], "lon")


def atm_step(a, u, v, diffusion, sides):
    n, s, e, w = sides
    laplace = n + s + e + w - 4.0 * a
    advection = u * (e - w) + v * (n - s)
    return a + diffusion * laplace - 0.5 * time_step * advection


def put_split(fields, high_ref, low_ref):
    rows = fields[0].shape[0]
    for i in range(4):
        if i < len(fields):
            high = fields[i].astype(BF16).astype(F32)
            low = fields[i] - high
        else:
            high = low = jnp.zeros((rows, LANES), F32)
        high_ref[pl.ds(i, rows, stride=4), :] = high
        low_ref[pl.ds(i, rows, stride=4), :] = low


def weight_copies(weight, held, sems):
    part = held.shape[0] // CHUNKS
    for c in range(CHUNKS):
        rows = pl.ds(c * part, part)
        yield pltpu.make_async_copy(weight.at[rows], held.at[rows], sems.at[c])


def start_weights(weight, held, sems):
    for copy in weight_copies(weight, held, sems):
        copy.start()


def wait_weights(weight, held, sems):
    for copy in weight_copies(weight, held, sems):
        copy.wait()


def product_rows(slots, weight, high_ref, low_ref, placed, channels, first=0):
    step = weight.shape[0] if weight.shape[0] <= STEP else math.gcd(weight.shape[0], STEP)

    def some(c, carry):
        for i in range(0, step, 2):
            own = c * step + i
            r = first + own
            at = pl.ds(pl.multiple_of(r * 4, 8), 8)
            left = jnp.concatenate([high_ref[at, :].astype(BF16), low_ref[at, :].astype(BF16)], axis=0)
            right = jnp.concatenate([weight[own], weight[own + 1]], axis=1)
            both = jnp.dot(left, right, preferred_element_type=F32)
            both = both[:8] + both[8:]
            placed[pl.ds(slots[0, r] * channels, channels), :] = both[:channels, :LANES]
            placed[pl.ds(slots[0, r + 1] * channels, channels), :] = both[4 : 4 + channels, LANES:]
        return carry

    lax.fori_loop(0, weight.shape[0] // step, some, 0)


def joined(rows, i, halves):
    return jnp.concatenate([rows[i * halves + h : i * halves + h + 1, :] for h in range(halves)], axis=1)


def slot_row(destination, capacity):
    rows = destination.shape[1]
    wide = jnp.broadcast_to(destination, (8, rows))
    column_of = jnp.concatenate([jnp.transpose(wide[:, i : i + LANES]) for i in range(0, rows, LANES)], axis=0)[:, 0:1]
    j = lax.broadcasted_iota(jnp.int32, (rows, rows), 0)
    i = lax.broadcasted_iota(jnp.int32, (rows, rows), 1)
    earlier = (column_of == wide[0:1, :]) & (j < i)
    rank = jnp.sum(jnp.where(earlier, 1.0, 0.0), axis=0, keepdims=True)
    return (destination * float(capacity) + rank).astype(jnp.int32)


def prepare_kernel(capacity, lists, weight, held, flux_slots, surface_slots, sems):
    start_weights(weight, held, sems)
    halves = lists.shape[0] // 4
    flux_slots[...] = slot_row(joined(lists, 0, halves), capacity)
    surface_slots[...] = slot_row(joined(lists, 2, halves), capacity)
    wait_weights(weight, held, sems)


def copies_of(source, target, sems, first):
    part = source.shape[0] // PARTS
    copies = []
    for c in range(PARTS):
        rows = pl.ds(c * part, part)
        copies.append(pltpu.make_async_copy(source.at[rows], target.at[rows], sems.at[first + c]))
        copies[-1].start()
    return copies


def wait_all(copies):
    for copy in copies:
        copy.wait()


def flux_kernel(halves, levels, slots_in, atm, diffusion, surface, close_rows, other_rows, close_cols, other_cols, weight, next_ref, sent, slots, high_ref, low_ref, made, sems, placed):
    read = pltpu.make_async_copy(slots_in, slots, sems.at[0])
    read.start()
    placed[...] = jnp.zeros(placed.shape, F32)
    east_turned, west_turned = edge_columns(close_cols, other_cols)
    u, v, coef = atm[0], atm[1], diffusion[...]
    norths, souths = edge_rows(close_rows, other_rows)
    after = []
    for i in range(4):
        row = slice(i * levels, i * levels + 1)
        sides = neighbours(
            atm[i], norths[row, :], souths[row, :], column(east_turned, i, halves), column(west_turned, i, halves)
        )
        after.append(atm_step(atm[i], u, v, coef, sides))
        made[i] = after[i]
    writes = copies_of(made, next_ref.at[:, 0], sems, 1)
    du, dv = after[0] - surface[1], after[1] - surface[2]
    speed = jnp.sqrt(1.0 + du * du + dv * dv)
    sst, humidity = surface[0], after[3]
    moisture = moisture_coef * speed * (sst - humidity) - rain_coef * humidity * humidity
    put_split(
        [heat_coef * speed * (after[2] - sst), moisture, drag_coef * speed * du, drag_coef * speed * dv],
        high_ref,
        low_ref,
    )
    read.wait()
    product_rows(slots, weight, high_ref, low_ref, placed, 4)
    wait_all(writes + copies_of(placed, sent, sems, 1 + PARTS))


def atm_rest_kernel(halves, levels, atm, diffusion, close_rows, other_rows, close_cols, other_cols, started, out, made, sems):
    coef = diffusion[...]
    te, tw = edge_columns(close_cols, other_cols)
    norths, souths = edge_rows(close_rows, other_rows)
    writes = []
    for level in range(1, levels):
        u, v = atm[0, level], atm[1, level]
        for i in range(4):
            at = i * (levels - 1) + level - 1
            row = slice(i * levels + level, i * levels + level + 1)
            a = atm[i, level]
            sides = neighbours(a, norths[row, :], souths[row, :], column(te, at, halves), column(tw, at, halves))
            made[at] = atm_step(a, u, v, coef, sides)
            writes.append(pltpu.make_async_copy(made.at[at], out.at[i, level], sems.at[at]))
            writes[-1].start()
    wait_all(writes)


def ocean_kernel(halves, base, levels, ocean, land, close_rows, other_rows, close_cols, other_cols, out, made, sems):
    mask = land[...].astype(F32)
    te, tw = edge_columns(close_cols, other_cols)
    norths, souths = edge_rows(close_rows, other_rows)
    row, at = slice(8 * levels, 8 * levels + 1), base + 4 * levels
    n, s, e, w = neighbours(mask, norths[row, :], souths[row, :], column(te, at, halves), column(tw, at, halves))
    count = n + s + e + w
    writes = []
    for var in range(4):
        for level in range(levels):
            place = var * levels + level
            at = base + place
            row = slice(4 * levels + place, 4 * levels + place + 1)
            o = ocean[var, level]
            n, s, e, w = neighbours(
                o * mask, norths[row, :], souths[row, :], column(te, at, halves), column(tw, at, halves)
            )
            lateral = n + s + e + w - count * o
            vertical = ocean[var, max(level - 1, 0)] + ocean[var, min(level + 1, levels - 1)] - 2.0 * o
            made[place] = mask * (o + ocean_diffusion * lateral + vertical_mixing * vertical)
            writes.append(pltpu.make_async_copy(made.at[place], out.at[var, level], sems.at[place]))
            writes[-1].start()
    wait_all(writes)


def far_lists(lists):
    size = lax.axis_size("comp")
    return [lax.ppermute(lists, "comp", [(i, (i - q) % size) for i in range(size)]) for q in range(2, size - 1)]


def lists_along_comp(lists, close, other, far):
    first = close.shape[0] - lists.shape[0]
    return jnp.stack([lists, close[first:], *far, other[first:]])


def lists_along_lon(held):
    size, bit, pieces = lax.axis_size("lon"), 1, [held]
    while bit < size:
        pieces.append(lax.ppermute(held, "lon", [(i, i ^ bit) for i in range(size)]))
        held, bit = jnp.concatenate([held, pieces[-1]], axis=0), 2 * bit
    return pieces


def arrivals_kernel(devices, capacity, *refs):
    *pieces, weight, early, first, second, all_ref, sorted_ref, sem = refs
    read = pltpu.make_async_copy(weight.at[pl.ds(0, early.shape[0])], early, sem)
    read.start()
    halves = pieces[0].shape[1] // 4
    rows = halves * LANES
    comp, lon = lax.axis_size("comp"), lax.axis_size("lon")
    my_comp, my_lon = lax.axis_index("comp"), lax.axis_index("lon")
    me = (my_comp * lon + my_lon).astype(F32)
    place = 0
    for piece in pieces:
        all_ref[place : place + piece.shape[0]] = piece[...]
        place += piece.shape[0]
    for s in range(devices):
        along = lax.rem(s // lon - my_comp + comp, comp)
        beside = (along == 1) | (along == comp - 1)
        along = jnp.where(beside & ~is_even("comp"), comp - along, along)
        block = all_ref[along + (my_lon ^ (s % lon)) * comp]
        for i in range(4):
            sorted_ref[i, s : s + 1, :] = joined(block, i, halves)
    j = lax.broadcasted_iota(jnp.int32, (rows, rows), 0)
    i = lax.broadcasted_iota(jnp.int32, (rows, rows), 1)
    before = jnp.where(j < i, 1.0, 0.0).astype(BF16)
    for which, out in enumerate((first, second)):
        named = sorted_ref[2 * which] == me
        target = sorted_ref[2 * which + 1]
        rank = jnp.dot(jnp.where(named, 1.0, 0.0).astype(BF16), before, preferred_element_type=F32)
        row = jnp.where(named, target + 1.0, 0.0)
        parts = [jnp.where(rank == float(k), row, 0.0) for k in range(capacity)]
        table = jnp.concatenate(parts, axis=0).astype(BF16)
        total = lax.dot_general(
            jnp.ones((8, rows), BF16), table, (((1,), (1,)), ((), ())), preferred_element_type=F32
        )
        wanted = lax.broadcasted_iota(jnp.int32, out.shape, 0).astype(F32) + 1.0
        out[...] = jnp.where(wanted == total[0:1, :], 1.0, 0.0).astype(BF16)
    read.wait()


def summed_channel(devices, capacity, arrived, chosen, channels, i):
    parts = [arrived[pl.ds(k * channels + i, devices, stride=capacity * channels), :] for k in range(capacity)]
    x = jnp.concatenate(parts, axis=0)
    high = x.astype(BF16)
    low = (x - high.astype(F32)).astype(BF16)
    total = jnp.dot(chosen[...], jnp.concatenate([high, low], axis=1), preferred_element_type=F32)
    return total[:, :LANES] + total[:, LANES:]


def forced_kernel(devices, capacity, slots_in, arrived, target, land, base, weight, early, after_this, next_ref, placed, slots, high_ref, low_ref, made, sems, chosen, held, weight_sems, land_held):
    chosen_read = pltpu.make_async_copy(target, chosen, sems.at[1 + 2 * PARTS])
    chosen_read.start()
    reads = copies_of(base.at[:, 0], made, sems, 1)
    reads += copies_of(land, land_held, sems, 1 + PARTS)
    slots_read = pltpu.make_async_copy(slots_in, slots, sems.at[0])
    slots_read.start()
    size = held.shape[0] // LATE
    for late in range(LATE):
        source = weight.at[pl.ds(early.shape[0] + late * size, size)]
        pltpu.make_async_copy(source, held.at[pl.ds(late * size, size)], weight_sems.at[late]).start()
    placed[...] = jnp.zeros(placed.shape, F32)
    chosen_read.wait()
    forcing = [summed_channel(devices, capacity, arrived, chosen, 4, i) for i in range(4)]
    wait_all(reads)
    mask = land_held[...].astype(F32)
    after = []
    for i in range(4):
        after.append(made[i] + mask * (forcing_gain * forcing[i]))
        made[i] = after[i]
    writes = copies_of(made, next_ref.at[:, 0], sems, 1)
    put_split([after[0], after[2], after[3]], high_ref, low_ref)
    slots_read.wait()
    product_rows(slots, early, high_ref, low_ref, placed, 3)
    first = early.shape[0]
    for late in range(LATE):
        size = held.shape[0] // LATE
        part = pl.ds(late * size, size)
        pltpu.make_async_copy(weight.at[pl.ds(first + late * size, size)], held.at[part], weight_sems.at[late]).wait()
        product_rows(slots, held.at[part], high_ref, low_ref, placed, 3, first + late * size)
    wait_all(writes)


def surface_kernel(devices, capacity, arrived, chosen, out, made, sems):
    writes = []
    for i in range(3):
        made[i] = summed_channel(devices, capacity, arrived, chosen, 3, i)
        writes.append(pltpu.make_async_copy(made.at[i], out.at[i], sems.at[i]))
        writes[i].start()
    wait_all(writes)


def whole(x):
    return pl.BlockSpec(x.shape, lambda *_: (0,) * len(x.shape))


def level_zero(x):
    return pl.BlockSpec((x.shape[0], 1) + x.shape[2:], lambda *_: (0, 0, 0, 0))


ANY = pl.BlockSpec(memory_space=pl.ANY)


def in_hbm(x):
    return pltpu.with_memory_space_constraint(x, pltpu.HBM)


def in_vmem(x):
    return pltpu.with_memory_space_constraint(x, pltpu.VMEM)


def body(
    atm_state, ocean_state, surface_state, atm_diffusion, land_sea, flux_dest, flux_row, flux_weight, surface_dest,
    surface_row, surface_weight,
):
    variables, levels, rows, cols = atm_state.shape
    devices = lax.axis_size("comp") * lax.axis_size("lon")
    capacity = max(2, 2 * rows // devices)
    width = devices * capacity
    halves = rows // LANES
    f32 = functools.partial(jax.ShapeDtypeStruct, dtype=F32)
    top = f32((variables, rows, cols))
    line = jax.ShapeDtypeStruct((1, rows), jnp.int32)
    all_rows = f32((-(-(2 * variables * levels + 1 + 4 * halves) // 8) * 8, cols))
    top_cols, own_lists = f32((variables * halves, cols)), f32((4 * halves, cols))
    made = [top, all_rows, all_rows, top_cols, top_cols, own_lists]
    atm_top, close_rows, other_rows, close_cols, other_cols, lists = pl.pallas_call(
        functools.partial(edges_kernel, halves, variables, levels, rows),
        grid=(1,),
        in_specs=[ANY] * 7,
        out_specs=[whole(e) for e in made],
        out_shape=made,
        scratch_shapes=[
            pltpu.VMEM((2, *all_rows.shape), F32),
            pltpu.VMEM((2, *top_cols.shape), F32),
            pltpu.VMEM((2, variables, levels, 8, cols), F32),
            pltpu.VMEM((2, variables, levels, 8, cols), F32),
            pltpu.VMEM((2, 8, cols), jnp.int32),
            pltpu.VMEM((4, 1, rows), jnp.int32),
            pltpu.SemaphoreType.DMA((variables + 10,)),
        ],
        compiler_params=params(),
        cost_estimate=cost(8),
        name="edges",
    )(
        *(in_hbm(x) for x in (atm_state, ocean_state, land_sea)),
        *(in_hbm(x.reshape(1, rows)) for x in (flux_dest, flux_row, surface_dest, surface_row)),
    )
    row_sides = exchange(close_rows, other_rows, "comp")
    sides = (*row_sides, *exchange(close_cols, other_cols, "lon"))
    in_memory = pl.BlockSpec(memory_space=pltpu.VMEM)
    held, flux_slots, surface_slots = pl.pallas_call(
        functools.partial(prepare_kernel, capacity),
        grid=(1,),
        in_specs=[whole(lists), ANY],
        out_specs=[in_memory, whole(line), whole(line)],
        out_shape=[pltpu.VMEM(flux_weight.shape, BF16)] + [pltpu.HBM(line.shape, jnp.int32)] * 2,
        scratch_shapes=[pltpu.SemaphoreType.DMA((CHUNKS,))],
        compiler_params=params(),
        cost_estimate=cost(4),
        name="prepare",
    )(lists, in_hbm(flux_weight))

    far_from, flux_slots = lax.optimization_barrier((lists, flux_slots))
    far = far_lists(far_from)

    work = [
        pltpu.SMEM((1, rows), jnp.int32),
        pltpu.VMEM((rows * 4, cols), F32),
        pltpu.VMEM((rows * 4, cols), F32),
        pltpu.VMEM(top.shape, F32),
        pltpu.SemaphoreType.DMA((2 + 2 * PARTS,)),
    ]
    atm_started, sent = pl.pallas_call(
        functools.partial(flux_kernel, halves, levels),
        grid=(1,),
        in_specs=[ANY]
        + [whole(e) for e in (atm_top, atm_diffusion, surface_state, *sides)]
        + [in_memory],
        out_specs=[ANY, ANY],
        scratch_shapes=[*work, pltpu.VMEM((width * 4, cols), F32)],
        out_shape=[f32(atm_state.shape), pltpu.HBM((width * 4, cols), F32)],
        compiler_params=params(),
        cost_estimate=cost(5),
        name="fluxes",
    )(in_hbm(flux_slots), atm_top, atm_diffusion, surface_state, *sides, in_vmem(held))
    sent, far = lax.optimization_barrier((sent, far))
    arrived = lax.all_to_all(
        sent.reshape(devices, capacity * 4, cols), AXES, split_axis=0, concat_axis=0, tiled=True
    ).reshape(width * 4, cols)

    along_comp = lists_along_comp(lists, *row_sides, far)
    along_comp, land, _ = lax.optimization_barrier((along_comp, land_sea, sent))
    pieces = lists_along_lon(along_comp)
    count = variables * (levels - 1) + variables * levels + 1
    padded = -(-count // 8) * 8
    rest_cols = f32((padded * halves, cols))
    rest = pl.pallas_call(
        functools.partial(rest_edges_kernel, halves, variables, levels),
        grid=(1,),
        in_specs=[whole(atm_state), whole(ocean_state), whole(land_sea)],
        out_specs=[whole(rest_cols)] * 2,
        out_shape=[rest_cols, rest_cols],
        scratch_shapes=[pltpu.VMEM((2, *rest_cols.shape), F32)],
        compiler_params=params(),
        cost_estimate=cost(8),
        name="rest_edges",
    )(atm_state, ocean_state, land)
    rest = (*row_sides, *exchange(*rest, "lon"))
    base = variables * (levels - 1)
    atm_next = pl.pallas_call(
        functools.partial(atm_rest_kernel, halves, levels),
        grid=(1,),
        in_specs=[whole(atm_state), whole(atm_diffusion)] + [whole(e) for e in rest] + [ANY],
        out_specs=ANY,
        out_shape=f32(atm_state.shape),
        scratch_shapes=[pltpu.VMEM((base, rows, cols), F32), pltpu.SemaphoreType.DMA((base,))],
        input_output_aliases={6: 0},
        compiler_params=params(),
        cost_estimate=cost(4),
        name="atm_rest",
    )(atm_state, atm_diffusion, *rest, atm_started)
    fields = variables * levels
    ocean_base = pl.pallas_call(
        functools.partial(ocean_kernel, halves, base, levels),
        grid=(1,),
        in_specs=[whole(ocean_state), whole(land_sea)] + [whole(e) for e in rest],
        out_specs=ANY,
        out_shape=pltpu.HBM(ocean_state.shape, F32),
        scratch_shapes=[pltpu.VMEM((fields, rows, cols), F32), pltpu.SemaphoreType.DMA((fields,))],
        compiler_params=params(),
        cost_estimate=cost(5),
        name="ocean_base",
    )(ocean_state, land_sea, *rest)
    target = jax.ShapeDtypeStruct((rows, width), BF16)
    early, flux_target, surface_target = pl.pallas_call(
        functools.partial(arrivals_kernel, devices, capacity),
        grid=(1,),
        in_specs=[whole(piece) for piece in pieces] + [ANY],
        out_specs=[in_memory, whole(target), whole(target)],
        scratch_shapes=[pltpu.VMEM((devices, 4 * halves, cols), F32), pltpu.VMEM((4, devices, rows), F32), pltpu.SemaphoreType.DMA(())],
        out_shape=[pltpu.VMEM((rows // CHUNKS * EARLY, cols, cols), BF16), pltpu.HBM(target.shape, BF16), target],
        compiler_params=params(),
        cost_estimate=cost(1),
        name="arrivals",
    )(*pieces, in_hbm(surface_weight))

    back_shape = f32((width * 3, cols))
    ocean_next, back = pl.pallas_call(
        functools.partial(forced_kernel, devices, capacity),
        grid=(1,),
        in_specs=[ANY, whole(arrived), ANY, ANY, ANY, ANY, in_memory, ANY],
        out_specs=[ANY, whole(back_shape)],
        scratch_shapes=[
            *work,
            pltpu.VMEM(target.shape, BF16),
            pltpu.VMEM((rows - rows // CHUNKS * EARLY, cols, cols), BF16),
            pltpu.SemaphoreType.DMA((LATE,)),
            pltpu.VMEM((rows, cols), jnp.int32),
        ],
        out_shape=[f32(ocean_state.shape), back_shape],
        input_output_aliases={4: 0},
        compiler_params=params(),
        cost_estimate=cost(5),
        name="forced",
    )(in_hbm(surface_slots), arrived, in_hbm(flux_target), in_hbm(land_sea), ocean_base, in_hbm(surface_weight), in_vmem(early), in_hbm(atm_next))
    returned = lax.all_to_all(
        back.reshape(devices, capacity * 3, cols), AXES, split_axis=0, concat_axis=0, tiled=True
    ).reshape(width * 3, cols)

    surface_next = pl.pallas_call(
        functools.partial(surface_kernel, devices, capacity),
        grid=(1,),
        in_specs=[whole(returned), whole(surface_target)],
        out_specs=ANY,
        out_shape=f32(surface_state.shape),
        scratch_shapes=[pltpu.VMEM(surface_state.shape, F32), pltpu.SemaphoreType.DMA((3,))],
        compiler_params=params(),
        cost_estimate=cost(1),
        name="surface",
    )(returned, surface_target)
    return (atm_next, ocean_next, surface_next)


def solution(mesh):
    in_specs = (
        P(None, None, "comp", "lon"),
        P(None, None, "comp", "lon"),
        P(None, "comp", "lon"),
        P("comp", "lon"),
        P("comp", "lon"),
        P(("comp", "lon"), None),
        P(("comp", "lon")),
        P(("comp", "lon"), None, None),
        P(("comp", "lon"), None),
        P(("comp", "lon")),
        P(("comp", "lon"), None, None),
    )
    out_specs = (P(None, None, "comp", "lon"), P(None, None, "comp", "lon"), P(None, "comp", "lon"))
    return jax.shard_map(body, mesh=mesh, in_specs=in_specs, out_specs=out_specs, check_vma=False)
```

```python
import functools
import math

import jax
import jax.numpy as jnp
from jax import lax
from jax.experimental import pallas as pl
from jax.experimental.pallas import tpu as pltpu
from jax.sharding import PartitionSpec as P

time_step = 0.1
ocean_diffusion = 0.2
vertical_mixing = 0.2
drag_coef = 0.4
heat_coef = 0.5
moisture_coef = 0.3
rain_coef = 0.2
forcing_gain = 0.5

AXES = ("lon", "comp")
LANES = 128
CHUNKS = 8
EARLY = 2
STEP = 128
LATE = 3
PARTS = 4
F32 = jnp.float32
BF16 = jnp.bfloat16
VMEM_LIMIT = 24 << 20


def cost(microseconds):
    return pl.CostEstimate(flops=int(microseconds * 1e9), bytes_accessed=1 << 20, transcendentals=0)


def params(**kw):
    return pltpu.CompilerParams(vmem_limit_bytes=VMEM_LIMIT, **kw)


def swap(x, axis, close):
    size = lax.axis_size(axis)
    pairs = [(i, i + 1 if i % 2 == 0 else i - 1) for i in range(size)]
    if not close:
        pairs = [(i, (i - 1 if i % 2 == 0 else i + 1) % size) for i in range(size)]
    return lax.ppermute(x, axis, pairs)


def exchange(close, other, axis):
    return swap(close, axis, True), swap(other, axis, False)


def is_even(axis):
    return lax.rem(lax.axis_index(axis), 2) == 0


def chosen_edges(first, last, axis):
    even = is_even(axis)
    return jnp.where(even, last, first), jnp.where(even, first, last)


def ahead_and_behind(close, other, axis):
    even = is_even(axis)
    return jnp.where(even, close[...], other[...]), jnp.where(even, other[...], close[...])


def inside():
    at = lax.axis_index("comp")
    return at < lax.axis_size("comp") - 1, at > 0


def edge_rows(close, other):
    north, south = ahead_and_behind(close, other, "comp")
    has_north, has_south = inside()
    return jnp.where(has_north, north, 0.0), jnp.where(has_south, south, 0.0)


def edge_columns(close, other):
    east, west = ahead_and_behind(close, other, "lon")
    return jnp.transpose(east), jnp.transpose(west)


def put_columns(field, at, halves, first_cols, last_cols):
    for h in range(halves):
        turned = jnp.transpose(field[h * LANES : (h + 1) * LANES, :])
        row = at * halves + h
        first_cols[row : row + 1, :] = turned[0:1, :]
        last_cols[row : row + 1, :] = turned[LANES - 1 : LANES, :]


def neighbours(x, north, south, east, west):
    rows, cols = x.shape
    row = lax.broadcasted_iota(jnp.int32, x.shape, 0)
    col = lax.broadcasted_iota(jnp.int32, x.shape, 1)
    n = jnp.where(row == rows - 1, north, pltpu.roll(x, rows - 1, 0))
    s = jnp.where(row == 0, south, pltpu.roll(x, 1, 0))
    e = jnp.where(col == cols - 1, east, pltpu.roll(x, cols - 1, 1))
    w = jnp.where(col == 0, west, pltpu.roll(x, 1, 1))
    return n, s, e, w


def column(turned, at, halves):
    parts = [turned[:, at * halves + h : at * halves + h + 1] for h in range(halves)]
    return jnp.concatenate(parts, axis=0)


def edges_kernel(halves, variables, levels, rows, atm, ocean, land, *refs):
    list_refs = refs[:4]
    held, close_rows, other_rows, close_cols, other_cols, lists, ends_rows, ends_cols, atm_ends, ocean_ends, land_ends, lines, sems = refs[4:]
    first_rows, last_rows = ends_rows.at[0], ends_rows.at[1]
    copies = [pltpu.make_async_copy(atm.at[v, 0], held.at[v], sems.at[v]) for v in range(variables)]
    ends = (pl.ds(0, 8), pl.ds(rows - 8, 8))
    for side in range(2):
        copies.append(pltpu.make_async_copy(atm.at[:, :, ends[side]], atm_ends.at[side], sems.at[variables + side]))
        copies.append(pltpu.make_async_copy(ocean.at[:, :, ends[side]], ocean_ends.at[side], sems.at[variables + 2 + side]))
        copies.append(pltpu.make_async_copy(land.at[ends[side]], land_ends.at[side], sems.at[variables + 4 + side]))
    for i, ref in enumerate(list_refs):
        copies.append(pltpu.make_async_copy(ref, lines.at[i], sems.at[variables + 6 + i]))
    for copy in copies:
        copy.start()
    for v in range(variables):
        copies[v].wait()
        put_columns(held[v], v, halves, ends_cols.at[0], ends_cols.at[1])
    close_cols[...], other_cols[...] = chosen_edges(ends_cols[0], ends_cols[1], "lon")
    wait_all(copies[variables:])
    for side, out in enumerate((first_rows, last_rows)):
        row = slice(0, 1) if side == 0 else slice(7, 8)
        mask = land_ends[side, row, :].astype(F32)
        at = 0
        for v in range(variables):
            for level in range(levels):
                out[at : at + 1, :] = atm_ends[side, v, level, row, :]
                at += 1
        for v in range(variables):
            for level in range(levels):
                out[at : at + 1, :] = ocean_ends[side, v, level, row, :] * mask
                at += 1
        out[at : at + 1, :] = mask
        out[at + 1 :, :] = jnp.zeros((out.shape[0] - at - 1, LANES), F32)
    for i in range(4):
        for h in range(halves):
            line = lines[i, :, h * LANES : (h + 1) * LANES].astype(F32)
            for out, at in ((first_rows, first_rows.shape[0] - 4 * halves), (last_rows, first_rows.shape[0] - 4 * halves), (lists, 0)):
                out[at + i * halves + h : at + i * halves + h + 1, :] = line
    close_rows[...], other_rows[...] = chosen_edges(ends_rows[0], ends_rows[1], "comp")


def rest_edges_kernel(halves, variables, levels, atm, ocean, land, close_cols, other_cols, ends):
    first_cols, last_cols = ends.at[0], ends.at[1]
    at = 0
    for v in range(variables):
        for level in range(1, levels):
            put_columns(atm[v, level], at, halves, first_cols, last_cols)
            at += 1
    mask = land[...].astype(F32)
    for v in range(variables):
        for level in range(levels):
            put_columns(ocean[v, level] * mask, at, halves, first_cols, last_cols)
            at += 1
    put_columns(mask, at, halves, first_cols, last_cols)
    used = (at + 1) * halves
    for ref in (first_cols, last_cols):
        if used < ref.shape[0]:
            ref[used:, :] = jnp.zeros((ref.shape[0] - used, LANES), F32)
    close_cols[...], other_cols[...] = chosen_edges(ends[0], ends[1], "lon")


def atm_step(a, u, v, diffusion, sides):
    n, s, e, w = sides
    laplace = n + s + e + w - 4.0 * a
    advection = u * (e - w) + v * (n - s)
    return a + diffusion * laplace - 0.5 * time_step * advection


def put_split(fields, high_ref, low_ref):
    rows = fields[0].shape[0]
    for i in range(4):
        if i < len(fields):
            high = fields[i].astype(BF16).astype(F32)
            low = fields[i] - high
        else:
            high = low = jnp.zeros((rows, LANES), F32)
        high_ref[pl.ds(i, rows, stride=4), :] = high
        low_ref[pl.ds(i, rows, stride=4), :] = low


def weight_copies(weight, held, sems):
    part = held.shape[0] // CHUNKS
    for c in range(CHUNKS):
        rows = pl.ds(c * part, part)
        yield pltpu.make_async_copy(weight.at[rows], held.at[rows], sems.at[c])


def start_weights(weight, held, sems):
    for copy in weight_copies(weight, held, sems):
        copy.start()


def wait_weights(weight, held, sems):
    for copy in weight_copies(weight, held, sems):
        copy.wait()


def product_rows(slots, weight, high_ref, low_ref, placed, channels, first=0):
    step = weight.shape[0] if weight.shape[0] <= STEP else math.gcd(weight.shape[0], STEP)

    def some(c, carry):
        for i in range(0, step, 2):
            own = c * step + i
            r = first + own
            at = pl.ds(pl.multiple_of(r * 4, 8), 8)
            left = jnp.concatenate([high_ref[at, :].astype(BF16), low_ref[at, :].astype(BF16)], axis=0)
            right = jnp.concatenate([weight[own], weight[own + 1]], axis=1)
            both = jnp.dot(left, right, preferred_element_type=F32)
            both = both[:8] + both[8:]
            placed[pl.ds(slots[0, r] * channels, channels), :] = both[:channels, :LANES]
            placed[pl.ds(slots[0, r + 1] * channels, channels), :] = both[4 : 4 + channels, LANES:]
        return carry

    lax.fori_loop(0, weight.shape[0] // step, some, 0)


def joined(rows, i, halves):
    return jnp.concatenate([rows[i * halves + h : i * halves + h + 1, :] for h in range(halves)], axis=1)


def slot_row(destination, capacity):
    rows = destination.shape[1]
    wide = jnp.broadcast_to(destination, (8, rows))
    column_of = jnp.concatenate([jnp.transpose(wide[:, i : i + LANES]) for i in range(0, rows, LANES)], axis=0)[:, 0:1]
    j = lax.broadcasted_iota(jnp.int32, (rows, rows), 0)
    i = lax.broadcasted_iota(jnp.int32, (rows, rows), 1)
    earlier = (column_of == wide[0:1, :]) & (j < i)
    rank = jnp.sum(jnp.where(earlier, 1.0, 0.0), axis=0, keepdims=True)
    comp, lon = lax.axis_size("comp"), lax.axis_size("lon")
    owner = destination.astype(jnp.int32)
    place = lax.rem(owner, lon) * comp + lax.div(owner, lon)
    return place * capacity + rank.astype(jnp.int32)


def prepare_kernel(capacity, lists, weight, held, flux_slots, surface_slots, sems):
    start_weights(weight, held, sems)
    halves = lists.shape[0] // 4
    flux_slots[...] = slot_row(joined(lists, 0, halves), capacity)
    surface_slots[...] = slot_row(joined(lists, 2, halves), capacity)
    wait_weights(weight, held, sems)


def copies_of(source, target, sems, first):
    part = source.shape[0] // PARTS
    copies = []
    for c in range(PARTS):
        rows = pl.ds(c * part, part)
        copies.append(pltpu.make_async_copy(source.at[rows], target.at[rows], sems.at[first + c]))
        copies[-1].start()
    return copies


def wait_all(copies):
    for copy in copies:
        copy.wait()


def flux_kernel(halves, levels, slots_in, atm, diffusion, surface, close_rows, other_rows, close_cols, other_cols, weight, next_ref, sent, slots, high_ref, low_ref, made, sems, placed):
    read = pltpu.make_async_copy(slots_in, slots, sems.at[0])
    read.start()
    placed[...] = jnp.zeros(placed.shape, F32)
    east_turned, west_turned = edge_columns(close_cols, other_cols)
    u, v, coef = atm[0], atm[1], diffusion[...]
    norths, souths = edge_rows(close_rows, other_rows)
    after = []
    for i in range(4):
        row = slice(i * levels, i * levels + 1)
        sides = neighbours(
            atm[i], norths[row, :], souths[row, :], column(east_turned, i, halves), column(west_turned, i, halves)
        )
        after.append(atm_step(atm[i], u, v, coef, sides))
        made[i] = after[i]
    writes = copies_of(made, next_ref.at[:, 0], sems, 1)
    du, dv = after[0] - surface[1], after[1] - surface[2]
    speed = jnp.sqrt(1.0 + du * du + dv * dv)
    sst, humidity = surface[0], after[3]
    moisture = moisture_coef * speed * (sst - humidity) - rain_coef * humidity * humidity
    put_split(
        [heat_coef * speed * (after[2] - sst), moisture, drag_coef * speed * du, drag_coef * speed * dv],
        high_ref,
        low_ref,
    )
    read.wait()
    product_rows(slots, weight, high_ref, low_ref, placed, 4)
    wait_all(writes + copies_of(placed, sent, sems, 1 + PARTS))


def atm_rest_kernel(halves, levels, atm, diffusion, close_rows, other_rows, close_cols, other_cols, started, out, made, sems):
    coef = diffusion[...]
    te, tw = edge_columns(close_cols, other_cols)
    norths, souths = edge_rows(close_rows, other_rows)
    writes = []
    for level in range(1, levels):
        u, v = atm[0, level], atm[1, level]
        for i in range(4):
            at = i * (levels - 1) + level - 1
            row = slice(i * levels + level, i * levels + level + 1)
            a = atm[i, level]
            sides = neighbours(a, norths[row, :], souths[row, :], column(te, at, halves), column(tw, at, halves))
            made[at] = atm_step(a, u, v, coef, sides)
            writes.append(pltpu.make_async_copy(made.at[at], out.at[i, level], sems.at[at]))
            writes[-1].start()
    wait_all(writes)


def ocean_kernel(halves, base, levels, ocean, land, close_rows, other_rows, close_cols, other_cols, out, made, sems):
    mask = land[...].astype(F32)
    te, tw = edge_columns(close_cols, other_cols)
    norths, souths = edge_rows(close_rows, other_rows)
    row, at = slice(8 * levels, 8 * levels + 1), base + 4 * levels
    n, s, e, w = neighbours(mask, norths[row, :], souths[row, :], column(te, at, halves), column(tw, at, halves))
    count = n + s + e + w
    writes = []
    for var in range(4):
        for level in range(levels):
            place = var * levels + level
            at = base + place
            row = slice(4 * levels + place, 4 * levels + place + 1)
            o = ocean[var, level]
            n, s, e, w = neighbours(
                o * mask, norths[row, :], souths[row, :], column(te, at, halves), column(tw, at, halves)
            )
            lateral = n + s + e + w - count * o
            vertical = ocean[var, max(level - 1, 0)] + ocean[var, min(level + 1, levels - 1)] - 2.0 * o
            made[place] = mask * (o + ocean_diffusion * lateral + vertical_mixing * vertical)
            writes.append(pltpu.make_async_copy(made.at[place], out.at[var, level], sems.at[place]))
            writes[-1].start()
    wait_all(writes)


def far_lists(lists):
    size = lax.axis_size("comp")
    return [lax.ppermute(lists, "comp", [(i, (i - q) % size) for i in range(size)]) for q in range(2, size - 1)]


def lists_along_comp(lists, close, other, far):
    first = close.shape[0] - lists.shape[0]
    return jnp.stack([lists, close[first:], *far, other[first:]])


def lists_along_lon(held):
    size, bit, pieces = lax.axis_size("lon"), 1, [held]
    while bit < size:
        pieces.append(lax.ppermute(held, "lon", [(i, i ^ bit) for i in range(size)]))
        held, bit = jnp.concatenate([held, pieces[-1]], axis=0), 2 * bit
    return pieces


def arrivals_kernel(devices, capacity, *refs):
    *pieces, weight, early, first, second, all_ref, sorted_ref, sem = refs
    read = pltpu.make_async_copy(weight.at[pl.ds(0, early.shape[0])], early, sem)
    read.start()
    halves = pieces[0].shape[1] // 4
    rows = halves * LANES
    comp, lon = lax.axis_size("comp"), lax.axis_size("lon")
    my_comp, my_lon = lax.axis_index("comp"), lax.axis_index("lon")
    me = (my_comp * lon + my_lon).astype(F32)
    place = 0
    for piece in pieces:
        all_ref[place : place + piece.shape[0]] = piece[...]
        place += piece.shape[0]
    for s in range(devices):
        along = lax.rem(s % comp - my_comp + comp, comp)
        beside = (along == 1) | (along == comp - 1)
        along = jnp.where(beside & ~is_even("comp"), comp - along, along)
        block = all_ref[along + (my_lon ^ (s // comp)) * comp]
        for i in range(4):
            sorted_ref[i, s : s + 1, :] = joined(block, i, halves)
    j = lax.broadcasted_iota(jnp.int32, (rows, rows), 0)
    i = lax.broadcasted_iota(jnp.int32, (rows, rows), 1)
    before = jnp.where(j < i, 1.0, 0.0).astype(BF16)
    for which, out in enumerate((first, second)):
        named = sorted_ref[2 * which] == me
        target = sorted_ref[2 * which + 1]
        rank = jnp.dot(jnp.where(named, 1.0, 0.0).astype(BF16), before, preferred_element_type=F32)
        row = jnp.where(named, target + 1.0, 0.0)
        parts = [jnp.where(rank == float(k), row, 0.0) for k in range(capacity)]
        table = jnp.concatenate(parts, axis=0).astype(BF16)
        total = lax.dot_general(
            jnp.ones((8, rows), BF16), table, (((1,), (1,)), ((), ())), preferred_element_type=F32
        )
        wanted = lax.broadcasted_iota(jnp.int32, out.shape, 0).astype(F32) + 1.0
        out[...] = jnp.where(wanted == total[0:1, :], 1.0, 0.0).astype(BF16)
    read.wait()


def summed_channel(devices, capacity, arrived, chosen, channels, i):
    parts = [arrived[pl.ds(k * channels + i, devices, stride=capacity * channels), :] for k in range(capacity)]
    x = jnp.concatenate(parts, axis=0)
    high = x.astype(BF16)
    low = (x - high.astype(F32)).astype(BF16)
    total = jnp.dot(chosen[...], jnp.concatenate([high, low], axis=1), preferred_element_type=F32)
    return total[:, :LANES] + total[:, LANES:]


def forced_kernel(devices, capacity, slots_in, arrived, target, land, base, weight, early, after_this, next_ref, placed, slots, high_ref, low_ref, made, sems, chosen, held, weight_sems, land_held):
    chosen_read = pltpu.make_async_copy(target, chosen, sems.at[1 + 2 * PARTS])
    chosen_read.start()
    reads = copies_of(base.at[:, 0], made, sems, 1)
    reads += copies_of(land, land_held, sems, 1 + PARTS)
    slots_read = pltpu.make_async_copy(slots_in, slots, sems.at[0])
    slots_read.start()
    size = held.shape[0] // LATE
    for late in range(LATE):
        source = weight.at[pl.ds(early.shape[0] + late * size, size)]
        pltpu.make_async_copy(source, held.at[pl.ds(late * size, size)], weight_sems.at[late]).start()
    placed[...] = jnp.zeros(placed.shape, F32)
    chosen_read.wait()
    forcing = [summed_channel(devices, capacity, arrived, chosen, 4, i) for i in range(4)]
    wait_all(reads)
    mask = land_held[...].astype(F32)
    after = []
    for i in range(4):
        after.append(made[i] + mask * (forcing_gain * forcing[i]))
        made[i] = after[i]
    writes = copies_of(made, next_ref.at[:, 0], sems, 1)
    put_split([after[0], after[2], after[3]], high_ref, low_ref)
    slots_read.wait()
    product_rows(slots, early, high_ref, low_ref, placed, 3)
    first = early.shape[0]
    for late in range(LATE):
        size = held.shape[0] // LATE
        part = pl.ds(late * size, size)
        pltpu.make_async_copy(weight.at[pl.ds(first + late * size, size)], held.at[part], weight_sems.at[late]).wait()
        product_rows(slots, held.at[part], high_ref, low_ref, placed, 3, first + late * size)
    wait_all(writes)


def surface_kernel(devices, capacity, arrived, chosen, out, made, sems):
    writes = []
    for i in range(3):
        made[i] = summed_channel(devices, capacity, arrived, chosen, 3, i)
        writes.append(pltpu.make_async_copy(made.at[i], out.at[i], sems.at[i]))
        writes[i].start()
    wait_all(writes)


def whole(x):
    return pl.BlockSpec(x.shape, lambda *_: (0,) * len(x.shape))


def level_zero(x):
    return pl.BlockSpec((x.shape[0], 1) + x.shape[2:], lambda *_: (0, 0, 0, 0))


ANY = pl.BlockSpec(memory_space=pl.ANY)


def in_hbm(x):
    return pltpu.with_memory_space_constraint(x, pltpu.HBM)


def in_vmem(x):
    return pltpu.with_memory_space_constraint(x, pltpu.VMEM)


def body(
    atm_state, ocean_state, surface_state, atm_diffusion, land_sea, flux_dest, flux_row, flux_weight, surface_dest,
    surface_row, surface_weight,
):
    variables, levels, rows, cols = atm_state.shape
    devices = lax.axis_size("comp") * lax.axis_size("lon")
    capacity = max(2, 2 * rows // devices)
    width = devices * capacity
    halves = rows // LANES
    f32 = functools.partial(jax.ShapeDtypeStruct, dtype=F32)
    top = f32((variables, rows, cols))
    line = jax.ShapeDtypeStruct((1, rows), jnp.int32)
    all_rows = f32((-(-(2 * variables * levels + 1 + 4 * halves) // 8) * 8, cols))
    top_cols, own_lists = f32((variables * halves, cols)), f32((4 * halves, cols))
    made = [top, all_rows, all_rows, top_cols, top_cols, own_lists]
    atm_top, close_rows, other_rows, close_cols, other_cols, lists = pl.pallas_call(
        functools.partial(edges_kernel, halves, variables, levels, rows),
        grid=(1,),
        in_specs=[ANY] * 7,
        out_specs=[whole(e) for e in made],
        out_shape=made,
        scratch_shapes=[
            pltpu.VMEM((2, *all_rows.shape), F32),
            pltpu.VMEM((2, *top_cols.shape), F32),
            pltpu.VMEM((2, variables, levels, 8, cols), F32),
            pltpu.VMEM((2, variables, levels, 8, cols), F32),
            pltpu.VMEM((2, 8, cols), jnp.int32),
            pltpu.VMEM((4, 1, rows), jnp.int32),
            pltpu.SemaphoreType.DMA((variables + 10,)),
        ],
        compiler_params=params(),
        cost_estimate=cost(8),
        name="edges",
    )(
        *(in_hbm(x) for x in (atm_state, ocean_state, land_sea)),
        *(in_hbm(x.reshape(1, rows)) for x in (flux_dest, flux_row, surface_dest, surface_row)),
    )
    row_sides = exchange(close_rows, other_rows, "comp")
    sides = (*row_sides, *exchange(close_cols, other_cols, "lon"))
    in_memory = pl.BlockSpec(memory_space=pltpu.VMEM)
    held, flux_slots, surface_slots = pl.pallas_call(
        functools.partial(prepare_kernel, capacity),
        grid=(1,),
        in_specs=[whole(lists), ANY],
        out_specs=[in_memory, whole(line), whole(line)],
        out_shape=[pltpu.VMEM(flux_weight.shape, BF16)] + [pltpu.HBM(line.shape, jnp.int32)] * 2,
        scratch_shapes=[pltpu.SemaphoreType.DMA((CHUNKS,))],
        compiler_params=params(),
        cost_estimate=cost(4),
        name="prepare",
    )(lists, in_hbm(flux_weight))

    far_from, flux_slots = lax.optimization_barrier((lists, flux_slots))
    far = far_lists(far_from)

    work = [
        pltpu.SMEM((1, rows), jnp.int32),
        pltpu.VMEM((rows * 4, cols), F32),
        pltpu.VMEM((rows * 4, cols), F32),
        pltpu.VMEM(top.shape, F32),
        pltpu.SemaphoreType.DMA((2 + 2 * PARTS,)),
    ]
    atm_started, sent = pl.pallas_call(
        functools.partial(flux_kernel, halves, levels),
        grid=(1,),
        in_specs=[ANY]
        + [whole(e) for e in (atm_top, atm_diffusion, surface_state, *sides)]
        + [in_memory],
        out_specs=[ANY, ANY],
        scratch_shapes=[*work, pltpu.VMEM((width * 4, cols), F32)],
        out_shape=[f32(atm_state.shape), pltpu.HBM((width * 4, cols), F32)],
        compiler_params=params(),
        cost_estimate=cost(5),
        name="fluxes",
    )(in_hbm(flux_slots), atm_top, atm_diffusion, surface_state, *sides, in_vmem(held))
    sent, far = lax.optimization_barrier((sent, far))
    arrived = lax.all_to_all(
        sent.reshape(devices, capacity * 4, cols), AXES, split_axis=0, concat_axis=0, tiled=True
    ).reshape(width * 4, cols)

    along_comp = lists_along_comp(lists, *row_sides, far)
    along_comp, land, _ = lax.optimization_barrier((along_comp, land_sea, sent))
    pieces = lists_along_lon(along_comp)
    count = variables * (levels - 1) + variables * levels + 1
    padded = -(-count // 8) * 8
    rest_cols = f32((padded * halves, cols))
    rest = pl.pallas_call(
        functools.partial(rest_edges_kernel, halves, variables, levels),
        grid=(1,),
        in_specs=[whole(atm_state), whole(ocean_state), whole(land_sea)],
        out_specs=[whole(rest_cols)] * 2,
        out_shape=[rest_cols, rest_cols],
        scratch_shapes=[pltpu.VMEM((2, *rest_cols.shape), F32)],
        compiler_params=params(),
        cost_estimate=cost(8),
        name="rest_edges",
    )(atm_state, ocean_state, land)
    rest = (*row_sides, *exchange(*rest, "lon"))
    base = variables * (levels - 1)
    atm_next = pl.pallas_call(
        functools.partial(atm_rest_kernel, halves, levels),
        grid=(1,),
        in_specs=[whole(atm_state), whole(atm_diffusion)] + [whole(e) for e in rest] + [ANY],
        out_specs=ANY,
        out_shape=f32(atm_state.shape),
        scratch_shapes=[pltpu.VMEM((base, rows, cols), F32), pltpu.SemaphoreType.DMA((base,))],
        input_output_aliases={6: 0},
        compiler_params=params(),
        cost_estimate=cost(4),
        name="atm_rest",
    )(atm_state, atm_diffusion, *rest, atm_started)
    fields = variables * levels
    ocean_base = pl.pallas_call(
        functools.partial(ocean_kernel, halves, base, levels),
        grid=(1,),
        in_specs=[whole(ocean_state), whole(land_sea)] + [whole(e) for e in rest],
        out_specs=ANY,
        out_shape=pltpu.HBM(ocean_state.shape, F32),
        scratch_shapes=[pltpu.VMEM((fields, rows, cols), F32), pltpu.SemaphoreType.DMA((fields,))],
        compiler_params=params(),
        cost_estimate=cost(5),
        name="ocean_base",
    )(ocean_state, land_sea, *rest)
    target = jax.ShapeDtypeStruct((rows, width), BF16)
    early, flux_target, surface_target = pl.pallas_call(
        functools.partial(arrivals_kernel, devices, capacity),
        grid=(1,),
        in_specs=[whole(piece) for piece in pieces] + [ANY],
        out_specs=[in_memory, whole(target), whole(target)],
        scratch_shapes=[pltpu.VMEM((devices, 4 * halves, cols), F32), pltpu.VMEM((4, devices, rows), F32), pltpu.SemaphoreType.DMA(())],
        out_shape=[pltpu.VMEM((rows // CHUNKS * EARLY, cols, cols), BF16), pltpu.HBM(target.shape, BF16), target],
        compiler_params=params(),
        cost_estimate=cost(1),
        name="arrivals",
    )(*pieces, in_hbm(surface_weight))

    back_shape = f32((width * 3, cols))
    ocean_next, back = pl.pallas_call(
        functools.partial(forced_kernel, devices, capacity),
        grid=(1,),
        in_specs=[ANY, whole(arrived), ANY, ANY, ANY, ANY, in_memory, ANY],
        out_specs=[ANY, whole(back_shape)],
        scratch_shapes=[
            *work,
            pltpu.VMEM(target.shape, BF16),
            pltpu.VMEM((rows - rows // CHUNKS * EARLY, cols, cols), BF16),
            pltpu.SemaphoreType.DMA((LATE,)),
            pltpu.VMEM((rows, cols), jnp.int32),
        ],
        out_shape=[f32(ocean_state.shape), back_shape],
        input_output_aliases={4: 0},
        compiler_params=params(),
        cost_estimate=cost(5),
        name="forced",
    )(in_hbm(surface_slots), arrived, in_hbm(flux_target), in_hbm(land_sea), ocean_base, in_hbm(surface_weight), in_vmem(early), in_hbm(atm_next))
    returned = lax.all_to_all(
        back.reshape(devices, capacity * 3, cols), AXES, split_axis=0, concat_axis=0, tiled=True
    ).reshape(width * 3, cols)

    surface_next = pl.pallas_call(
        functools.partial(surface_kernel, devices, capacity),
        grid=(1,),
        in_specs=[whole(returned), whole(surface_target)],
        out_specs=ANY,
        out_shape=f32(surface_state.shape),
        scratch_shapes=[pltpu.VMEM(surface_state.shape, F32), pltpu.SemaphoreType.DMA((3,))],
        compiler_params=params(),
        cost_estimate=cost(1),
        name="surface",
    )(returned, surface_target)
    return (atm_next, ocean_next, surface_next)


def solution(mesh):
    in_specs = (
        P(None, None, "comp", "lon"),
        P(None, None, "comp", "lon"),
        P(None, "comp", "lon"),
        P("comp", "lon"),
        P("comp", "lon"),
        P(("comp", "lon"), None),
        P(("comp", "lon")),
        P(("comp", "lon"), None, None),
        P(("comp", "lon"), None),
        P(("comp", "lon")),
        P(("comp", "lon"), None, None),
    )
    out_specs = (P(None, None, "comp", "lon"), P(None, None, "comp", "lon"), P(None, "comp", "lon"))
    return jax.shard_map(body, mesh=mesh, in_specs=in_specs, out_specs=out_specs, check_vma=False)
```
